32 devices in a mesh: grp: 4 (over y, x), edge: 8 (over z, core).
Axes of the slice: x: 2, y: 2, z: 4, core: 2. Of those that a mesh axis runs over, the one named last changes fastest.
Arguments:
- edge_embed: bfloat16 [65536, 512], P(('grp', 'edge')), may hold values from -6 to 6
- atom_embed: bfloat16 [4096, 256], P(('grp', 'edge')), may hold values from -6 to 6
- radial_basis: bfloat16 [65536, 128], P(('grp', 'edge')), may hold values from 0 to 1
- triplet_basis: bfloat16 [65536, 256], P(('grp', 'edge')), may hold values from -6 to 6
- quadruplet_basis: bfloat16 [65536, 256], P(('grp', 'edge')), may hold values from -6 to 6
- triplet_source_row: int32 [65536, 16], P(('grp', 'edge')), may hold values from 0 to 2175, as said below
- triplet_mask: int32 [65536, 16], P(('grp', 'edge')), may hold values 0 or 1
- quadruplet_source_row: int32 [65536, 8], P(('grp', 'edge')), may hold values from 0 to 2175, as said below
- quadruplet_mask: int32 [65536, 8], P(('grp', 'edge')), may hold values 0 or 1
- edge_target_atom: int32 [32, 2048], P(('grp', 'edge')), may hold values from 0 to 127, never falling along the last dimension, each value on 1 to 30 neighbouring positions
- borrowed_edges: int32 [32, 8, 16], P(('grp', 'edge')), may hold values from 0 to 16383, as said below
- w_source_trip: bfloat16 [512, 512], replicated, may hold values from -0.25 to 0.25
- w_rbf_trip: bfloat16 [128, 512], replicated, may hold values from -0.5 to 0.5
- w_down_trip: bfloat16 [512, 64], replicated, may hold values from -0.25 to 0.25
- w_source_quad: bfloat16 [512, 512], replicated, may hold values from -0.25 to 0.25
- w_rbf_quad: bfloat16 [128, 512], replicated, may hold values from -0.5 to 0.5
- w_down_quad: bfloat16 [512, 32], replicated, may hold values from -0.25 to 0.25
- triplet_bilinear_weight: bfloat16 [1024, 64], replicated, may hold values from -0.1875 to 0.1875
- w_up_trip: bfloat16 [64, 512], replicated, may hold values from -0.75 to 0.75
- w_bilinear_quad: bfloat16 [1024, 32], replicated, may hold values from -0.1875 to 0.1875
- w_up_quad: bfloat16 [32, 512], replicated, may hold values from -1 to 1
- w_skip: bfloat16 [512, 512], replicated, may hold values from -0.25 to 0.25
- w_res_first: bfloat16 [512, 512], replicated, may hold values from -0.25 to 0.25
- w_res_second: bfloat16 [512, 512], replicated, may hold values from -0.25 to 0.25
- w_rbf_atom: bfloat16 [128, 512], replicated, may hold values from -0.5 to 0.5
- w_atom: bfloat16 [512, 256], replicated, may hold values from -0.25 to 0.25
- w_concat: bfloat16 [768, 512], replicated, may hold values from -0.21875 to 0.21875
- w_rbf_out: bfloat16 [128, 512], replicated, may hold values from -0.5 to 0.5
- w_out: bfloat16 [512, 256], replicated, may hold values from -0.25 to 0.25
- edge_cotangent: bfloat16 [65536, 512], P(('grp', 'edge')), may hold values from -6 to 6
- atom_cotangent: bfloat16 [4096, 256], P(('grp', 'edge')), may hold values from -6 to 6
- output_cotangent: bfloat16 [4096, 256], P(('grp', 'edge')), may hold values from -6 to 6
Outputs:
- edge_update: bfloat16 [65536, 512], P(('grp', 'edge'))
- atom_update: bfloat16 [4096, 256], P(('grp', 'edge'))
- atom_output: bfloat16 [4096, 256], P(('grp', 'edge'))
- grad_edge_embed: bfloat16 [65536, 512], P(('grp', 'edge'))
- grad_atom_embed: bfloat16 [4096, 256], P(('grp', 'edge'))
- grad_w_source_trip: float32 [512, 512], P('edge')
- grad_w_rbf_trip: float32 [128, 512], P('edge')
- grad_w_down_trip: float32 [512, 64], P('edge')
- grad_w_source_quad: float32 [512, 512], P('edge')
- grad_w_rbf_quad: float32 [128, 512], P('edge')
- grad_w_down_quad: float32 [512, 32], P('edge')
- grad_w_bilinear_trip: float32 [1024, 64], P('edge')
- grad_w_up_trip: float32 [64, 512], P(None, 'edge')
- grad_w_bilinear_quad: float32 [1024, 32], P('edge')
- grad_w_up_quad: float32 [32, 512], P(None, 'edge')
- grad_w_skip: float32 [512, 512], P('edge')
- grad_w_res_first: float32 [512, 512], P('edge')
- grad_w_res_second: float32 [512, 512], P('edge')
- grad_w_rbf_atom: float32 [128, 512], P('edge')
- grad_w_atom: float32 [512, 256], P('edge')
- grad_w_concat: float32 [768, 512], P('edge')
- grad_w_rbf_out: float32 [128, 512], P('edge')
- grad_w_out: float32 [512, 256], P('edge')
The draws below stay inside these ranges and needn't reach their ends.
Inputs may be any that keep to these rules, and one draw needn't show every extreme that they name: `borrowed_edges`: entry (b, p, j) is the id, within the structure group of block b, of an edge of that group's block p: it lies in [p * 2048, (p + 1) * 2048); the 16 entries of one (b, p) are distinct. `triplet_source_row`: A value v below 2048 is row v of the own block; a value 2048 + p * 16 + j reads entry (p, j) of the block's borrowed_edges, with p never the block's own index within its group. `quadruplet_source_row`: as for triplet_source_row.
All inputs are finite; a program needn't handle non-finite values. No bound on the sum of `triplet_mask` or of `quadruplet_mask` on one device may be relied on, other than what follows from the above.
Results may differ from the reference program's by a relative error of at most 0.02.
Values may be sent and summed in bfloat16 or wider, within the bound.
No kernel may reach another device: no remote copies, remote signals or barrier semaphores. Data moves between devices by JAX's collectives and lax.ppermute only.
A program may use at most 320 MiB of HBM per device.

```python
import math
import jax
import jax.numpy as jnp
import numpy as np
from jax import lax

EMB_ATOM = 256
EMB_EDGE = 512
TRIPLET_WIDTH = 64
EMB_QUAD = 32
RBF = 128
CIRCULAR_BASIS = 16
SPHERICAL_BASIS = 32
NEIGHBOURS = 30
BLOCK_EDGES = 2048
TRIPLET_SLOTS = 16
QUADRUPLET_SLOTS = 8
ATOMS_DEV = 128
GHOST_CAP = 16
PEERS = 8
TOTAL_BLOCKS = 32
TOTAL_EDGES = 65536
ATOMS = 4096


def ghost_plan(key):
    base = jax.random.fold_in(key, 11)
    first, second = jax.random.split(base, 2)
    counts = jax.random.randint(first, (TOTAL_BLOCKS, PEERS), GHOST_CAP // 2, GHOST_CAP + 1)
    busiest = jax.random.randint(second, (TOTAL_BLOCKS // PEERS, 1), 0, PEERS)
    busiest = jnp.repeat(busiest, PEERS, axis=0)
    peer_ids = jnp.arange(PEERS, dtype=jnp.int32)[None, :]
    own_ids = (jnp.arange(TOTAL_BLOCKS, dtype=jnp.int32) % PEERS)[:, None]
    counts = jnp.where(peer_ids == busiest, GHOST_CAP, counts)
    counts = jnp.where(peer_ids == PEERS - 1, GHOST_CAP, counts)
    counts = jnp.where(peer_ids == own_ids, 0, counts)
    return (counts, own_ids)


def draw_borrowed_edges(key, part):
    scores = jax.random.randint(jax.random.fold_in(key, 5), (TOTAL_BLOCKS, PEERS, BLOCK_EDGES), 0, 2 ** 30 // BLOCK_EDGES)
    positions = jnp.arange(BLOCK_EDGES, dtype=jnp.int32)
    scores = scores * BLOCK_EDGES + positions[None, None, :]
    block_ids = jnp.arange(TOTAL_BLOCKS, dtype=jnp.int32)[:, None, None]
    peer_ids = jnp.arange(PEERS, dtype=jnp.int32)[None, :, None]
    place = positions[None, None, :]
    forced = (block_ids == 0) & ((peer_ids == 0) & (place == 0) | (peer_ids == PEERS - 1) & (place == BLOCK_EDGES - 1))
    scores = jnp.where(forced, 2 ** 30 + place, scores)
    chosen = lax.top_k(scores, GHOST_CAP)[1].astype(jnp.int32)
    return chosen + (jnp.arange(PEERS, dtype=jnp.int32) * BLOCK_EDGES)[None, :, None]


def slot_sources(key, salt, slots):
    counts, own_ids = ghost_plan(key)
    keys = jax.random.split(jax.random.fold_in(key, salt), 4)
    draw_shape = (TOTAL_BLOCKS, BLOCK_EDGES, slots)
    local_flag = jax.random.randint(keys[0], draw_shape, 0, 2)
    local_row = jax.random.randint(keys[1], draw_shape, 0, BLOCK_EDGES)
    distance = jax.random.randint(keys[2], draw_shape, 1, PEERS)
    owner = (own_ids[:, :, None] + distance) % PEERS
    available = jnp.take_along_axis(counts[:, None, :], owner.reshape(TOTAL_BLOCKS, 1, -1), axis=2).reshape(draw_shape)
    ghost_slot = jax.random.randint(keys[3], draw_shape, 0, 2 ** 20) % available
    value = jnp.where(local_flag == 1, local_row, BLOCK_EDGES + owner * GHOST_CAP + ghost_slot)
    value = value.at[0, 0, 0].set(BLOCK_EDGES + PEERS * GHOST_CAP - 1)
    value = value.at[0, 1, 0].set(0)
    return value.reshape(TOTAL_BLOCKS * BLOCK_EDGES, slots).astype(jnp.int32)


def draw_triplet_source_row(key, part):
    return slot_sources(key, 23, TRIPLET_SLOTS)


def draw_quadruplet_source_row(key, part):
    return slot_sources(key, 29, QUADRUPLET_SLOTS)


def place_ends(values, rng, smallest, largest):
    shape = values.shape
    spot = [jax.random.randint(jax.random.fold_in(rng, axis), (), 0, shape[axis]) for axis in range(len(shape))]
    values = values.at[tuple(spot)].set(smallest)
    longest = shape.index(max(shape))
    spot[longest] = (spot[longest] + 1) % shape[longest]
    return values.at[tuple(spot)].set(largest)


def shard_levels(key, dims, cuts, least, top_value):
    factor_of = 1.0
    for axis_at, blocks in cuts:
        heights = jax.random.uniform(jax.random.fold_in(jax.random.fold_in(key, 6), axis_at), (blocks,), jnp.float32, least / len(cuts), top_value / len(cuts))
        factor_of = factor_of * jnp.repeat(jnp.exp(heights), dims[axis_at] // blocks).reshape((-1,) + (1,) * (len(dims) - 1 - axis_at))
    return factor_of


def profile(number_of, total, reach, slope):
    portions = [(1 << 20) // math.isqrt(standing ** slope) + 1 for standing in range(2, number_of + 1)]
    spare, holding = total - reach - (number_of - 1), [1] * (number_of - 1)
    while spare > 0:
        movable = [i for i in range(number_of - 1) if holding[i] < reach]
        mass, left = sum([portions[i] for i in movable]), spare
        for i in movable:
            more = min(reach - holding[i], max(1, left * portions[i] // mass), spare)
            holding[i] = holding[i] + more
            spare = spare - more
    return np.array([reach] + holding)


def uneven_parts(rng, amount, total, most, skew):
    if amount == 2:
        one = jax.random.randint(rng, (), max(1, total - most), min(most, total - 1) + 1)
        return jnp.stack([one, total - one])
    sizes = jnp.asarray(profile(amount, total, most, skew), jnp.int32)
    twos = (amount - 1) // 2
    source_of, taker = sizes[1:1 + 2 * twos:2], sizes[2:2 + 2 * twos:2]
    margin = jnp.minimum(source_of - 1, most - taker)
    passed = jax.random.randint(jax.random.fold_in(rng, 1), (twos,), 0, 1 << 20) % (margin + 1)
    sizes = sizes.at[1:1 + 2 * twos:2].set(source_of - passed).at[2:2 + 2 * twos:2].set(taker + passed)
    return sizes[jax.random.permutation(jax.random.fold_in(rng, 2), amount)]


def scatter_about(rng, extent, scale, reach, pieces=(), kind=jnp.bfloat16):
    gain = shard_levels(rng, extent, pieces, -0.22, 0.18) if pieces else 1.0
    entries = jax.random.normal(rng, extent, jnp.float32) * scale * gain
    return jnp.minimum(jnp.maximum(entries, -reach), reach).astype(kind)


def setup_inputs(seed: int = 0) -> dict:
    streams_of = jax.random.split(jax.random.key(seed), 33)
    edge_embed = scatter_about(streams_of[0], (TOTAL_EDGES, EMB_EDGE), 1.0, 6.0, ((0, 32),))
    atom_embed = scatter_about(streams_of[1], (ATOMS, EMB_ATOM), 1.0, 6.0, ((0, 32),))
    radial_basis = jnp.clip(1.0 * jax.random.uniform(streams_of[2], (TOTAL_EDGES, RBF), jnp.float32) ** shard_levels(streams_of[2], (TOTAL_EDGES, RBF), ((0, 32),), -0.2, 0.2), 0.0, 1.0).astype(jnp.bfloat16)
    triplet_basis = scatter_about(streams_of[3], (TOTAL_EDGES, TRIPLET_SLOTS * CIRCULAR_BASIS), 1.0, 6.0, ((0, 32),))
    quadruplet_basis = scatter_about(streams_of[4], (TOTAL_EDGES, QUADRUPLET_SLOTS * SPHERICAL_BASIS), 1.0, 6.0, ((0, 32),))
    triplet_source_row = draw_triplet_source_row(jax.random.fold_in(streams_of[32], 71), 0)
    triplet_mask = place_ends((jax.random.randint(streams_of[6], (TOTAL_EDGES, TRIPLET_SLOTS), 0, 4) < 3).astype(jnp.int32), jax.random.fold_in(streams_of[6], 1), 0, 1)
    quadruplet_source_row = draw_quadruplet_source_row(jax.random.fold_in(streams_of[32], 71), 0)
    quadruplet_mask = place_ends((jax.random.randint(streams_of[8], (TOTAL_EDGES, QUADRUPLET_SLOTS), 0, 4) < 3).astype(jnp.int32), jax.random.fold_in(streams_of[8], 1), 0, 1)
    edge_target_atom = jax.vmap(lambda own: jnp.searchsorted(jnp.cumsum(uneven_parts(own, ATOMS_DEV, BLOCK_EDGES, NEIGHBOURS, 1)), jnp.arange(BLOCK_EDGES), side="right"))(jax.random.split(streams_of[9], TOTAL_BLOCKS)).reshape((TOTAL_BLOCKS, BLOCK_EDGES)).astype(jnp.int32)
    borrowed_edges = draw_borrowed_edges(jax.random.fold_in(streams_of[32], 71), 0)
    w_source_trip = scatter_about(streams_of[11], (EMB_EDGE, EMB_EDGE), EMB_EDGE ** -0.5, 0.25)
    w_rbf_trip = scatter_about(streams_of[12], (RBF, EMB_EDGE), RBF ** -0.5, 0.5)
    w_down_trip = scatter_about(streams_of[13], (EMB_EDGE, TRIPLET_WIDTH), EMB_EDGE ** -0.5, 0.25)
    w_source_quad = scatter_about(streams_of[14], (EMB_EDGE, EMB_EDGE), EMB_EDGE ** -0.5, 0.25)
    w_rbf_quad = scatter_about(streams_of[15], (RBF, EMB_EDGE), RBF ** -0.5, 0.5)
    w_down_quad = scatter_about(streams_of[16], (EMB_EDGE, EMB_QUAD), EMB_EDGE ** -0.5, 0.25)
    triplet_bilinear_weight = scatter_about(streams_of[17], (CIRCULAR_BASIS * TRIPLET_WIDTH, TRIPLET_WIDTH), (CIRCULAR_BASIS * TRIPLET_WIDTH) ** -0.5, 0.1875)
    w_up_trip = scatter_about(streams_of[18], (TRIPLET_WIDTH, EMB_EDGE), TRIPLET_WIDTH ** -0.5, 0.75)
    w_bilinear_quad = scatter_about(streams_of[19], (SPHERICAL_BASIS * EMB_QUAD, EMB_QUAD), (SPHERICAL_BASIS * EMB_QUAD) ** -0.5, 0.1875)
    w_up_quad = scatter_about(streams_of[20], (EMB_QUAD, EMB_EDGE), EMB_QUAD ** -0.5, 1.0)
    w_skip = scatter_about(streams_of[21], (EMB_EDGE, EMB_EDGE), EMB_EDGE ** -0.5, 0.25)
    w_res_first = scatter_about(streams_of[22], (EMB_EDGE, EMB_EDGE), EMB_EDGE ** -0.5, 0.25)
    w_res_second = scatter_about(streams_of[23], (EMB_EDGE, EMB_EDGE), EMB_EDGE ** -0.5, 0.25)
    w_rbf_atom = scatter_about(streams_of[24], (RBF, EMB_EDGE), RBF ** -0.5, 0.5)
    w_atom = scatter_about(streams_of[25], (EMB_EDGE, EMB_ATOM), EMB_EDGE ** -0.5, 0.25)
    w_concat = scatter_about(streams_of[26], (EMB_ATOM + EMB_EDGE, EMB_EDGE), (EMB_ATOM + EMB_EDGE) ** -0.5, 0.21875)
    w_rbf_out = scatter_about(streams_of[27], (RBF, EMB_EDGE), RBF ** -0.5, 0.5)
    w_out = scatter_about(streams_of[28], (EMB_EDGE, EMB_ATOM), EMB_EDGE ** -0.5, 0.25)
    edge_cotangent = scatter_about(streams_of[29], (TOTAL_EDGES, EMB_EDGE), 1.0, 6.0, ((0, 32),))
    atom_cotangent = scatter_about(streams_of[30], (ATOMS, EMB_ATOM), 1.0, 6.0, ((0, 32),))
    output_cotangent = scatter_about(streams_of[31], (ATOMS, EMB_ATOM), 1.0, 6.0, ((0, 32),))
    return {"edge_embed": edge_embed, "atom_embed": atom_embed, "radial_basis": radial_basis, "triplet_basis": triplet_basis, "quadruplet_basis": quadruplet_basis, "triplet_source_row": triplet_source_row, "triplet_mask": triplet_mask, "quadruplet_source_row": quadruplet_source_row, "quadruplet_mask": quadruplet_mask, "edge_target_atom": edge_target_atom, "borrowed_edges": borrowed_edges, "w_source_trip": w_source_trip, "w_rbf_trip": w_rbf_trip, "w_down_trip": w_down_trip, "w_source_quad": w_source_quad, "w_rbf_quad": w_rbf_quad, "w_down_quad": w_down_quad, "triplet_bilinear_weight": triplet_bilinear_weight, "w_up_trip": w_up_trip, "w_bilinear_quad": w_bilinear_quad, "w_up_quad": w_up_quad, "w_skip": w_skip, "w_res_first": w_res_first, "w_res_second": w_res_second, "w_rbf_atom": w_rbf_atom, "w_atom": w_atom, "w_concat": w_concat, "w_rbf_out": w_rbf_out, "w_out": w_out, "edge_cotangent": edge_cotangent, "atom_cotangent": atom_cotangent, "output_cotangent": output_cotangent}


HALF_ROOT = 1.0 / math.sqrt(2.0)
THIRD_ROOT = 1.0 / math.sqrt(3.0)

@jax.custom_vjp
def low(v):
    return lax.optimization_barrier(v.astype(jnp.bfloat16)).astype(jnp.float32)

@jax.custom_vjp
def low_back(v):
    return v

def low_keep(v):
    return (low(v), None)

def low_pass(kept, grad):
    return (grad,)

def back_keep(v):
    return (v, None)

def back_low(kept, grad):
    return (low(grad),)
low.defvjp(low_keep, low_pass)
low_back.defvjp(back_keep, back_low)

def matmul(operand, weight):
    return jnp.dot(operand, weight, precision=lax.Precision.HIGHEST)

def project(weights, edge_rows, radial):
    w_source_trip, w_rbf_trip, w_down_trip, w_source_quad, w_rbf_quad, w_down_quad = weights[:6]
    source_pre = low_back(matmul(edge_rows, w_source_trip))
    radial_pre = low_back(matmul(radial, w_rbf_trip))
    mixed_trip = low(jax.nn.silu(source_pre) * radial_pre)
    down_trip = low(jax.nn.silu(low_back(matmul(mixed_trip, w_down_trip))))
    quad_pre = low_back(matmul(edge_rows, w_source_quad))
    quad_radial = low_back(matmul(radial, w_rbf_quad))
    mixed_quad = low(jax.nn.silu(quad_pre) * quad_radial)
    down_quad = low(jax.nn.silu(low_back(matmul(mixed_quad, w_down_quad))))
    return jnp.concatenate([down_trip, down_quad], axis=1)

def bilinear_sum(rows_table, sources, slot_mask, coefficients, slots):
    picked = rows_table[sources] * slot_mask[:, :, None]
    coefficient = coefficients.reshape(coefficients.shape[0], slots, -1)
    summed = jnp.einsum('ekc,eki->eci', coefficient, picked, precision=lax.Precision.HIGHEST)
    return low_back(low(summed.reshape(summed.shape[0], -1)))

def device_forward(weights, table_all, single):
    device_index, edge_rows, atom_rows, radial, trip_coeff, quad_coeff, trip_sources, trip_slots, quad_sources, quad_slots, owner_atom, ghost_rows = single
    w_source_trip, w_rbf_trip, w_down_trip, w_source_quad, w_rbf_quad, w_down_quad, triplet_bilinear_weight, w_up_trip, w_bilinear_quad, w_up_quad, w_skip, w_res_first, w_res_second, w_rbf_atom, w_atom, w_concat, w_rbf_out, w_out = weights
    group_id = device_index // PEERS
    group_table = lax.dynamic_slice_in_dim(table_all, group_id * (PEERS * BLOCK_EDGES), PEERS * BLOCK_EDGES, 0)
    local_table = lax.dynamic_slice_in_dim(table_all, device_index * BLOCK_EDGES, BLOCK_EDGES, 0)
    full_table = jnp.concatenate([local_table, group_table[ghost_rows.reshape(-1)]], axis=0)
    trip_sum = bilinear_sum(full_table[:, :TRIPLET_WIDTH], trip_sources, trip_slots, trip_coeff, TRIPLET_SLOTS)
    quad_sum = bilinear_sum(full_table[:, TRIPLET_WIDTH:], quad_sources, quad_slots, quad_coeff, QUADRUPLET_SLOTS)
    hidden_trip = low(jax.nn.silu(low_back(matmul(trip_sum, triplet_bilinear_weight))))
    hidden_quad = low(jax.nn.silu(low_back(matmul(quad_sum, w_bilinear_quad))))
    trip_message = jax.nn.silu(low_back(matmul(hidden_trip, w_up_trip)))
    quad_message = jax.nn.silu(low_back(matmul(hidden_quad, w_up_quad)))
    skip_message = jax.nn.silu(low_back(matmul(edge_rows, w_skip)))
    mixed = (skip_message + trip_message + quad_message) * THIRD_ROOT
    res_hidden = low(jax.nn.silu(low_back(matmul(low(mixed), w_res_first))))
    refined = (mixed + jax.nn.silu(low_back(matmul(res_hidden, w_res_second)))) * HALF_ROOT
    merged = (edge_rows + refined) * HALF_ROOT
    onehot = (owner_atom[:, None] == jnp.arange(ATOMS_DEV, dtype=jnp.int32)[None, :]).astype(jnp.float32)
    radial_atom = low_back(matmul(radial, w_rbf_atom))
    weighted = low(merged * radial_atom)
    gathered = matmul(onehot.T, weighted)
    atom_new = (atom_rows + jax.nn.silu(low_back(matmul(low(gathered), w_atom)))) * HALF_ROOT
    concat_rows = jnp.concatenate([matmul(onehot, low(atom_new)), low(merged)], axis=1)
    edge_new = (merged + jax.nn.silu(low_back(matmul(concat_rows, w_concat)))) * HALF_ROOT
    radial_out = low_back(matmul(radial, w_rbf_out))
    out_weighted = low(edge_new * radial_out)
    out_gathered = matmul(onehot.T, out_weighted)
    atom_output = low_back(matmul(low(out_gathered), w_out))
    return (edge_new, atom_new, atom_output)

def reference(edge_embed, atom_embed, radial_basis, triplet_basis, quadruplet_basis, triplet_source_row, triplet_mask, quadruplet_source_row, quadruplet_mask, edge_target_atom, borrowed_edges, w_source_trip, w_rbf_trip, w_down_trip, w_source_quad, w_rbf_quad, w_down_quad, triplet_bilinear_weight, w_up_trip, w_bilinear_quad, w_up_quad, w_skip, w_res_first, w_res_second, w_rbf_atom, w_atom, w_concat, w_rbf_out, w_out, edge_cotangent, atom_cotangent, output_cotangent):
    radial_blocks = radial_basis.astype(jnp.float32).reshape(TOTAL_BLOCKS, BLOCK_EDGES, RBF)
    packed_remainder = (triplet_basis.astype(jnp.float32).reshape(TOTAL_BLOCKS, BLOCK_EDGES, TRIPLET_SLOTS * CIRCULAR_BASIS), quadruplet_basis.astype(jnp.float32).reshape(TOTAL_BLOCKS, BLOCK_EDGES, QUADRUPLET_SLOTS * SPHERICAL_BASIS), triplet_source_row.reshape(TOTAL_BLOCKS, BLOCK_EDGES, TRIPLET_SLOTS), triplet_mask.astype(jnp.float32).reshape(TOTAL_BLOCKS, BLOCK_EDGES, TRIPLET_SLOTS), quadruplet_source_row.reshape(TOTAL_BLOCKS, BLOCK_EDGES, QUADRUPLET_SLOTS), quadruplet_mask.astype(jnp.float32).reshape(TOTAL_BLOCKS, BLOCK_EDGES, QUADRUPLET_SLOTS), edge_target_atom, borrowed_edges)

    def forward(weights, edge_rows, atom_rows):
        edge_blocks = edge_rows.reshape(TOTAL_BLOCKS, BLOCK_EDGES, EMB_EDGE)
        projector = jax.checkpoint(project)
        table_all = lax.map(lambda paired: projector(weights, paired[0], paired[1]), (edge_blocks, radial_blocks))
        table_all = table_all.reshape(TOTAL_BLOCKS * BLOCK_EDGES, TRIPLET_WIDTH + EMB_QUAD)
        stepper = jax.checkpoint(device_forward)
        packed = (jnp.arange(TOTAL_BLOCKS, dtype=jnp.int32), edge_blocks, atom_rows.reshape(TOTAL_BLOCKS, ATOMS_DEV, EMB_ATOM), radial_blocks) + packed_remainder
        edge_new, atom_new, atom_output = lax.map(lambda single: stepper(weights, table_all, single), packed)
        return (edge_new.reshape(TOTAL_EDGES, EMB_EDGE), atom_new.reshape(ATOMS, EMB_ATOM), atom_output.reshape(ATOMS, EMB_ATOM))
    weights = (w_source_trip.astype(jnp.float32), w_rbf_trip.astype(jnp.float32), w_down_trip.astype(jnp.float32), w_source_quad.astype(jnp.float32), w_rbf_quad.astype(jnp.float32), w_down_quad.astype(jnp.float32), triplet_bilinear_weight.astype(jnp.float32), w_up_trip.astype(jnp.float32), w_bilinear_quad.astype(jnp.float32), w_up_quad.astype(jnp.float32), w_skip.astype(jnp.float32), w_res_first.astype(jnp.float32), w_res_second.astype(jnp.float32), w_rbf_atom.astype(jnp.float32), w_atom.astype(jnp.float32), w_concat.astype(jnp.float32), w_rbf_out.astype(jnp.float32), w_out.astype(jnp.float32))
    results, pullback = jax.vjp(forward, weights, edge_embed.astype(jnp.float32), atom_embed.astype(jnp.float32))
    grad_weights, grad_edges, grad_atoms = pullback((edge_cotangent.astype(jnp.float32), atom_cotangent.astype(jnp.float32), output_cotangent.astype(jnp.float32)))
    return (results[0].astype(jnp.bfloat16), results[1].astype(jnp.bfloat16), results[2].astype(jnp.bfloat16), grad_edges.astype(jnp.bfloat16), grad_atoms.astype(jnp.bfloat16), grad_weights[0], grad_weights[1], grad_weights[2], grad_weights[3], grad_weights[4], grad_weights[5], grad_weights[6], grad_weights[7], grad_weights[8], grad_weights[9], grad_weights[10], grad_weights[11], grad_weights[12], grad_weights[13], grad_weights[14], grad_weights[15], grad_weights[16], grad_weights[17])
```

```python
import math

import jax
import jax.numpy as jnp
from jax import lax
from jax.experimental import pallas as pl
from jax.experimental.pallas import tpu as pltpu
from jax.sharding import PartitionSpec as P

HALF_ROOT = 1.0 / math.sqrt(2.0)
THIRD_ROOT = 1.0 / math.sqrt(3.0)
LOW = jnp.bfloat16
WIDE = jnp.float32
TILE = 256
VMEM_BYTES = 60 * 1024 * 1024


def sigma(v):
    return 0.5 * jnp.tanh(0.5 * v) + 0.5


def slope_of(v, s):
    return s * (1.0 + v * (1.0 - s))


def nn(a, b):
    return jnp.dot(a, b, preferred_element_type=WIDE)


def nt(a, b):
    return lax.dot_general(a, b, (((1,), (1,)), ((), ())), preferred_element_type=WIDE)


def tn(a, b):
    return lax.dot_general(a, b, (((0,), (0,)), ((), ())), preferred_element_type=WIDE)


def split_pair(v):
    high = v.astype(LOW)
    rest = (v - high.astype(WIDE)).astype(LOW)
    return jnp.concatenate([high, rest], axis=0)


def whole(array):
    rank = len(array.shape)
    return pl.BlockSpec(array.shape, lambda i: (0,) * rank)


def rows(width):
    return pl.BlockSpec((TILE, width), lambda i: (i, 0))


def cols(height):
    return pl.BlockSpec((height, TILE), lambda i: (0, i))


def fixed(*shape):
    return pl.BlockSpec(shape, lambda i: (0,) * len(shape))


def call(body, name, steps, ins, in_specs, outs, out_specs, scratch):
    return pl.pallas_call(
        body,
        name=name,
        out_shape=[jax.ShapeDtypeStruct(s, t) for s, t in outs],
        grid_spec=pltpu.PrefetchScalarGridSpec(
            num_scalar_prefetch=0,
            grid=(steps,),
            in_specs=in_specs,
            out_specs=out_specs,
            scratch_shapes=scratch,
        ),
        compiler_params=pltpu.CompilerParams(
            dimension_semantics=("arbitrary",), vmem_limit_bytes=VMEM_BYTES
        ),
    )(*ins)


def source_body(edge, radial, ws3, wr3, wd3, ws4, wr4, wd4, table, down):
    e = edge[...]
    r = radial[...]
    pre3 = nn(e, ws3[...])
    mix3 = (pre3 * sigma(pre3) * nn(r, wr3[...])).astype(LOW)
    down3 = nt(wd3[...], mix3)
    pre4 = nn(e, ws4[...])
    mix4 = (pre4 * sigma(pre4) * nn(r, wr4[...])).astype(LOW)
    down4 = nt(wd4[...], mix4)
    both = jnp.concatenate([down3, down4], axis=0)
    down[...] = both
    table[...] = (both * sigma(both)).astype(LOW)


def fill_slabs(tab, ghost, t3, t4, n3, n4):
    local = tab.shape[1] // TILE
    for s in range(local):
        t3[s * n3 : (s + 1) * n3, :] = tab[0:n3, s * TILE : (s + 1) * TILE]
        t4[s * n4 : (s + 1) * n4, :] = tab[n3 : n3 + n4, s * TILE : (s + 1) * TILE]
    for g in range(ghost.shape[1] // TILE):
        s = local + g
        t3[s * n3 : (s + 1) * n3, :] = ghost[0:n3, g * TILE : (g + 1) * TILE]
        t4[s * n4 : (s + 1) * n4, :] = ghost[n3 : n3 + n4, g * TILE : (g + 1) * TILE]


def pick(tab, index_row, width):
    slabs = tab.shape[0] // width
    low_part = index_row & (TILE - 1)
    slab = index_row >> 8
    hot = (lax.broadcasted_iota(jnp.int32, (TILE, TILE), 0) == low_part).astype(LOW)
    found = nn(tab[...], hot)
    got = jnp.zeros((width, TILE), WIDE)
    for s in range(slabs):
        got = jnp.where(slab == s, found[s * width : (s + 1) * width, :], got)
    return got


def weigh(coef, picked, out, slots, basis, width):
    chunk = 32
    for h in range(width // chunk):
        for cb in range(basis // 4):
            acc = [None] * 4
            for k in range(slots):
                g = picked[k, h * chunk : (h + 1) * chunk, :]
                for j in range(4):
                    row = k * basis + cb * 4 + j
                    term = coef[row : row + 1, :] * g
                    acc[j] = term if acc[j] is None else acc[j] + term
            for j in range(4):
                at = (cb * 4 + j) * width + h * chunk
                out[at : at + chunk, :] = acc[j].astype(LOW)


def gather_body(
    tab, ghost, i3, i4, b3, b4, w3t, w4t, s3, s4, p3, p4, t3, t4, g3, g4, c3, c4
):
    n3, n4 = w3t.shape[0], w4t.shape[0]
    k3, k4 = i3.shape[0], i4.shape[0]

    @pl.when(pl.program_id(0) == 0)
    def _():
        fill_slabs(tab, ghost, t3, t4, n3, n4)

    c3[...] = b3[...].astype(WIDE).T
    c4[...] = b4[...].astype(WIDE).T

    def step3(k, carry):
        g3[k] = pick(t3, i3[pl.ds(k, 1), :], n3)
        return carry

    lax.fori_loop(0, k3, step3, 0, unroll=4)

    def step4(k, carry):
        g4[k] = pick(t4, i4[pl.ds(k, 1), :], n4)
        return carry

    lax.fori_loop(0, k4, step4, 0, unroll=4)
    weigh(c3, g3, s3, k3, c3.shape[0] // k3, n3)
    weigh(c4, g4, s4, k4, c4.shape[0] // k4, n4)
    p3[...] = nn(w3t[...], s3[...])
    p4[...] = nn(w4t[...], s4[...])


def mix_body(
    edge, radial, p3, p4, trow, wu3, wu4, wsk, wr1, wr2, wra, wat, atom,
    merged, mixlow, reshid, dsk, du3, du4, dr1, dr2, gath, anew, aslope, acc,
):
    step = pl.program_id(0)
    atoms = acc.shape[0]
    v3 = p3[...]
    v4 = p4[...]
    h3 = (v3 * sigma(v3)).T.astype(LOW)
    h4 = (v4 * sigma(v4)).T.astype(LOW)
    up3 = nn(h3, wu3[...])
    s = sigma(up3)
    du3[...] = slope_of(up3, s).astype(LOW)
    total = up3 * s
    up4 = nn(h4, wu4[...])
    s = sigma(up4)
    du4[...] = slope_of(up4, s).astype(LOW)
    total = total + up4 * s
    skip = nn(edge[...], wsk[...])
    s = sigma(skip)
    dsk[...] = slope_of(skip, s).astype(LOW)
    mixed = (total + skip * s) * THIRD_ROOT
    low_mixed = mixed.astype(LOW)
    mixlow[...] = low_mixed
    res = nn(low_mixed, wr1[...])
    s = sigma(res)
    dr1[...] = slope_of(res, s).astype(LOW)
    hid = (res * s).astype(LOW)
    reshid[...] = hid
    res2 = nn(hid, wr2[...])
    s = sigma(res2)
    dr2[...] = (0.5 * slope_of(res2, s)).astype(LOW)
    out = (edge[...].astype(WIDE) + (mixed + res2 * s) * HALF_ROOT) * HALF_ROOT
    merged[...] = out
    weighted = (out * nn(radial[...], wra[...])).astype(LOW)
    hot_t = (lax.broadcasted_iota(jnp.int32, (atoms, TILE), 0) == trow[...]).astype(LOW)
    part = nn(hot_t, weighted)

    @pl.when(step == 0)
    def _():
        acc[...] = part

    @pl.when(step > 0)
    def _():
        acc[...] += part

    @pl.when(step == pl.num_programs(0) - 1)
    def _():
        g = acc[...].astype(LOW)
        gath[...] = g
        pre = nn(g, wat[...])
        sa = sigma(pre)
        aslope[...] = HALF_ROOT * slope_of(pre, sa)
        anew[...] = ((atom[...].astype(WIDE) + pre * sa) * HALF_ROOT).astype(LOW)


def out_body(
    merged, radial, trow, tcol, anew, cot, wc, wro, wout, ocot, acot, aslope, gath, wat,
    enew, gmer, gwc, gro, goa, aout, gatom, gw2, ogat, seg, both, awc, aro,
):
    step = pl.program_id(0)
    atoms, wide = ogat.shape
    aw = anew.shape[1]

    @pl.when(step == 0)
    def _():
        both[:, 0:wide] = split_pair(nt(ocot[...], wout[...]))
        both[:, wide : 2 * wide] = split_pair(nn(anew[...], wc[0:aw, :]))
        ogat[...] = jnp.zeros_like(ogat)
        seg[...] = jnp.zeros_like(seg)
        awc[...] = jnp.zeros_like(awc)
        aro[...] = jnp.zeros_like(aro)

    hot_t = (lax.broadcasted_iota(jnp.int32, (atoms, TILE), 0) == trow[...]).astype(LOW)
    lane = lax.broadcasted_iota(jnp.int32, (TILE, 2 * atoms), 1)
    hot = ((lane & (atoms - 1)) == tcol[...]).astype(LOW)
    spread = nn(hot, both[...])
    gow = spread[:, 0:wide]
    m = merged[...]
    ml = m.astype(LOW)
    wcm = wc[aw:, :]
    pre = spread[:, wide:] + nn(ml, wcm)
    s = sigma(pre)
    new = (m + pre * s) * HALF_ROOT
    enew[...] = new.astype(LOW)
    rout = nn(radial[...], wro[...])
    ogat[...] += nn(hot_t, (new * rout).astype(LOW))
    gnew = cot[...].astype(WIDE) + gow * rout
    aro[...] += tn(radial[...], (gow * new).astype(LOW))
    lc = (gnew * (HALF_ROOT * slope_of(pre, s))).astype(LOW)
    awc[...] += tn(ml, lc)
    seg[...] += nn(hot_t, lc)
    gmer[...] = gnew * HALF_ROOT + nt(lc, wcm)

    @pl.when(step == pl.num_programs(0) - 1)
    def _():
        ol = ogat[...].astype(LOW)
        aout[...] = nn(ol, wout[...]).astype(LOW)
        goa[:, 0:aw] = tn(ol, ocot[...]).astype(LOW)
        gwc[aw:, :] = awc[...].astype(LOW)
        gro[...] = aro[...].astype(LOW)
        pair = split_pair(seg[...])
        hi = pair[0:atoms, :]
        lo = pair[atoms:, :]
        gwc[0:aw, :] = (tn(anew[...], hi) + tn(anew[...], lo)).astype(LOW)
        wca = wc[0:aw, :]
        ga = acot[...].astype(WIDE) + nt(hi, wca) + nt(lo, wca)
        gatom[...] = (ga * HALF_ROOT).astype(LOW)
        la = (ga * aslope[...]).astype(LOW)
        goa[:, aw : 2 * aw] = tn(gath[...], la).astype(LOW)
        gw2[...] = split_pair(nt(la, wat[...]))


def back_body(
    edge, radial, tcol, merged, gmer, gw2, p3, p4, mixlow, reshid, dsk, du3, du4, dr1, dr2,
    wu3, wu4, wsk, wr1, wr2, wra,
    gpart, lb3, lb4, gsk, gr1, gr2, gra, gup, ask, ar1, ar2, ara, aup,
):
    step = pl.program_id(0)
    pair = gw2.shape[0]
    n3 = wu3.shape[0]

    @pl.when(step == 0)
    def _():
        ask[...] = jnp.zeros_like(ask)
        ar1[...] = jnp.zeros_like(ar1)
        ar2[...] = jnp.zeros_like(ar2)
        ara[...] = jnp.zeros_like(ara)
        aup[...] = jnp.zeros_like(aup)

    lane = lax.broadcasted_iota(jnp.int32, (TILE, pair), 1)
    hot = ((lane & (pair // 2 - 1)) == tcol[...]).astype(LOW)
    gw = nn(hot, gw2[...])
    gm = gmer[...] + gw * nn(radial[...], wra[...])
    ara[...] += tn(radial[...], (gw * merged[...]).astype(LOW))
    l2 = (gm * dr2[...].astype(WIDE)).astype(LOW)
    ar2[...] += tn(reshid[...], l2)
    l1 = (nt(l2, wr2[...]) * dr1[...].astype(WIDE)).astype(LOW)
    ar1[...] += tn(mixlow[...], l1)
    gmix = (gm * 0.5 + nt(l1, wr1[...])) * THIRD_ROOT
    ls = (gmix * dsk[...].astype(WIDE)).astype(LOW)
    l3 = (gmix * du3[...].astype(WIDE)).astype(LOW)
    l4 = (gmix * du4[...].astype(WIDE)).astype(LOW)
    ask[...] += tn(edge[...], ls)
    gpart[...] = gm * HALF_ROOT + nt(ls, wsk[...])
    v3 = p3[...]
    s3 = sigma(v3)
    v4 = p4[...]
    s4 = sigma(v4)
    aup[0:n3, :] += nn((v3 * s3).astype(LOW), l3)
    aup[n3:, :] += nn((v4 * s4).astype(LOW), l4)
    lb3[...] = (nt(wu3[...], l3) * slope_of(v3, s3)).astype(LOW)
    lb4[...] = (nt(wu4[...], l4) * slope_of(v4, s4)).astype(LOW)

    @pl.when(step == pl.num_programs(0) - 1)
    def _():
        gsk[...] = ask[...].astype(LOW)
        gr1[...] = ar1[...].astype(LOW)
        gr2[...] = ar2[...].astype(LOW)
        gra[...] = ara[...].astype(LOW)
        gup[...] = aup[...].T.astype(LOW)


def unweigh(coef, dsum, index, spread, hots, slots, basis, width):
    chunk = 32
    slabs = spread.shape[0] // width
    for k in range(slots):
        low_part = index[k : k + 1, :] & (TILE - 1)
        hot = (lax.broadcasted_iota(jnp.int32, (TILE, TILE), 0) == low_part).astype(LOW)
        hots[:, k * TILE : (k + 1) * TILE] = hot
    for h in range(width // chunk):
        for kb in range(slots // 4):
            acc = [None] * 4
            for c in range(basis):
                at = c * width + h * chunk
                d = dsum[at : at + chunk, :]
                for j in range(4):
                    row = (kb * 4 + j) * basis + c
                    term = coef[row : row + 1, :] * d
                    acc[j] = term if acc[j] is None else acc[j] + term
            for j in range(4):
                k = kb * 4 + j
                slab = index[k : k + 1, :] >> 8
                for s in range(slabs):
                    at = s * width + h * chunk
                    spread[at : at + chunk, k * TILE : (k + 1) * TILE] = jnp.where(
                        slab == s, acc[j], 0.0
                    ).astype(LOW)


def scatter_body(
    lb3, lb4, i3, i4, b3, b4, w3, w4, s3, s4, grad, gbil, a3, a4, abil, c3, c4, d3, d4, v3, v4, h3, h4
):
    step = pl.program_id(0)
    n3, n4 = w3.shape[1], w4.shape[1]
    k3, k4 = i3.shape[0], i4.shape[0]

    @pl.when(step == 0)
    def _():
        a3[...] = jnp.zeros_like(a3)
        a4[...] = jnp.zeros_like(a4)
        abil[...] = jnp.zeros_like(abil)

    c3[...] = b3[...].astype(WIDE).T
    c4[...] = b4[...].astype(WIDE).T
    d3[...] = nn(w3[...], lb3[...])
    d4[...] = nn(w4[...], lb4[...])
    abil[:, 0:n3] += nt(s3[...], lb3[...])
    abil[:, n3 : n3 + n4] += nt(s4[...], lb4[...])
    unweigh(c3, d3, i3, v3, h3, k3, c3.shape[0] // k3, n3)
    a3[...] += nt(v3[...], h3[...])
    unweigh(c4, d4, i4, v4, h4, k4, c4.shape[0] // k4, n4)
    a4[...] += nt(v4[...], h4[...])

    @pl.when(step == pl.num_programs(0) - 1)
    def _():
        for s in range(a3.shape[0] // n3):
            grad[0:n3, s * TILE : (s + 1) * TILE] = a3[s * n3 : (s + 1) * n3, :]
            grad[n3 : n3 + n4, s * TILE : (s + 1) * TILE] = a4[s * n4 : (s + 1) * n4, :]
        gbil[...] = abil[...].astype(LOW)


def source_back_body(
    edge, radial, gpart, grad, down, ret, ask, ws3, wr3, wd3, ws4, wr4, wd4,
    gedge, gs3, gs4, gr3, gr4, gdn, as3, as4, ar3, ar4, adn,
):
    step = pl.program_id(0)
    n3 = wd3.shape[0]

    @pl.when(step == 0)
    def _():
        as3[...] = jnp.zeros_like(as3)
        as4[...] = jnp.zeros_like(as4)
        ar3[...] = jnp.zeros_like(ar3)
        ar4[...] = jnp.zeros_like(ar4)
        adn[...] = jnp.zeros_like(adn)

    lane = lax.broadcasted_iota(jnp.int32, (ask.shape[0], TILE), 1) + step * TILE
    back = nn(ret[...], (lane == ask[...]).astype(LOW))
    v = down[...]
    ld = (grad[...] + back) * slope_of(v, sigma(v))
    ldt = ld.astype(LOW)
    low_rows = ld.T.astype(LOW)
    e = edge[...]
    r = radial[...]
    pre = nn(e, ws3[...])
    rad = nn(r, wr3[...])
    s = sigma(pre)
    act = pre * s
    adn[0:n3, :] += nn(ldt[0:n3, :], (act * rad).astype(LOW))
    gm = nn(low_rows[:, 0:n3], wd3[...])
    l3 = (gm * rad * slope_of(pre, s)).astype(LOW)
    ar3[...] += tn(r, (gm * act).astype(LOW))
    as3[...] += tn(e, l3)
    pre = nn(e, ws4[...])
    rad = nn(r, wr4[...])
    s = sigma(pre)
    act = pre * s
    adn[n3:, :] += nn(ldt[n3:, :], (act * rad).astype(LOW))
    gm = nn(low_rows[:, n3:], wd4[...])
    l4 = (gm * rad * slope_of(pre, s)).astype(LOW)
    ar4[...] += tn(r, (gm * act).astype(LOW))
    as4[...] += tn(e, l4)
    gedge[...] = (gpart[...] + nt(l3, ws3[...]) + nt(l4, ws4[...])).astype(LOW)

    @pl.when(step == pl.num_programs(0) - 1)
    def _():
        gs3[...] = as3[...].astype(LOW)
        gs4[...] = as4[...].astype(LOW)
        gr3[...] = ar3[...].astype(LOW)
        gr4[...] = ar4[...].astype(LOW)
        gdn[...] = adn[...].T.astype(LOW)


def swap(v, axis, bit):
    count = lax.axis_size(axis)
    return lax.ppermute(v, axis, [(j, j ^ (1 << bit)) for j in range(count)])


def bits_of(axis):
    return range(lax.axis_size(axis).bit_length() - 1)


def reduce_shares(packed):
    v = packed
    place = lax.axis_index("edge")
    for bit in bits_of("edge"):
        side = (place >> bit) & 1
        v = v.reshape(v.shape[0] // 2, 2, *v.shape[1:])
        kept = lax.dynamic_index_in_dim(v, side, 1, keepdims=False)
        sent = lax.dynamic_index_in_dim(v, 1 - side, 1, keepdims=False)
        got = swap(sent, "edge", bit)
        v = (kept.astype(WIDE) + got.astype(WIDE)).astype(LOW)
    v = v[0]
    last = bits_of("grp")[-1]
    for bit in bits_of("grp"):
        v = v.astype(WIDE) + swap(v, "grp", bit).astype(WIDE)
        if bit != last:
            v = v.astype(LOW)
    return v


def by_rows(g, count):
    return g.reshape(count, g.shape[0] // count, g.shape[1])


def fold(g, count):
    parts = g.reshape(count, 4, g.shape[0] // count // 4, g.shape[1])
    parts = jnp.pad(parts, ((0, 0), (0, 0), (0, 0), (0, 128 - g.shape[1])))
    return jnp.concatenate([parts[:, q] for q in range(4)], axis=2)


def unfold(g):
    return jnp.concatenate([g[:, q * 128 : q * 128 + 96] for q in range(4)], axis=0)


def per_device(
    edge_embed, atom_embed, radial_basis, triplet_basis, quadruplet_basis,
    triplet_source_row, triplet_mask, quadruplet_source_row, quadruplet_mask,
    edge_target_atom, borrowed_edges,
    w_source_trip, w_rbf_trip, w_down_trip, w_source_quad, w_rbf_quad, w_down_quad,
    triplet_bilinear_weight, w_up_trip, w_bilinear_quad, w_up_quad, w_skip,
    w_res_first, w_res_second, w_rbf_atom, w_atom, w_concat, w_rbf_out, w_out,
    edge_cotangent, atom_cotangent, output_cotangent,
):
    edges, wide = edge_embed.shape
    atoms, aw = atom_embed.shape
    rbf = radial_basis.shape[1]
    peers = lax.axis_size("edge")
    cap = borrowed_edges.shape[2]
    steps = edges // TILE
    n3, n4 = w_down_trip.shape[1], w_down_quad.shape[1]
    nb = n3 + n4
    k3, k4 = triplet_mask.shape[1], quadruplet_mask.shape[1]
    f3, f4 = triplet_bilinear_weight.shape[0], w_bilinear_quad.shape[0]
    q3, q4 = triplet_basis.shape[1], quadruplet_basis.shape[1]
    ghosts = peers * cap
    ghosts_up = -(-ghosts // TILE) * TILE
    slabs = (edges + ghosts_up) // TILE

    wanted = borrowed_edges[0] - (jnp.arange(peers, dtype=jnp.int32) * edges)[:, None]
    asked = lax.all_to_all(wanted, "edge", split_axis=0, concat_axis=0, tiled=True).reshape(-1)

    wd3t, wd4t = w_down_trip.T, w_down_quad.T
    w3t, w4t = triplet_bilinear_weight.T, w_bilinear_quad.T
    i3 = jnp.where(triplet_mask > 0, triplet_source_row, -1).T
    i4 = jnp.where(quadruplet_mask > 0, quadruplet_source_row, -1).T
    trow = edge_target_atom
    tcol = edge_target_atom.reshape(edges, 1)

    src_ins = (edge_embed, radial_basis, w_source_trip, w_rbf_trip, wd3t, w_source_quad, w_rbf_quad, wd4t)
    table, down = call(
        source_body, "source_rows", steps, src_ins,
        [rows(wide), rows(rbf)] + [whole(w) for w in src_ins[2:]],
        [((nb, edges), LOW), ((nb, edges), WIDE)],
        [cols(nb), cols(nb)],
        [],
    )

    hot_out = (asked[:, None] == jnp.arange(edges, dtype=jnp.int32)[None, :]).astype(LOW)
    outgoing = nt(hot_out, table).astype(LOW).reshape(peers, -1)
    ghost = lax.all_to_all(outgoing, "edge", split_axis=0, concat_axis=0, tiled=True)
    ghost = jnp.pad(ghost.reshape(ghosts, nb).T, ((0, 0), (0, ghosts_up - ghosts)))

    s3, s4, p3, p4 = call(
        gather_body, "gather_sums", steps,
        (table, ghost, i3, i4, triplet_basis, quadruplet_basis, w3t, w4t),
        [whole(table), whole(ghost), cols(k3), cols(k4), rows(q3), rows(q4), whole(w3t), whole(w4t)],
        [((f3, edges), LOW), ((f4, edges), LOW), ((n3, edges), WIDE), ((n4, edges), WIDE)],
        [cols(f3), cols(f4), cols(n3), cols(n4)],
        [
            pltpu.VMEM((slabs * n3, TILE), LOW), pltpu.VMEM((slabs * n4, TILE), LOW),
            pltpu.VMEM((k3, n3, TILE), WIDE), pltpu.VMEM((k4, n4, TILE), WIDE),
            pltpu.VMEM((q3, TILE), WIDE), pltpu.VMEM((q4, TILE), WIDE),
        ],
    )

    act = ((edges, wide), LOW)
    merged, mixlow, reshid, dsk, du3, du4, dr1, dr2, gath, anew, aslope = call(
        mix_body, "edge_update", steps,
        (edge_embed, radial_basis, p3, p4, trow, w_up_trip, w_up_quad, w_skip, w_res_first,
         w_res_second, w_rbf_atom, w_atom, atom_embed),
        [rows(wide), rows(rbf), cols(n3), cols(n4), cols(1)]
        + [whole(w) for w in (w_up_trip, w_up_quad, w_skip, w_res_first, w_res_second, w_rbf_atom, w_atom, atom_embed)],
        [((edges, wide), WIDE), act, act, act, act, act, act, act,
         ((atoms, wide), LOW), ((atoms, aw), LOW), ((atoms, aw), WIDE)],
        [rows(wide)] * 8 + [fixed(atoms, wide), fixed(atoms, aw), fixed(atoms, aw)],
        [pltpu.VMEM((atoms, wide), WIDE)],
    )

    enew, gmer, gwc, gro, goa, aout, gatom, gw2 = call(
        out_body, "output_block", steps,
        (merged, radial_basis, trow, tcol, anew, edge_cotangent, w_concat, w_rbf_out, w_out,
         output_cotangent, atom_cotangent, aslope, gath, w_atom),
        [rows(wide), rows(rbf), cols(1), rows(1), whole(anew), rows(wide)]
        + [whole(w) for w in (w_concat, w_rbf_out, w_out, output_cotangent, atom_cotangent, aslope, gath, w_atom)],
        [act, ((edges, wide), WIDE), (w_concat.shape, LOW), (w_rbf_out.shape, LOW),
         ((wide, 2 * aw), LOW), ((atoms, aw), LOW), ((atoms, aw), LOW), ((2 * atoms, wide), LOW)],
        [rows(wide), rows(wide), whole(w_concat), whole(w_rbf_out), fixed(wide, 2 * aw),
         fixed(atoms, aw), fixed(atoms, aw), fixed(2 * atoms, wide)],
        [
            pltpu.VMEM((atoms, wide), WIDE), pltpu.VMEM((atoms, wide), WIDE),
            pltpu.VMEM((2 * atoms, 2 * wide), LOW),
            pltpu.VMEM((w_concat.shape[0] - aw, wide), WIDE), pltpu.VMEM(w_rbf_out.shape, WIDE),
        ],
    )
    first = jnp.concatenate([by_rows(gwc, peers), by_rows(goa, peers), by_rows(gro, peers)], axis=1)
    first = reduce_shares(first)

    gpart, lb3, lb4, gsk, gr1, gr2, gra, gup = call(
        back_body, "edge_update_back", steps,
        (edge_embed, radial_basis, tcol, merged, gmer, gw2, p3, p4, mixlow, reshid, dsk, du3, du4,
         dr1, dr2, w_up_trip, w_up_quad, w_skip, w_res_first, w_res_second, w_rbf_atom),
        [rows(wide), rows(rbf), rows(1), rows(wide), rows(wide), whole(gw2), cols(n3), cols(n4)]
        + [rows(wide)] * 7
        + [whole(w) for w in (w_up_trip, w_up_quad, w_skip, w_res_first, w_res_second, w_rbf_atom)],
        [((edges, wide), WIDE), ((n3, edges), LOW), ((n4, edges), LOW), (w_skip.shape, LOW),
         (w_skip.shape, LOW), (w_skip.shape, LOW), (w_rbf_atom.shape, LOW), ((wide, nb), LOW)],
        [rows(wide), cols(n3), cols(n4), whole(w_skip), whole(w_skip), whole(w_skip),
         whole(w_rbf_atom), fixed(wide, nb)],
        [pltpu.VMEM(w_skip.shape, WIDE)] * 3
        + [pltpu.VMEM(w_rbf_atom.shape, WIDE), pltpu.VMEM((nb, wide), WIDE)],
    )

    grad, gbil = call(
        scatter_body, "scatter_sums", steps,
        (lb3, lb4, i3, i4, triplet_basis, quadruplet_basis, triplet_bilinear_weight, w_bilinear_quad, s3, s4),
        [cols(n3), cols(n4), cols(k3), cols(k4), rows(q3), rows(q4), whole(triplet_bilinear_weight),
         whole(w_bilinear_quad), cols(f3), cols(f4)],
        [((nb, slabs * TILE), WIDE), ((f3, nb), LOW)],
        [fixed(nb, slabs * TILE), fixed(f3, nb)],
        [
            pltpu.VMEM((slabs * n3, TILE), WIDE), pltpu.VMEM((slabs * n4, TILE), WIDE),
            pltpu.VMEM((f3, nb), WIDE),
            pltpu.VMEM((q3, TILE), WIDE), pltpu.VMEM((q4, TILE), WIDE),
            pltpu.VMEM((f3, TILE), WIDE), pltpu.VMEM((f4, TILE), WIDE),
            pltpu.VMEM((slabs * n3, k3 * TILE), LOW), pltpu.VMEM((slabs * n4, k4 * TILE), LOW),
            pltpu.VMEM((TILE, k3 * TILE), LOW), pltpu.VMEM((TILE, k4 * TILE), LOW),
        ],
    )
    second = jnp.concatenate(
        [by_rows(gsk, peers), by_rows(gr1, peers), by_rows(gr2, peers), by_rows(gra, peers),
         fold(gup, peers), fold(gbil, peers)],
        axis=1,
    )
    second = reduce_shares(second)

    back = grad[:, edges : edges + ghosts].astype(LOW).T.reshape(peers, -1)
    back = lax.all_to_all(back, "edge", split_axis=0, concat_axis=0, tiled=True)
    back = back.reshape(ghosts, nb).T
    askcol = asked.reshape(ghosts, 1)

    sb_ins = (edge_embed, radial_basis, gpart, grad, down, back, askcol) + src_ins[2:]
    gedge, gs3, gs4, gr3, gr4, gdn = call(
        source_back_body, "source_rows_back", steps, sb_ins,
        [rows(wide), rows(rbf), rows(wide), cols(nb), cols(nb), whole(back), whole(askcol)]
        + [whole(w) for w in src_ins[2:]],
        [act, (w_skip.shape, LOW), (w_skip.shape, LOW), (w_rbf_trip.shape, LOW),
         (w_rbf_trip.shape, LOW), ((wide, nb), LOW)],
        [rows(wide), whole(w_skip), whole(w_skip), whole(w_rbf_trip), whole(w_rbf_trip), fixed(wide, nb)],
        [pltpu.VMEM(w_skip.shape, WIDE)] * 2
        + [pltpu.VMEM(w_rbf_trip.shape, WIDE)] * 2
        + [pltpu.VMEM((nb, wide), WIDE)],
    )
    third = jnp.concatenate(
        [by_rows(gs3, peers), by_rows(gs4, peers), by_rows(gr3, peers), by_rows(gr4, peers), fold(gdn, peers)],
        axis=1,
    )
    third = reduce_shares(third)

    a = wide // peers
    b = rbf // peers
    c = w_concat.shape[0] // peers
    r_concat = first[0:c]
    r_oa = first[c : c + a]
    r_out = first[c + a : c + a + b]
    r_sk = second[0:a]
    r_r1 = second[a : 2 * a]
    r_r2 = second[2 * a : 3 * a]
    r_ra = second[3 * a : 3 * a + b]
    at = 3 * a + b
    r_up = unfold(second[at : at + a // 4]).T
    r_bil = unfold(second[at + a // 4 :])
    r_s3 = third[0:a]
    r_s4 = third[a : 2 * a]
    r_r3 = third[2 * a : 2 * a + b]
    r_r4 = third[2 * a + b : 2 * a + 2 * b]
    r_dn = unfold(third[2 * a + 2 * b :])
    return (
        enew, anew, aout, gedge, gatom,
        r_s3, r_r3, r_dn[:, 0:n3], r_s4, r_r4, r_dn[:, n3:],
        r_bil[:, 0:n3], r_up[0:n3], r_bil[:, n3:], r_up[n3:],
        r_sk, r_r1, r_r2, r_ra, r_oa[:, aw:], r_concat, r_out, r_oa[:, 0:aw],
    )


def solution(mesh):
    both = P(("grp", "edge"), None)
    placed = (both,) * 10 + (P(("grp", "edge"), None, None),) + (P(),) * 18 + (both,) * 3
    shares = [P("edge", None)] * 18
    shares[7] = P(None, "edge")
    shares[9] = P(None, "edge")
    return jax.shard_map(
        per_device, mesh=mesh, in_specs=placed, out_specs=(both,) * 5 + tuple(shares), check_vma=False
    )
```

```python
import functools
import math

import jax
import jax.numpy as jnp
from jax import lax
from jax.experimental import pallas as pl
from jax.experimental.pallas import tpu as pltpu
from jax.sharding import PartitionSpec as P

HALF_ROOT = 1.0 / math.sqrt(2.0)
THIRD_ROOT = 1.0 / math.sqrt(3.0)
LOW = jnp.bfloat16
WIDE = jnp.float32
TILE = 256
LANES = 128
VMEM_BYTES = 60 * 1024 * 1024


def sigma(v):
    return 0.5 * jnp.tanh(0.5 * v) + 0.5


def slope_of(v, s):
    return s * (1.0 + v * (1.0 - s))


def nn(a, b):
    return jnp.dot(a, b, preferred_element_type=WIDE)


def nt(a, b):
    return lax.dot_general(a, b, (((1,), (1,)), ((), ())), preferred_element_type=WIDE)


def tn(a, b):
    return lax.dot_general(a, b, (((0,), (0,)), ((), ())), preferred_element_type=WIDE)


def split_pair(v):
    high = v.astype(LOW)
    rest = (v - high.astype(WIDE)).astype(LOW)
    return jnp.concatenate([high, rest], axis=0)


def whole(array):
    rank = len(array.shape)
    return pl.BlockSpec(array.shape, lambda i: (0,) * rank)


def rows(width):
    return pl.BlockSpec((TILE, width), lambda i: (i, 0))


def cols(height):
    return pl.BlockSpec((height, TILE), lambda i: (0, i))


def fixed(*shape):
    return pl.BlockSpec(shape, lambda i: (0,) * len(shape))


def call(body, name, steps, micros, ins, in_specs, outs, out_specs, scratch):
    return pl.pallas_call(
        body,
        name=name,
        out_shape=[jax.ShapeDtypeStruct(s, t) for s, t in outs],
        grid_spec=pltpu.PrefetchScalarGridSpec(
            num_scalar_prefetch=0,
            grid=(steps,),
            in_specs=in_specs,
            out_specs=out_specs,
            scratch_shapes=scratch,
        ),
        compiler_params=pltpu.CompilerParams(
            dimension_semantics=("arbitrary",), vmem_limit_bytes=VMEM_BYTES
        ),
        cost_estimate=pl.CostEstimate(
            flops=int(micros * 1.1e9), transcendentals=0, bytes_accessed=1 << 22
        ),
    )(*ins)


def source_body(
    edge, radial, asked, ws3, wr3, wd3, ws4, wr4, wd4, table, down, sent, t3, t4, acc
):
    step = pl.program_id(0)
    ghosts = asked.shape[1]

    @pl.when(step == 0)
    def _():
        t3[...] = wd3[...].astype(WIDE).T.astype(LOW)
        t4[...] = wd4[...].astype(WIDE).T.astype(LOW)
        acc[...] = jnp.zeros_like(acc)

    e = edge[...]
    r = radial[...]
    pre3 = nn(e, ws3[...])
    mix3 = (pre3 * sigma(pre3) * nn(r, wr3[...])).astype(LOW)
    down3 = nt(t3[...], mix3)
    pre4 = nn(e, ws4[...])
    mix4 = (pre4 * sigma(pre4) * nn(r, wr4[...])).astype(LOW)
    down4 = nt(t4[...], mix4)
    both = jnp.concatenate([down3, down4], axis=0)
    down[...] = both
    found = (both * sigma(both)).astype(LOW)
    table[...] = found
    place = lax.broadcasted_iota(jnp.int32, (TILE, ghosts), 0) + step * TILE
    acc[0 : found.shape[0], :] += nn(found, (place == asked[...]).astype(LOW))

    @pl.when(step == pl.num_programs(0) - 1)
    def _():
        sent[...] = acc[...].T.astype(LOW)


def fill_slabs(tab, ghost, t3, t4, n3, n4):
    local = tab.shape[1] // TILE
    for s in range(local):
        t3[s * n3 : (s + 1) * n3, :] = tab[0:n3, s * TILE : (s + 1) * TILE]
        t4[s * n4 : (s + 1) * n4, :] = tab[n3 : n3 + n4, s * TILE : (s + 1) * TILE]
    for g in range(0, ghost.shape[0], TILE):
        s = local + g // TILE
        size = min(TILE, ghost.shape[0] - g)
        part = ghost[g : g + size, :].astype(WIDE).T
        if size < TILE:
            part = jnp.concatenate([part, jnp.zeros((LANES, TILE - size), WIDE)], axis=1)
        t3[s * n3 : (s + 1) * n3, :] = part[0:n3, :].astype(LOW)
        t4[s * n4 : (s + 1) * n4, :] = part[n3 : n3 + n4, :].astype(LOW)


def pick(tab, index_row, width):
    slabs = tab.shape[0] // width
    low_part = index_row & (TILE - 1)
    slab = index_row >> 8
    hot = (lax.broadcasted_iota(jnp.int32, (TILE, TILE), 0) == low_part).astype(LOW)
    found = nn(tab[...], hot)
    got = jnp.zeros((width, TILE), WIDE)
    for s in range(slabs):
        got = jnp.where(slab == s, found[s * width : (s + 1) * width, :], got)
    return got


def weigh(coef, picked, out, slots, basis, width):
    chunk = 32
    for h in range(width // chunk):
        for cb in range(basis // 4):
            acc = [None] * 4
            for k in range(slots):
                g = picked[k, h * chunk : (h + 1) * chunk, :]
                for j in range(4):
                    row = k * basis + cb * 4 + j
                    term = coef[row : row + 1, :] * g
                    acc[j] = term if acc[j] is None else acc[j] + term
            for j in range(4):
                at = (cb * 4 + j) * width + h * chunk
                out[at : at + chunk, :] = acc[j].astype(LOW)


def gather_body(
    tab, ghost, i3, i4, b3, b4, w3, w4, s3, s4, p3, p4, t3, t4, g3, g4, c3, c4, w3t, w4t
):
    n3, n4 = w3t.shape[0], w4t.shape[0]
    k3, k4 = i3.shape[0], i4.shape[0]

    @pl.when(pl.program_id(0) == 0)
    def _():
        w3t[...] = w3[...].astype(WIDE).T.astype(LOW)
        w4t[...] = w4[...].astype(WIDE).T.astype(LOW)
        fill_slabs(tab, ghost, t3, t4, n3, n4)

    c3[...] = b3[...].astype(WIDE).T
    c4[...] = b4[...].astype(WIDE).T

    def step3(k, carry):
        g3[k] = pick(t3, i3[pl.ds(k, 1), :], n3)
        return carry

    lax.fori_loop(0, k3, step3, 0, unroll=4)

    def step4(k, carry):
        g4[k] = pick(t4, i4[pl.ds(k, 1), :], n4)
        return carry

    lax.fori_loop(0, k4, step4, 0, unroll=4)
    weigh(c3, g3, s3, k3, c3.shape[0] // k3, n3)
    weigh(c4, g4, s4, k4, c4.shape[0] // k4, n4)
    p3[...] = nn(w3t[...], s3[...])
    p4[...] = nn(w4t[...], s4[...])


def mix_body(
    edge, radial, p3, p4, trow, wu3, wu4, wsk, wr1, wr2, wra, wat, atom,
    merged, mixlow, reshid, dsk, du3, du4, dr1, dr2, gath, anew, aslope, acc,
):
    step = pl.program_id(0)
    atoms = acc.shape[0]
    v3 = p3[...]
    v4 = p4[...]
    h3 = (v3 * sigma(v3)).T.astype(LOW)
    h4 = (v4 * sigma(v4)).T.astype(LOW)
    up3 = nn(h3, wu3[...])
    s = sigma(up3)
    du3[...] = slope_of(up3, s).astype(LOW)
    total = up3 * s
    up4 = nn(h4, wu4[...])
    s = sigma(up4)
    du4[...] = slope_of(up4, s).astype(LOW)
    total = total + up4 * s
    skip = nn(edge[...], wsk[...])
    s = sigma(skip)
    dsk[...] = slope_of(skip, s).astype(LOW)
    mixed = (total + skip * s) * THIRD_ROOT
    low_mixed = mixed.astype(LOW)
    mixlow[...] = low_mixed
    res = nn(low_mixed, wr1[...])
    s = sigma(res)
    dr1[...] = slope_of(res, s).astype(LOW)
    hid = (res * s).astype(LOW)
    reshid[...] = hid
    res2 = nn(hid, wr2[...])
    s = sigma(res2)
    dr2[...] = (0.5 * slope_of(res2, s)).astype(LOW)
    out = (edge[...].astype(WIDE) + (mixed + res2 * s) * HALF_ROOT) * HALF_ROOT
    merged[...] = out
    weighted = (out * nn(radial[...], wra[...])).astype(LOW)
    hot_t = (lax.broadcasted_iota(jnp.int32, (atoms, TILE), 0) == trow[...]).astype(LOW)
    part = nn(hot_t, weighted)

    @pl.when(step == 0)
    def _():
        acc[...] = part

    @pl.when(step > 0)
    def _():
        acc[...] += part

    @pl.when(step == pl.num_programs(0) - 1)
    def _():
        g = acc[...].astype(LOW)
        gath[...] = g
        pre = nn(g, wat[...])
        sa = sigma(pre)
        aslope[...] = HALF_ROOT * slope_of(pre, sa)
        anew[...] = ((atom[...].astype(WIDE) + pre * sa) * HALF_ROOT).astype(LOW)


def out_body(
    merged, radial, trow, anew, cot, wc, wro, wout, ocot, acot, aslope, gath, wat,
    enew, gmer, gwc, gro, goa, aout, gatom, gw2, ogat, seg, both, awc, aro,
):
    step = pl.program_id(0)
    atoms, wide = ogat.shape
    aw = anew.shape[1]

    @pl.when(step == 0)
    def _():
        both[:, 0:wide] = split_pair(nt(ocot[...], wout[...]))
        both[:, wide : 2 * wide] = split_pair(nn(anew[...], wc[0:aw, :]))
        ogat[...] = jnp.zeros_like(ogat)
        seg[...] = jnp.zeros_like(seg)
        awc[...] = jnp.zeros_like(awc)
        aro[...] = jnp.zeros_like(aro)

    hot_t = (lax.broadcasted_iota(jnp.int32, (atoms, TILE), 0) == trow[...]).astype(LOW)
    spread = tn(jnp.concatenate([hot_t, hot_t], axis=0), both[...])
    gow = spread[:, 0:wide]
    m = merged[...]
    ml = m.astype(LOW)
    wcm = wc[aw:, :]
    pre = spread[:, wide:] + nn(ml, wcm)
    s = sigma(pre)
    new = (m + pre * s) * HALF_ROOT
    enew[...] = new.astype(LOW)
    rout = nn(radial[...], wro[...])
    ogat[...] += nn(hot_t, (new * rout).astype(LOW))
    gnew = cot[...].astype(WIDE) + gow * rout
    aro[...] += tn(radial[...], (gow * new).astype(LOW))
    lc = (gnew * (HALF_ROOT * slope_of(pre, s))).astype(LOW)
    awc[...] += tn(ml, lc)
    seg[...] += nn(hot_t, lc)
    gmer[...] = gnew * HALF_ROOT + nt(lc, wcm)

    @pl.when(step == pl.num_programs(0) - 1)
    def _():
        ol = ogat[...].astype(LOW)
        aout[...] = nn(ol, wout[...]).astype(LOW)
        goa[:, 0:aw] = tn(ol, ocot[...]).astype(LOW)
        gwc[aw:, :] = awc[...].astype(LOW)
        gro[...] = aro[...].astype(LOW)
        pair = split_pair(seg[...])
        hi = pair[0:atoms, :]
        lo = pair[atoms:, :]
        gwc[0:aw, :] = (tn(anew[...], hi) + tn(anew[...], lo)).astype(LOW)
        wca = wc[0:aw, :]
        ga = acot[...].astype(WIDE) + nt(hi, wca) + nt(lo, wca)
        gatom[...] = (ga * HALF_ROOT).astype(LOW)
        la = (ga * aslope[...]).astype(LOW)
        goa[:, aw : 2 * aw] = tn(gath[...], la).astype(LOW)
        gw2[...] = split_pair(nt(la, wat[...]))


def back_body(
    edge, radial, trow, s3, s4, merged, gmer, gw2, p3, p4, mixlow, reshid, dsk, du3, du4, dr1, dr2,
    wu3, wu4, wsk, wr1, wr2, wra,
    gpart, lb3, lb4, gsk, gr1, gr2, gra, gup, gbil, ask, ar1, ar2, ara, aup, abil,
):
    step = pl.program_id(0)
    pair = gw2.shape[0]
    n3 = wu3.shape[0]

    @pl.when(step == 0)
    def _():
        ask[...] = jnp.zeros_like(ask)
        ar1[...] = jnp.zeros_like(ar1)
        ar2[...] = jnp.zeros_like(ar2)
        ara[...] = jnp.zeros_like(ara)
        aup[...] = jnp.zeros_like(aup)
        abil[...] = jnp.zeros_like(abil)

    hot_t = (lax.broadcasted_iota(jnp.int32, (pair // 2, TILE), 0) == trow[...]).astype(LOW)
    gw = tn(jnp.concatenate([hot_t, hot_t], axis=0), gw2[...])
    gm = gmer[...] + gw * nn(radial[...], wra[...])
    ara[...] += tn(radial[...], (gw * merged[...]).astype(LOW))
    l2 = (gm * dr2[...].astype(WIDE)).astype(LOW)
    ar2[...] += tn(reshid[...], l2)
    l1 = (nt(l2, wr2[...]) * dr1[...].astype(WIDE)).astype(LOW)
    ar1[...] += tn(mixlow[...], l1)
    gmix = (gm * 0.5 + nt(l1, wr1[...])) * THIRD_ROOT
    ls = (gmix * dsk[...].astype(WIDE)).astype(LOW)
    l3 = (gmix * du3[...].astype(WIDE)).astype(LOW)
    l4 = (gmix * du4[...].astype(WIDE)).astype(LOW)
    ask[...] += tn(edge[...], ls)
    gpart[...] = gm * HALF_ROOT + nt(ls, wsk[...])
    v3 = p3[...]
    g3 = sigma(v3)
    v4 = p4[...]
    g4 = sigma(v4)
    aup[0:n3, :] += nn((v3 * g3).astype(LOW), l3)
    aup[n3:, :] += nn((v4 * g4).astype(LOW), l4)
    low3 = (nt(wu3[...], l3) * slope_of(v3, g3)).astype(LOW)
    low4 = (nt(wu4[...], l4) * slope_of(v4, g4)).astype(LOW)
    lb3[...] = low3
    lb4[...] = low4
    abil[:, 0:n3] += nt(s3[...], low3)
    abil[:, n3:] += nt(s4[...], low4)

    @pl.when(step == pl.num_programs(0) - 1)
    def _():
        gsk[...] = ask[...].astype(LOW)
        gr1[...] = ar1[...].astype(LOW)
        gr2[...] = ar2[...].astype(LOW)
        gra[...] = ara[...].astype(LOW)
        gup[...] = aup[...].T.astype(LOW)
        gbil[...] = abil[...].astype(LOW)


def unweigh(coef, dsum, index, spread, hots, slots, basis, width):
    chunk = 32
    slabs = spread.shape[0] // width
    for k in range(slots):
        low_part = index[k : k + 1, :] & (TILE - 1)
        hot = (lax.broadcasted_iota(jnp.int32, (TILE, TILE), 0) == low_part).astype(LOW)
        hots[:, k * TILE : (k + 1) * TILE] = hot
    for h in range(width // chunk):
        for kb in range(slots // 4):
            acc = [None] * 4
            for c in range(basis):
                at = c * width + h * chunk
                d = dsum[at : at + chunk, :]
                for j in range(4):
                    row = (kb * 4 + j) * basis + c
                    term = coef[row : row + 1, :] * d
                    acc[j] = term if acc[j] is None else acc[j] + term
            for j in range(4):
                k = kb * 4 + j
                slab = index[k : k + 1, :] >> 8
                for s in range(slabs):
                    at = s * width + h * chunk
                    spread[at : at + chunk, k * TILE : (k + 1) * TILE] = jnp.where(
                        slab == s, acc[j], 0.0
                    ).astype(LOW)


def scatter_body(lb, idx, basis, w, *rest, edges, other):
    if other:
        beside, grad, far, acc, coef, dsum, spread, hots = rest
    else:
        grad, far, acc, coef, dsum, spread, hots = rest
    step = pl.program_id(0)
    n = w.shape[1]
    slots = idx.shape[0]

    @pl.when(step == 0)
    def _():
        acc[...] = jnp.zeros_like(acc)

    coef[...] = basis[...].astype(WIDE).T
    dsum[...] = nn(w[...], lb[...])
    unweigh(coef, dsum, idx, spread, hots, slots, coef.shape[0] // slots, n)
    acc[...] += nt(spread[...], hots[...])

    @pl.when(step == pl.num_programs(0) - 1)
    def _():
        local = edges // TILE
        for s in range(local):
            grad[:, s * TILE : (s + 1) * TILE] = acc[s * n : (s + 1) * n, :]
        for s in range(local, acc.shape[0] // n):
            part = acc[s * n : (s + 1) * n, :]
            if other:
                more = beside[:, (s - local) * TILE : (s - local + 1) * TILE]
                filler = jnp.zeros((LANES - n - more.shape[0], TILE), WIDE)
                part = jnp.concatenate([part, more, filler], axis=0).T.astype(LOW)
                size = min(TILE, far.shape[0] - (s - local) * TILE)
                far[(s - local) * TILE : (s - local) * TILE + size, :] = part[0:size, :]
            else:
                far[:, (s - local) * TILE : (s - local + 1) * TILE] = part


def source_back_body(
    edge, radial, gpart, grad3, grad4, down, ret, asked, ws3, wr3, wd3, ws4, wr4, wd4,
    gedge, gs3, gs4, gr3, gr4, gdn, as3, as4, ar3, ar4, adn, t3, t4, rt,
):
    step = pl.program_id(0)
    n3, n4 = grad3.shape[0], grad4.shape[0]

    @pl.when(step == 0)
    def _():
        t3[...] = wd3[...].astype(WIDE).T.astype(LOW)
        t4[...] = wd4[...].astype(WIDE).T.astype(LOW)
        rt[...] = ret[...].astype(WIDE).T.astype(LOW)
        as3[...] = jnp.zeros_like(as3)
        as4[...] = jnp.zeros_like(as4)
        ar3[...] = jnp.zeros_like(ar3)
        ar4[...] = jnp.zeros_like(ar4)
        adn[...] = jnp.zeros_like(adn)

    place = lax.broadcasted_iota(jnp.int32, (TILE, asked.shape[1]), 0) + step * TILE
    back = nt(rt[...], (place == asked[...]).astype(LOW))
    v = down[...]
    ld = jnp.concatenate([grad3[...], grad4[...]], axis=0) + back[0 : n3 + n4, :]
    ld = ld * slope_of(v, sigma(v))
    ldt = ld.astype(LOW)
    low_rows = ld.T.astype(LOW)
    e = edge[...]
    r = radial[...]
    pre = nn(e, ws3[...])
    rad = nn(r, wr3[...])
    s = sigma(pre)
    act = pre * s
    adn[0:n3, :] += nn(ldt[0:n3, :], (act * rad).astype(LOW))
    gm = nn(low_rows[:, 0:n3], t3[...])
    l3 = (gm * rad * slope_of(pre, s)).astype(LOW)
    ar3[...] += tn(r, (gm * act).astype(LOW))
    as3[...] += tn(e, l3)
    pre = nn(e, ws4[...])
    rad = nn(r, wr4[...])
    s = sigma(pre)
    act = pre * s
    adn[n3:, :] += nn(ldt[n3:, :], (act * rad).astype(LOW))
    gm = nn(low_rows[:, n3:], t4[...])
    l4 = (gm * rad * slope_of(pre, s)).astype(LOW)
    ar4[...] += tn(r, (gm * act).astype(LOW))
    as4[...] += tn(e, l4)
    gedge[...] = (gpart[...] + nt(l3, ws3[...]) + nt(l4, ws4[...])).astype(LOW)

    @pl.when(step == pl.num_programs(0) - 1)
    def _():
        gs3[...] = as3[...].astype(LOW)
        gs4[...] = as4[...].astype(LOW)
        gr3[...] = ar3[...].astype(LOW)
        gr4[...] = ar4[...].astype(LOW)
        gdn[...] = adn[...].T.astype(LOW)


def swap(v, axis, mask):
    count = lax.axis_size(axis)
    return lax.ppermute(v, axis, [(j, j ^ mask) for j in range(count)])


def groups_of(axis, first):
    top = lax.axis_size(axis).bit_length() - 1
    return [(at, min(2, top - at)) for at in range(first, top, 2)]


def scatter_step(v, axis, at, width):
    parts = 1 << width
    own = (lax.axis_index(axis) >> at) & (parts - 1)
    v = v.reshape(v.shape[0] // parts, parts, *v.shape[1:])
    total = lax.dynamic_index_in_dim(v, own, 1, keepdims=False).astype(WIDE)
    for m in range(1, parts):
        sent = lax.dynamic_index_in_dim(v, own ^ m, 1, keepdims=False)
        total = total + swap(sent, axis, m << at).astype(WIDE)
    return total.astype(LOW)


def core_sum(v):
    return scatter_step(v, "edge", 0, 1)


def group_sum(v):
    own = lax.axis_index("grp")
    total = lax.dynamic_index_in_dim(v, own, 1, keepdims=False).astype(WIDE)
    for m in range(1, v.shape[1]):
        sent = lax.dynamic_index_in_dim(v, own ^ m, 1, keepdims=False)
        total = total + swap(sent, "grp", m).astype(WIDE)
    return total.astype(LOW)


def share_sum(v):
    for at, width in groups_of("edge", 1):
        v = scatter_step(v, "edge", at, width)
    return v[0]


def group_gather(v):
    own = lax.axis_index("grp")
    count = lax.axis_size("grp")
    out = jnp.zeros((count,) + v.shape, LOW)
    out = lax.dynamic_update_index_in_dim(out, v, own, 0)
    for m in range(1, count):
        out = lax.dynamic_update_index_in_dim(out, swap(v, "grp", m), own ^ m, 0)
    return out.astype(WIDE)


def exchange(v, peers):
    parts = v.reshape(peers, v.shape[0] // peers, v.shape[1])
    return lax.all_to_all(parts, "edge", split_axis=0, concat_axis=0, tiled=True).reshape(v.shape)


def by_rows(g, count):
    parts = g.reshape(count, g.shape[0] // count, g.shape[1])
    return jnp.stack([parts[:, :, q : q + 128] for q in range(0, g.shape[1], 128)], axis=1)


def fold(g, count):
    parts = g.reshape(count, 4, g.shape[0] // count // 4, g.shape[1])
    return jnp.pad(parts, ((0, 0), (0, 0), (0, 0), (0, 128 - g.shape[1])))


def wide_rows(g, start, stop):
    return jnp.concatenate([g[q, start:stop] for q in range(g.shape[0])], axis=1)


def unfold(g, start, stop, width):
    return g[:, start:stop, 0:width].reshape(g.shape[0] * (stop - start), width)


def per_device(
    edge_embed, atom_embed, radial_basis, triplet_basis, quadruplet_basis,
    triplet_source_row, triplet_mask, quadruplet_source_row, quadruplet_mask,
    edge_target_atom, borrowed_edges,
    w_source_trip, w_rbf_trip, w_down_trip, w_source_quad, w_rbf_quad, w_down_quad,
    triplet_bilinear_weight, w_up_trip, w_bilinear_quad, w_up_quad, w_skip,
    w_res_first, w_res_second, w_rbf_atom, w_atom, w_concat, w_rbf_out, w_out,
    edge_cotangent, atom_cotangent, output_cotangent,
):
    edges, wide = edge_embed.shape
    atoms, aw = atom_embed.shape
    rbf = radial_basis.shape[1]
    peers = lax.axis_size("edge")
    cap = borrowed_edges.shape[2]
    steps = edges // TILE
    n3, n4 = w_down_trip.shape[1], w_down_quad.shape[1]
    nb = n3 + n4
    k3, k4 = triplet_mask.shape[1], quadruplet_mask.shape[1]
    f3, f4 = triplet_bilinear_weight.shape[0], w_bilinear_quad.shape[0]
    q3, q4 = triplet_basis.shape[1], quadruplet_basis.shape[1]
    ghosts = peers * cap
    ghosts_up = -(-ghosts // TILE) * TILE
    slabs = (edges + ghosts_up) // TILE

    wanted = borrowed_edges[0] - (jnp.arange(peers, dtype=jnp.int32) * edges)[:, None]
    asked = lax.all_to_all(wanted, "edge", split_axis=0, concat_axis=0, tiled=True).reshape(1, ghosts)

    i3 = jnp.where(triplet_mask > 0, triplet_source_row, -1).T
    i4 = jnp.where(quadruplet_mask > 0, quadruplet_source_row, -1).T
    trow = edge_target_atom
    sources = (w_source_trip, w_rbf_trip, w_down_trip, w_source_quad, w_rbf_quad, w_down_quad)
    turned = [pltpu.VMEM((n3, wide), LOW), pltpu.VMEM((n4, wide), LOW)]

    table, down, sent = call(
        source_body, "source_rows", steps, 10, (edge_embed, radial_basis, asked) + sources,
        [rows(wide), rows(rbf), whole(asked)] + [whole(w) for w in sources],
        [((nb, edges), LOW), ((nb, edges), WIDE), ((ghosts, LANES), LOW)],
        [cols(nb), cols(nb), fixed(ghosts, LANES)],
        turned + [pltpu.VMEM((LANES, ghosts), WIDE)],
    )
    ghost = exchange(sent, peers)

    s3, s4, p3, p4 = call(
        gather_body, "gather_sums", steps, 38,
        (table, ghost, i3, i4, triplet_basis, quadruplet_basis, triplet_bilinear_weight, w_bilinear_quad),
        [whole(table), whole(ghost), cols(k3), cols(k4), rows(q3), rows(q4),
         whole(triplet_bilinear_weight), whole(w_bilinear_quad)],
        [((f3, edges), LOW), ((f4, edges), LOW), ((n3, edges), WIDE), ((n4, edges), WIDE)],
        [cols(f3), cols(f4), cols(n3), cols(n4)],
        [
            pltpu.VMEM((slabs * n3, TILE), LOW), pltpu.VMEM((slabs * n4, TILE), LOW),
            pltpu.VMEM((k3, n3, TILE), WIDE), pltpu.VMEM((k4, n4, TILE), WIDE),
            pltpu.VMEM((q3, TILE), WIDE), pltpu.VMEM((q4, TILE), WIDE),
            pltpu.VMEM((n3, f3), LOW), pltpu.VMEM((n4, f4), LOW),
        ],
    )

    act = ((edges, wide), LOW)
    ups = (w_up_trip, w_up_quad, w_skip, w_res_first, w_res_second, w_rbf_atom)
    merged, mixlow, reshid, dsk, du3, du4, dr1, dr2, gath, anew, aslope = call(
        mix_body, "edge_update", steps, 19,
        (edge_embed, radial_basis, p3, p4, trow) + ups + (w_atom, atom_embed),
        [rows(wide), rows(rbf), cols(n3), cols(n4), cols(1)] + [whole(w) for w in ups + (w_atom, atom_embed)],
        [((edges, wide), WIDE), act, act, act, act, act, act, act,
         ((atoms, wide), LOW), ((atoms, aw), LOW), ((atoms, aw), WIDE)],
        [rows(wide)] * 8 + [fixed(atoms, wide), fixed(atoms, aw), fixed(atoms, aw)],
        [pltpu.VMEM((atoms, wide), WIDE)],
    )

    outs = (w_concat, w_rbf_out, w_out, output_cotangent, atom_cotangent, aslope, gath, w_atom)
    enew, gmer, gwc, gro, goa, aout, gatom, gw2 = call(
        out_body, "output_block", steps, 16,
        (merged, radial_basis, trow, anew, edge_cotangent) + outs,
        [rows(wide), rows(rbf), cols(1), whole(anew), rows(wide)] + [whole(w) for w in outs],
        [act, ((edges, wide), WIDE), (w_concat.shape, LOW), (w_rbf_out.shape, LOW),
         ((wide, 2 * aw), LOW), ((atoms, aw), LOW), ((atoms, aw), LOW), ((2 * atoms, wide), LOW)],
        [rows(wide), rows(wide), whole(w_concat), whole(w_rbf_out), fixed(wide, 2 * aw),
         fixed(atoms, aw), fixed(atoms, aw), fixed(2 * atoms, wide)],
        [
            pltpu.VMEM((atoms, wide), WIDE), pltpu.VMEM((atoms, wide), WIDE),
            pltpu.VMEM((2 * atoms, 2 * wide), LOW),
            pltpu.VMEM((w_concat.shape[0] - aw, wide), WIDE), pltpu.VMEM(w_rbf_out.shape, WIDE),
        ],
    )
    first = jnp.concatenate([by_rows(gwc, peers), by_rows(goa, peers), by_rows(gro, peers)], axis=2)
    first = core_sum(first)

    gpart, lb3, lb4, gsk, gr1, gr2, gra, gup, gbil = call(
        back_body, "edge_update_back", steps, 22,
        (edge_embed, radial_basis, trow, s3, s4, merged, gmer, gw2, p3, p4, mixlow, reshid, dsk,
         du3, du4, dr1, dr2) + ups,
        [rows(wide), rows(rbf), cols(1), cols(f3), cols(f4), rows(wide), rows(wide), whole(gw2),
         cols(n3), cols(n4)] + [rows(wide)] * 7 + [whole(w) for w in ups],
        [((edges, wide), WIDE), ((n3, edges), LOW), ((n4, edges), LOW), (w_skip.shape, LOW),
         (w_skip.shape, LOW), (w_skip.shape, LOW), (w_rbf_atom.shape, LOW), ((wide, nb), LOW), ((f3, nb), LOW)],
        [rows(wide), cols(n3), cols(n4), whole(w_skip), whole(w_skip), whole(w_skip),
         whole(w_rbf_atom), fixed(wide, nb), fixed(f3, nb)],
        [pltpu.VMEM(w_skip.shape, WIDE)] * 3
        + [pltpu.VMEM(w_rbf_atom.shape, WIDE), pltpu.VMEM((nb, wide), WIDE), pltpu.VMEM((f3, nb), WIDE)],
    )
    second = jnp.concatenate(
        [by_rows(gsk, peers), by_rows(gr1, peers), by_rows(gr2, peers), by_rows(gra, peers),
         fold(gup, peers), fold(gbil, peers)],
        axis=2,
    )
    lb4, first = lax.optimization_barrier((lb4, first))
    first = group_sum(first)
    second = core_sum(second)

    def scatter(lb, idx, basis, w, beside, name, micros):
        n, slots, q, f = w.shape[1], idx.shape[0], basis.shape[1], w.shape[0]
        ins = (lb, idx, basis, w) + ((beside,) if beside is not None else ())
        far = (n, ghosts_up) if beside is None else (ghosts, LANES)
        far_type = WIDE if beside is None else LOW
        body = functools.partial(scatter_body, edges=edges, other=beside is not None)
        return call(
            body, name, steps, micros, ins,
            [cols(n), cols(slots), rows(q), whole(w)] + [whole(x) for x in ins[4:]],
            [((n, edges), WIDE), (far, far_type)],
            [fixed(n, edges), fixed(*far)],
            [
                pltpu.VMEM((slabs * n, TILE), WIDE), pltpu.VMEM((q, TILE), WIDE), pltpu.VMEM((f, TILE), WIDE),
                pltpu.VMEM((slabs * n, slots * TILE), LOW), pltpu.VMEM((TILE, slots * TILE), LOW),
            ],
        )

    grad4, far4 = scatter(lb4, i4, quadruplet_basis, w_bilinear_quad, None, "scatter_quad", 11)
    lb3, far4, first, second = lax.optimization_barrier((lb3, far4, first, second))
    first = share_sum(first)
    second = group_sum(second)
    grad3, far = scatter(lb3, i3, triplet_basis, triplet_bilinear_weight, far4, "scatter_trip", 20)
    ret = exchange(far, peers)
    ret, first, second = lax.optimization_barrier((ret, first, second))
    first = group_gather(first)
    second = share_sum(second)

    gedge, gs3, gs4, gr3, gr4, gdn = call(
        source_back_body, "source_rows_back", steps, 19,
        (edge_embed, radial_basis, gpart, grad3, grad4, down, ret, asked) + sources,
        [rows(wide), rows(rbf), rows(wide), cols(n3), cols(n4), cols(nb), whole(ret), whole(asked)]
        + [whole(w) for w in sources],
        [act, (w_skip.shape, LOW), (w_skip.shape, LOW), (w_rbf_trip.shape, LOW),
         (w_rbf_trip.shape, LOW), ((wide, nb), LOW)],
        [rows(wide), whole(w_skip), whole(w_skip), whole(w_rbf_trip), whole(w_rbf_trip), fixed(wide, nb)],
        [pltpu.VMEM(w_skip.shape, WIDE)] * 2
        + [pltpu.VMEM(w_rbf_trip.shape, WIDE)] * 2
        + [pltpu.VMEM((nb, wide), WIDE)] + turned + [pltpu.VMEM((LANES, ghosts), LOW)],
    )
    third = jnp.concatenate(
        [by_rows(gs3, peers), by_rows(gs4, peers), by_rows(gr3, peers), by_rows(gr4, peers), fold(gdn, peers)],
        axis=2,
    )
    third, first, second = lax.optimization_barrier((third, first, second))
    third = core_sum(third)
    second = group_gather(second)
    third = group_gather(share_sum(group_sum(third)))

    a = wide // peers
    b = rbf // peers
    c = w_concat.shape[0] // peers
    r_concat = wide_rows(first, 0, c)
    r_oa = wide_rows(first, c, c + a)
    r_out = wide_rows(first, c + a, c + a + b)
    r_sk = wide_rows(second, 0, a)
    r_r1 = wide_rows(second, a, 2 * a)
    r_r2 = wide_rows(second, 2 * a, 3 * a)
    at = 3 * a + b
    r_ra = wide_rows(second, 3 * a, at)
    r_up = unfold(second, at, at + a // 4, nb).T
    r_bil = unfold(second, at + a // 4, second.shape[1], nb)
    r_s3 = wide_rows(third, 0, a)
    r_s4 = wide_rows(third, a, 2 * a)
    r_r3 = wide_rows(third, 2 * a, 2 * a + b)
    r_r4 = wide_rows(third, 2 * a + b, 2 * a + 2 * b)
    r_dn = unfold(third, 2 * a + 2 * b, third.shape[1], nb)
    return (
        enew, anew, aout, gedge, gatom,
        r_s3, r_r3, r_dn[:, 0:n3], r_s4, r_r4, r_dn[:, n3:],
        r_bil[:, 0:n3], r_up[0:n3], r_bil[:, n3:], r_up[n3:],
        r_sk, r_r1, r_r2, r_ra, r_oa[:, aw:], r_concat, r_out, r_oa[:, 0:aw],
    )


def solution(mesh):
    both = P(("grp", "edge"), None)
    placed = (both,) * 10 + (P(("grp", "edge"), None, None),) + (P(),) * 18 + (both,) * 3
    shares = [P("edge", None)] * 18
    shares[7] = P(None, "edge")
    shares[9] = P(None, "edge")
    return jax.shard_map(
        per_device, mesh=mesh, in_specs=placed, out_specs=(both,) * 5 + tuple(shares), check_vma=False
    )
```

```python
import functools
import math

import jax
import jax.numpy as jnp
from jax import lax
from jax.experimental import pallas as pl
from jax.experimental.pallas import tpu as pltpu
from jax.sharding import PartitionSpec as P

HALF_ROOT = 1.0 / math.sqrt(2.0)
THIRD_ROOT = 1.0 / math.sqrt(3.0)
LOW = jnp.bfloat16
WIDE = jnp.float32
TILE = 256
LANES = 128
GROUP = 4
VMEM_BYTES = 60 * 1024 * 1024


def sigma(v):
    return 0.5 * jnp.tanh(0.5 * v) + 0.5


def slope_of(v, s):
    return s * (1.0 + v * (1.0 - s))


def nn(a, b):
    return jnp.dot(a, b, preferred_element_type=WIDE)


def nt(a, b):
    return lax.dot_general(a, b, (((1,), (1,)), ((), ())), preferred_element_type=WIDE)


def tn(a, b):
    return lax.dot_general(a, b, (((0,), (0,)), ((), ())), preferred_element_type=WIDE)


def split_pair(v):
    high = v.astype(LOW)
    rest = (v - high.astype(WIDE)).astype(LOW)
    return jnp.concatenate([high, rest], axis=0)


def whole(array):
    rank = len(array.shape)
    return pl.BlockSpec(array.shape, lambda i: (0,) * rank)


def rows(width):
    return pl.BlockSpec((TILE, width), lambda i: (i, 0))


def cols(height):
    return pl.BlockSpec((height, TILE), lambda i: (0, i))


def fixed(*shape):
    return pl.BlockSpec(shape, lambda i: (0,) * len(shape))


def call(body, name, steps, micros, ins, in_specs, outs, out_specs, scratch):
    return pl.pallas_call(
        body,
        name=name,
        out_shape=[jax.ShapeDtypeStruct(s, t) for s, t in outs],
        grid_spec=pltpu.PrefetchScalarGridSpec(
            num_scalar_prefetch=0,
            grid=(steps,),
            in_specs=in_specs,
            out_specs=out_specs,
            scratch_shapes=scratch,
        ),
        compiler_params=pltpu.CompilerParams(
            dimension_semantics=("arbitrary",), vmem_limit_bytes=VMEM_BYTES
        ),
        cost_estimate=pl.CostEstimate(
            flops=int(micros * 1.1e9), transcendentals=0, bytes_accessed=1 << 22
        ),
    )(*ins)


def source_body(
    edge, radial, asked, ws3, wr3, wd3, ws4, wr4, wd4, table, down, sent, t3, t4, acc
):
    step = pl.program_id(0)
    ghosts = asked.shape[1]

    @pl.when(step == 0)
    def _():
        t3[...] = wd3[...].astype(WIDE).T.astype(LOW)
        t4[...] = wd4[...].astype(WIDE).T.astype(LOW)
        acc[...] = jnp.zeros_like(acc)

    e = edge[...]
    r = radial[...]
    pre3 = nn(e, ws3[...])
    mix3 = (pre3 * sigma(pre3) * nn(r, wr3[...])).astype(LOW)
    down3 = nt(t3[...], mix3)
    pre4 = nn(e, ws4[...])
    mix4 = (pre4 * sigma(pre4) * nn(r, wr4[...])).astype(LOW)
    down4 = nt(t4[...], mix4)
    both = jnp.concatenate([down3, down4], axis=0)
    down[...] = both
    found = (both * sigma(both)).astype(LOW)
    table[...] = found
    place = lax.broadcasted_iota(jnp.int32, (TILE, ghosts), 0) + step * TILE
    acc[0 : found.shape[0], :] += nn(found, (place == asked[...]).astype(LOW))

    @pl.when(step == pl.num_programs(0) - 1)
    def _():
        sent[...] = acc[...].T.astype(LOW)


def fill_slabs(tab, ghost, t3, t4, n3, n4):
    local = tab.shape[1] // TILE
    for s in range(local):
        t3[s * n3 : (s + 1) * n3, :] = tab[0:n3, s * TILE : (s + 1) * TILE]
        t4[s * n4 : (s + 1) * n4, :] = tab[n3 : n3 + n4, s * TILE : (s + 1) * TILE]
    for g in range(0, ghost.shape[0], TILE):
        s = local + g // TILE
        size = min(TILE, ghost.shape[0] - g)
        part = ghost[g : g + size, :].astype(WIDE).T
        if size < TILE:
            part = jnp.concatenate([part, jnp.zeros((LANES, TILE - size), WIDE)], axis=1)
        t3[s * n3 : (s + 1) * n3, :] = part[0:n3, :].astype(LOW)
        t4[s * n4 : (s + 1) * n4, :] = part[n3 : n3 + n4, :].astype(LOW)


def hot_of(low_part):
    place = lax.broadcasted_iota(jnp.int32, (TILE, TILE), 0).astype(WIDE).astype(LOW)
    return jnp.where(place == low_part, jnp.ones((), LOW), jnp.zeros((), LOW))


def pick(tab, index_row, width):
    slabs = tab.shape[0] // width
    low_part = (index_row & (TILE - 1)).astype(WIDE).astype(LOW)
    slab = jnp.broadcast_to((index_row >> 8).astype(WIDE), (width, TILE)).astype(LOW)
    found = nn(tab[...], hot_of(low_part)).astype(LOW)
    got = jnp.zeros((width, TILE), LOW)
    for s in range(slabs):
        got = jnp.where(slab == s, found[s * width : (s + 1) * width, :], got)
    return got


def weigh(coef, picked, out, group, basis, width):
    for cb in range(basis // 4):
        acc = [None] * 4
        for k in range(group * GROUP, (group + 1) * GROUP):
            g = picked[k]
            for j in range(4):
                row = k * basis + cb * 4 + j
                term = jnp.broadcast_to(coef[row : row + 1, :], g.shape).astype(LOW) * g
                acc[j] = term if acc[j] is None else acc[j] + term
        for j in range(4):
            at = (cb * 4 + j) * width
            before = out[at : at + width, :] + acc[j] if group else acc[j]
            out[at : at + width, :] = before


def gather_body(
    tab, ghost, i3, i4, b3, b4, w3, w4, s3, s4, p3, p4, t3, t4, g3, g4, c3, c4, w3t, w4t
):
    n3, n4 = w3t.shape[0], w4t.shape[0]
    k3, k4 = i3.shape[0], i4.shape[0]

    @pl.when(pl.program_id(0) == 0)
    def _():
        w3t[...] = w3[...].astype(WIDE).T.astype(LOW)
        w4t[...] = w4[...].astype(WIDE).T.astype(LOW)
        fill_slabs(tab, ghost, t3, t4, n3, n4)

    c3[...] = b3[...].astype(WIDE).T
    c4[...] = b4[...].astype(WIDE).T

    work = [(t3, i3, g3, c3, s3, n3, k3, j) for j in range(k3 // GROUP)]
    work += [(t4, i4, g4, c4, s4, n4, k4, j) for j in range(k4 // GROUP)]
    for at in range(len(work) + 1):
        if at < len(work):
            t, i, g, _, _, n, _, j = work[at]
            for k in range(j * GROUP, (j + 1) * GROUP):
                g[k] = pick(t, i[k : k + 1, :], n)
        if at:
            _, _, g, c, out, n, count, j = work[at - 1]
            weigh(c, g, out, j, c.shape[0] // count, n)
    p3[...] = nn(w3t[...], s3[...])
    p4[...] = nn(w4t[...], s4[...])


def mix_body(
    edge, radial, p3, p4, trow, wu3, wu4, wsk, wr1, wr2, wra, wat, atom,
    merged, mixlow, reshid, dsk, du3, du4, dr1, dr2, gath, anew, aslope, acc,
):
    step = pl.program_id(0)
    atoms = acc.shape[0]
    v3 = p3[...]
    v4 = p4[...]
    h3 = (v3 * sigma(v3)).T.astype(LOW)
    h4 = (v4 * sigma(v4)).T.astype(LOW)
    up3 = nn(h3, wu3[...])
    s = sigma(up3)
    du3[...] = slope_of(up3, s).astype(LOW)
    total = up3 * s
    up4 = nn(h4, wu4[...])
    s = sigma(up4)
    du4[...] = slope_of(up4, s).astype(LOW)
    total = total + up4 * s
    skip = nn(edge[...], wsk[...])
    s = sigma(skip)
    dsk[...] = slope_of(skip, s).astype(LOW)
    mixed = (total + skip * s) * THIRD_ROOT
    low_mixed = mixed.astype(LOW)
    mixlow[...] = low_mixed
    res = nn(low_mixed, wr1[...])
    s = sigma(res)
    dr1[...] = slope_of(res, s).astype(LOW)
    hid = (res * s).astype(LOW)
    reshid[...] = hid
    res2 = nn(hid, wr2[...])
    s = sigma(res2)
    dr2[...] = (0.5 * slope_of(res2, s)).astype(LOW)
    out = (edge[...].astype(WIDE) + (mixed + res2 * s) * HALF_ROOT) * HALF_ROOT
    merged[...] = out
    weighted = (out * nn(radial[...], wra[...])).astype(LOW)
    hot_t = (lax.broadcasted_iota(jnp.int32, (atoms, TILE), 0) == trow[...]).astype(LOW)
    part = nn(hot_t, weighted)

    @pl.when(step == 0)
    def _():
        acc[...] = part

    @pl.when(step > 0)
    def _():
        acc[...] += part

    @pl.when(step == pl.num_programs(0) - 1)
    def _():
        g = acc[...].astype(LOW)
        gath[...] = g
        pre = nn(g, wat[...])
        sa = sigma(pre)
        aslope[...] = HALF_ROOT * slope_of(pre, sa)
        anew[...] = ((atom[...].astype(WIDE) + pre * sa) * HALF_ROOT).astype(LOW)


def out_body(
    merged, radial, trow, anew, cot, wc, wro, wout, ocot, acot, aslope, gath, wat,
    enew, gmer, gwc, gro, goa, aout, gatom, gw2, ogat, seg, both, awc, aro,
):
    step = pl.program_id(0)
    atoms, wide = ogat.shape
    aw = anew.shape[1]

    @pl.when(step == 0)
    def _():
        both[:, 0:wide] = split_pair(nt(ocot[...], wout[...]))
        both[:, wide : 2 * wide] = split_pair(nn(anew[...], wc[0:aw, :]))
        ogat[...] = jnp.zeros_like(ogat)
        seg[...] = jnp.zeros_like(seg)
        awc[...] = jnp.zeros_like(awc)
        aro[...] = jnp.zeros_like(aro)

    hot_t = (lax.broadcasted_iota(jnp.int32, (atoms, TILE), 0) == trow[...]).astype(LOW)
    spread = tn(jnp.concatenate([hot_t, hot_t], axis=0), both[...])
    gow = spread[:, 0:wide]
    m = merged[...]
    ml = m.astype(LOW)
    wcm = wc[aw:, :]
    pre = spread[:, wide:] + nn(ml, wcm)
    s = sigma(pre)
    new = (m + pre * s) * HALF_ROOT
    enew[...] = new.astype(LOW)
    rout = nn(radial[...], wro[...])
    ogat[...] += nn(hot_t, (new * rout).astype(LOW))
    gnew = cot[...].astype(WIDE) + gow * rout
    aro[...] += tn(radial[...], (gow * new).astype(LOW))
    lc = (gnew * (HALF_ROOT * slope_of(pre, s))).astype(LOW)
    awc[...] += tn(ml, lc)
    seg[...] += nn(hot_t, lc)
    gmer[...] = gnew * HALF_ROOT + nt(lc, wcm)

    @pl.when(step == pl.num_programs(0) - 1)
    def _():
        ol = ogat[...].astype(LOW)
        aout[...] = nn(ol, wout[...]).astype(LOW)
        goa[:, 0:aw] = tn(ol, ocot[...]).astype(LOW)
        gwc[aw:, :] = awc[...].astype(LOW)
        gro[...] = aro[...].astype(LOW)
        pair = split_pair(seg[...])
        hi = pair[0:atoms, :]
        lo = pair[atoms:, :]
        gwc[0:aw, :] = (tn(anew[...], hi) + tn(anew[...], lo)).astype(LOW)
        wca = wc[0:aw, :]
        ga = acot[...].astype(WIDE) + nt(hi, wca) + nt(lo, wca)
        gatom[...] = (ga * HALF_ROOT).astype(LOW)
        la = (ga * aslope[...]).astype(LOW)
        goa[:, aw : 2 * aw] = tn(gath[...], la).astype(LOW)
        gw2[...] = split_pair(nt(la, wat[...]))


def back_body(
    edge, radial, trow, s3, s4, merged, gmer, gw2, p3, p4, mixlow, reshid, dsk, du3, du4, dr1, dr2,
    wu3, wu4, wsk, wr1, wr2, wra,
    gpart, lb3, lb4, gsk, gr1, gr2, gra, gup, gbil, ask, ar1, ar2, ara, aup, abil,
):
    step = pl.program_id(0)
    pair = gw2.shape[0]
    n3 = wu3.shape[0]

    @pl.when(step == 0)
    def _():
        ask[...] = jnp.zeros_like(ask)
        ar1[...] = jnp.zeros_like(ar1)
        ar2[...] = jnp.zeros_like(ar2)
        ara[...] = jnp.zeros_like(ara)
        aup[...] = jnp.zeros_like(aup)
        abil[...] = jnp.zeros_like(abil)

    hot_t = (lax.broadcasted_iota(jnp.int32, (pair // 2, TILE), 0) == trow[...]).astype(LOW)
    gw = tn(jnp.concatenate([hot_t, hot_t], axis=0), gw2[...])
    gm = gmer[...] + gw * nn(radial[...], wra[...])
    ara[...] += tn(radial[...], (gw * merged[...]).astype(LOW))
    l2 = (gm * dr2[...].astype(WIDE)).astype(LOW)
    ar2[...] += tn(reshid[...], l2)
    l1 = (nt(l2, wr2[...]) * dr1[...].astype(WIDE)).astype(LOW)
    ar1[...] += tn(mixlow[...], l1)
    gmix = (gm * 0.5 + nt(l1, wr1[...])) * THIRD_ROOT
    ls = (gmix * dsk[...].astype(WIDE)).astype(LOW)
    l3 = (gmix * du3[...].astype(WIDE)).astype(LOW)
    l4 = (gmix * du4[...].astype(WIDE)).astype(LOW)
    ask[...] += tn(edge[...], ls)
    gpart[...] = gm * HALF_ROOT + nt(ls, wsk[...])
    v3 = p3[...]
    g3 = sigma(v3)
    v4 = p4[...]
    g4 = sigma(v4)
    aup[0:n3, :] += nn((v3 * g3).astype(LOW), l3)
    aup[n3:, :] += nn((v4 * g4).astype(LOW), l4)
    low3 = (nt(wu3[...], l3) * slope_of(v3, g3)).astype(LOW)
    low4 = (nt(wu4[...], l4) * slope_of(v4, g4)).astype(LOW)
    lb3[...] = low3
    lb4[...] = low4
    abil[:, 0:n3] += nt(s3[...], low3)
    abil[:, n3:] += nt(s4[...], low4)

    @pl.when(step == pl.num_programs(0) - 1)
    def _():
        gsk[...] = ask[...].astype(LOW)
        gr1[...] = ar1[...].astype(LOW)
        gr2[...] = ar2[...].astype(LOW)
        gra[...] = ara[...].astype(LOW)
        gup[...] = aup[...].T.astype(LOW)
        gbil[...] = abil[...].astype(LOW)


def unweigh(coef, dsum, index, spread, hots, group, basis, width):
    slabs = spread.shape[0] // width
    for k in range(group * GROUP, (group + 1) * GROUP):
        low_part = (index[k : k + 1, :] & (TILE - 1)).astype(WIDE).astype(LOW)
        hots[:, k * TILE : (k + 1) * TILE] = hot_of(low_part)
    acc = [None] * GROUP
    for c in range(basis):
        d = dsum[c * width : (c + 1) * width, :]
        for j in range(GROUP):
            row = (group * GROUP + j) * basis + c
            term = jnp.broadcast_to(coef[row : row + 1, :], d.shape).astype(LOW) * d
            acc[j] = term if acc[j] is None else acc[j] + term
    for j in range(GROUP):
        k = group * GROUP + j
        slab = jnp.broadcast_to((index[k : k + 1, :] >> 8).astype(WIDE), (width, TILE)).astype(LOW)
        for s in range(slabs):
            spread[s * width : (s + 1) * width, k * TILE : (k + 1) * TILE] = jnp.where(
                slab == s, acc[j], jnp.zeros((), LOW)
            )


def scatter_body(lb, idx, basis, w, *rest, edges, other):
    if other:
        beside, grad, far, acc, coef, dsum, spread, hots = rest
    else:
        grad, far, acc, coef, dsum, spread, hots = rest
    step = pl.program_id(0)
    n = w.shape[1]
    slots = idx.shape[0]

    @pl.when(step == 0)
    def _():
        acc[...] = jnp.zeros_like(acc)

    coef[...] = basis[...].astype(WIDE).T
    dsum[...] = nn(w[...], lb[...]).astype(LOW)
    for group in range(slots // GROUP):
        part = slice(group * GROUP * TILE, (group + 1) * GROUP * TILE)
        unweigh(coef, dsum, idx, spread, hots, group, coef.shape[0] // slots, n)
        acc[...] += nt(spread[:, part], hots[:, part])

    @pl.when(step == pl.num_programs(0) - 1)
    def _():
        local = edges // TILE
        for s in range(local):
            grad[:, s * TILE : (s + 1) * TILE] = acc[s * n : (s + 1) * n, :]
        for s in range(local, acc.shape[0] // n):
            part = acc[s * n : (s + 1) * n, :]
            if other:
                more = beside[:, (s - local) * TILE : (s - local + 1) * TILE]
                filler = jnp.zeros((LANES - n - more.shape[0], TILE), WIDE)
                part = jnp.concatenate([part, more, filler], axis=0).T.astype(LOW)
                size = min(TILE, far.shape[0] - (s - local) * TILE)
                far[(s - local) * TILE : (s - local) * TILE + size, :] = part[0:size, :]
            else:
                far[:, (s - local) * TILE : (s - local + 1) * TILE] = part


def source_back_body(
    edge, radial, gpart, grad3, grad4, down, ret, asked, ws3, wr3, wd3, ws4, wr4, wd4,
    gedge, gs3, gs4, gr3, gr4, gdn, as3, as4, ar3, ar4, adn, t3, t4, rt,
):
    step = pl.program_id(0)
    n3, n4 = grad3.shape[0], grad4.shape[0]

    @pl.when(step == 0)
    def _():
        t3[...] = wd3[...].astype(WIDE).T.astype(LOW)
        t4[...] = wd4[...].astype(WIDE).T.astype(LOW)
        rt[...] = ret[...].astype(WIDE).T.astype(LOW)
        as3[...] = jnp.zeros_like(as3)
        as4[...] = jnp.zeros_like(as4)
        ar3[...] = jnp.zeros_like(ar3)
        ar4[...] = jnp.zeros_like(ar4)
        adn[...] = jnp.zeros_like(adn)

    place = lax.broadcasted_iota(jnp.int32, (TILE, asked.shape[1]), 0) + step * TILE
    back = nt(rt[...], (place == asked[...]).astype(LOW))
    v = down[...]
    ld = jnp.concatenate([grad3[...], grad4[...]], axis=0) + back[0 : n3 + n4, :]
    ld = ld * slope_of(v, sigma(v))
    ldt = ld.astype(LOW)
    low_rows = ld.T.astype(LOW)
    e = edge[...]
    r = radial[...]
    pre = nn(e, ws3[...])
    rad = nn(r, wr3[...])
    s = sigma(pre)
    act = pre * s
    adn[0:n3, :] += nn(ldt[0:n3, :], (act * rad).astype(LOW))
    gm = nn(low_rows[:, 0:n3], t3[...])
    l3 = (gm * rad * slope_of(pre, s)).astype(LOW)
    ar3[...] += tn(r, (gm * act).astype(LOW))
    as3[...] += tn(e, l3)
    pre = nn(e, ws4[...])
    rad = nn(r, wr4[...])
    s = sigma(pre)
    act = pre * s
    adn[n3:, :] += nn(ldt[n3:, :], (act * rad).astype(LOW))
    gm = nn(low_rows[:, n3:], t4[...])
    l4 = (gm * rad * slope_of(pre, s)).astype(LOW)
    ar4[...] += tn(r, (gm * act).astype(LOW))
    as4[...] += tn(e, l4)
    gedge[...] = (gpart[...] + nt(l3, ws3[...]) + nt(l4, ws4[...])).astype(LOW)

    @pl.when(step == pl.num_programs(0) - 1)
    def _():
        gs3[...] = as3[...].astype(LOW)
        gs4[...] = as4[...].astype(LOW)
        gr3[...] = ar3[...].astype(LOW)
        gr4[...] = ar4[...].astype(LOW)
        gdn[...] = adn[...].T.astype(LOW)


def swap(v, axis, mask):
    count = lax.axis_size(axis)
    return lax.ppermute(v, axis, [(j, j ^ mask) for j in range(count)])


def groups_of(axis, first):
    top = lax.axis_size(axis).bit_length() - 1
    return [(at, min(2, top - at)) for at in range(first, top, 2)]


def scatter_step(v, axis, at, width):
    parts = 1 << width
    own = (lax.axis_index(axis) >> at) & (parts - 1)
    v = v.reshape(v.shape[0] // parts, parts, *v.shape[1:])
    total = lax.dynamic_index_in_dim(v, own, 1, keepdims=False).astype(WIDE)
    for m in range(1, parts):
        sent = lax.dynamic_index_in_dim(v, own ^ m, 1, keepdims=False)
        total = total + swap(sent, axis, m << at).astype(WIDE)
    return total.astype(LOW)


def core_sum(v):
    return scatter_step(v, "edge", 0, 1)


def group_sum(v):
    own = lax.axis_index("grp")
    total = lax.dynamic_index_in_dim(v, own, 1, keepdims=False).astype(WIDE)
    for m in range(1, v.shape[1]):
        sent = lax.dynamic_index_in_dim(v, own ^ m, 1, keepdims=False)
        total = total + swap(sent, "grp", m).astype(WIDE)
    return total.astype(LOW)


def share_sum(v):
    for at, width in groups_of("edge", 1):
        v = scatter_step(v, "edge", at, width)
    return v[0]


def group_gather(v):
    own = lax.axis_index("grp")
    count = lax.axis_size("grp")
    out = jnp.zeros((count,) + v.shape, LOW)
    out = lax.dynamic_update_index_in_dim(out, v, own, 0)
    for m in range(1, count):
        out = lax.dynamic_update_index_in_dim(out, swap(v, "grp", m), own ^ m, 0)
    return out.astype(WIDE)


def exchange(v, peers):
    parts = v.reshape(peers, v.shape[0] // peers, v.shape[1])
    return lax.all_to_all(parts, "edge", split_axis=0, concat_axis=0, tiled=True).reshape(v.shape)


def by_rows(g, count):
    parts = g.reshape(count, g.shape[0] // count, g.shape[1])
    return jnp.stack([parts[:, :, q : q + 128] for q in range(0, g.shape[1], 128)], axis=1)


def fold(g, count):
    parts = g.reshape(count, 4, g.shape[0] // count // 4, g.shape[1])
    return jnp.pad(parts, ((0, 0), (0, 0), (0, 0), (0, 128 - g.shape[1])))


def wide_rows(g, start, stop):
    return jnp.concatenate([g[q, start:stop] for q in range(g.shape[0])], axis=1)


def unfold(g, start, stop, width):
    return g[:, start:stop, 0:width].reshape(g.shape[0] * (stop - start), width)


def per_device(
    edge_embed, atom_embed, radial_basis, triplet_basis, quadruplet_basis,
    triplet_source_row, triplet_mask, quadruplet_source_row, quadruplet_mask,
    edge_target_atom, borrowed_edges,
    w_source_trip, w_rbf_trip, w_down_trip, w_source_quad, w_rbf_quad, w_down_quad,
    triplet_bilinear_weight, w_up_trip, w_bilinear_quad, w_up_quad, w_skip,
    w_res_first, w_res_second, w_rbf_atom, w_atom, w_concat, w_rbf_out, w_out,
    edge_cotangent, atom_cotangent, output_cotangent,
):
    edges, wide = edge_embed.shape
    atoms, aw = atom_embed.shape
    rbf = radial_basis.shape[1]
    peers = lax.axis_size("edge")
    cap = borrowed_edges.shape[2]
    steps = edges // TILE
    n3, n4 = w_down_trip.shape[1], w_down_quad.shape[1]
    nb = n3 + n4
    k3, k4 = triplet_mask.shape[1], quadruplet_mask.shape[1]
    f3, f4 = triplet_bilinear_weight.shape[0], w_bilinear_quad.shape[0]
    q3, q4 = triplet_basis.shape[1], quadruplet_basis.shape[1]
    ghosts = peers * cap
    ghosts_up = -(-ghosts // TILE) * TILE
    slabs = (edges + ghosts_up) // TILE

    wanted = borrowed_edges[0] - (jnp.arange(peers, dtype=jnp.int32) * edges)[:, None]
    asked = lax.all_to_all(wanted, "edge", split_axis=0, concat_axis=0, tiled=True).reshape(1, ghosts)

    i3 = jnp.where(triplet_mask > 0, triplet_source_row, -1).T
    i4 = jnp.where(quadruplet_mask > 0, quadruplet_source_row, -1).T
    trow = edge_target_atom
    sources = (w_source_trip, w_rbf_trip, w_down_trip, w_source_quad, w_rbf_quad, w_down_quad)
    turned = [pltpu.VMEM((n3, wide), LOW), pltpu.VMEM((n4, wide), LOW)]

    table, down, sent = call(
        source_body, "source_rows", steps, 10, (edge_embed, radial_basis, asked) + sources,
        [rows(wide), rows(rbf), whole(asked)] + [whole(w) for w in sources],
        [((nb, edges), LOW), ((nb, edges), WIDE), ((ghosts, LANES), LOW)],
        [cols(nb), cols(nb), fixed(ghosts, LANES)],
        turned + [pltpu.VMEM((LANES, ghosts), WIDE)],
    )
    ghost = exchange(sent, peers)

    s3, s4, p3, p4 = call(
        gather_body, "gather_sums", steps, 38,
        (table, ghost, i3, i4, triplet_basis, quadruplet_basis, triplet_bilinear_weight, w_bilinear_quad),
        [whole(table), whole(ghost), cols(k3), cols(k4), rows(q3), rows(q4),
         whole(triplet_bilinear_weight), whole(w_bilinear_quad)],
        [((f3, edges), LOW), ((f4, edges), LOW), ((n3, edges), WIDE), ((n4, edges), WIDE)],
        [cols(f3), cols(f4), cols(n3), cols(n4)],
        [
            pltpu.VMEM((slabs * n3, TILE), LOW), pltpu.VMEM((slabs * n4, TILE), LOW),
            pltpu.VMEM((k3, n3, TILE), LOW), pltpu.VMEM((k4, n4, TILE), LOW),
            pltpu.VMEM((q3, TILE), WIDE), pltpu.VMEM((q4, TILE), WIDE),
            pltpu.VMEM((n3, f3), LOW), pltpu.VMEM((n4, f4), LOW),
        ],
    )

    act = ((edges, wide), LOW)
    ups = (w_up_trip, w_up_quad, w_skip, w_res_first, w_res_second, w_rbf_atom)
    merged, mixlow, reshid, dsk, du3, du4, dr1, dr2, gath, anew, aslope = call(
        mix_body, "edge_update", steps, 19,
        (edge_embed, radial_basis, p3, p4, trow) + ups + (w_atom, atom_embed),
        [rows(wide), rows(rbf), cols(n3), cols(n4), cols(1)] + [whole(w) for w in ups + (w_atom, atom_embed)],
        [((edges, wide), WIDE), act, act, act, act, act, act, act,
         ((atoms, wide), LOW), ((atoms, aw), LOW), ((atoms, aw), WIDE)],
        [rows(wide)] * 8 + [fixed(atoms, wide), fixed(atoms, aw), fixed(atoms, aw)],
        [pltpu.VMEM((atoms, wide), WIDE)],
    )

    outs = (w_concat, w_rbf_out, w_out, output_cotangent, atom_cotangent, aslope, gath, w_atom)
    enew, gmer, gwc, gro, goa, aout, gatom, gw2 = call(
        out_body, "output_block", steps, 16,
        (merged, radial_basis, trow, anew, edge_cotangent) + outs,
        [rows(wide), rows(rbf), cols(1), whole(anew), rows(wide)] + [whole(w) for w in outs],
        [act, ((edges, wide), WIDE), (w_concat.shape, LOW), (w_rbf_out.shape, LOW),
         ((wide, 2 * aw), LOW), ((atoms, aw), LOW), ((atoms, aw), LOW), ((2 * atoms, wide), LOW)],
        [rows(wide), rows(wide), whole(w_concat), whole(w_rbf_out), fixed(wide, 2 * aw),
         fixed(atoms, aw), fixed(atoms, aw), fixed(2 * atoms, wide)],
        [
            pltpu.VMEM((atoms, wide), WIDE), pltpu.VMEM((atoms, wide), WIDE),
            pltpu.VMEM((2 * atoms, 2 * wide), LOW),
            pltpu.VMEM((w_concat.shape[0] - aw, wide), WIDE), pltpu.VMEM(w_rbf_out.shape, WIDE),
        ],
    )
    first = jnp.concatenate([by_rows(gwc, peers), by_rows(goa, peers), by_rows(gro, peers)], axis=2)
    first = core_sum(first)

    gpart, lb3, lb4, gsk, gr1, gr2, gra, gup, gbil = call(
        back_body, "edge_update_back", steps, 22,
        (edge_embed, radial_basis, trow, s3, s4, merged, gmer, gw2, p3, p4, mixlow, reshid, dsk,
         du3, du4, dr1, dr2) + ups,
        [rows(wide), rows(rbf), cols(1), cols(f3), cols(f4), rows(wide), rows(wide), whole(gw2),
         cols(n3), cols(n4)] + [rows(wide)] * 7 + [whole(w) for w in ups],
        [((edges, wide), WIDE), ((n3, edges), LOW), ((n4, edges), LOW), (w_skip.shape, LOW),
         (w_skip.shape, LOW), (w_skip.shape, LOW), (w_rbf_atom.shape, LOW), ((wide, nb), LOW), ((f3, nb), LOW)],
        [rows(wide), cols(n3), cols(n4), whole(w_skip), whole(w_skip), whole(w_skip),
         whole(w_rbf_atom), fixed(wide, nb), fixed(f3, nb)],
        [pltpu.VMEM(w_skip.shape, WIDE)] * 3
        + [pltpu.VMEM(w_rbf_atom.shape, WIDE), pltpu.VMEM((nb, wide), WIDE), pltpu.VMEM((f3, nb), WIDE)],
    )
    second = jnp.concatenate(
        [by_rows(gsk, peers), by_rows(gr1, peers), by_rows(gr2, peers), by_rows(gra, peers),
         fold(gup, peers), fold(gbil, peers)],
        axis=2,
    )
    lb4, first = lax.optimization_barrier((lb4, first))
    first = group_sum(first)
    second = core_sum(second)

    def scatter(lb, idx, basis, w, beside, name, micros):
        n, slots, q, f = w.shape[1], idx.shape[0], basis.shape[1], w.shape[0]
        ins = (lb, idx, basis, w) + ((beside,) if beside is not None else ())
        far = (n, ghosts_up) if beside is None else (ghosts, LANES)
        far_type = WIDE if beside is None else LOW
        body = functools.partial(scatter_body, edges=edges, other=beside is not None)
        return call(
            body, name, steps, micros, ins,
            [cols(n), cols(slots), rows(q), whole(w)] + [whole(x) for x in ins[4:]],
            [((n, edges), WIDE), (far, far_type)],
            [fixed(n, edges), fixed(*far)],
            [
                pltpu.VMEM((slabs * n, TILE), WIDE), pltpu.VMEM((q, TILE), WIDE), pltpu.VMEM((f, TILE), LOW),
                pltpu.VMEM((slabs * n, slots * TILE), LOW), pltpu.VMEM((TILE, slots * TILE), LOW),
            ],
        )

    grad4, far4 = scatter(lb4, i4, quadruplet_basis, w_bilinear_quad, None, "scatter_quad", 11)
    lb3, far4, first, second = lax.optimization_barrier((lb3, far4, first, second))
    first = share_sum(first)
    second = group_sum(second)
    grad3, far = scatter(lb3, i3, triplet_basis, triplet_bilinear_weight, far4, "scatter_trip", 20)
    ret = exchange(far, peers)
    ret, first, second = lax.optimization_barrier((ret, first, second))
    first = group_gather(first)
    second = share_sum(second)

    gedge, gs3, gs4, gr3, gr4, gdn = call(
        source_back_body, "source_rows_back", steps, 19,
        (edge_embed, radial_basis, gpart, grad3, grad4, down, ret, asked) + sources,
        [rows(wide), rows(rbf), rows(wide), cols(n3), cols(n4), cols(nb), whole(ret), whole(asked)]
        + [whole(w) for w in sources],
        [act, (w_skip.shape, LOW), (w_skip.shape, LOW), (w_rbf_trip.shape, LOW),
         (w_rbf_trip.shape, LOW), ((wide, nb), LOW)],
        [rows(wide), whole(w_skip), whole(w_skip), whole(w_rbf_trip), whole(w_rbf_trip), fixed(wide, nb)],
        [pltpu.VMEM(w_skip.shape, WIDE)] * 2
        + [pltpu.VMEM(w_rbf_trip.shape, WIDE)] * 2
        + [pltpu.VMEM((nb, wide), WIDE)] + turned + [pltpu.VMEM((LANES, ghosts), LOW)],
    )
    third = jnp.concatenate(
        [by_rows(gs3, peers), by_rows(gs4, peers), by_rows(gr3, peers), by_rows(gr4, peers), fold(gdn, peers)],
        axis=2,
    )
    third, first, second = lax.optimization_barrier((third, first, second))
    third = core_sum(third)
    second = group_gather(second)
    third = group_gather(share_sum(group_sum(third)))

    a = wide // peers
    b = rbf // peers
    c = w_concat.shape[0] // peers
    r_concat = wide_rows(first, 0, c)
    r_oa = wide_rows(first, c, c + a)
    r_out = wide_rows(first, c + a, c + a + b)
    r_sk = wide_rows(second, 0, a)
    r_r1 = wide_rows(second, a, 2 * a)
    r_r2 = wide_rows(second, 2 * a, 3 * a)
    at = 3 * a + b
    r_ra = wide_rows(second, 3 * a, at)
    r_up = unfold(second, at, at + a // 4, nb).T
    r_bil = unfold(second, at + a // 4, second.shape[1], nb)
    r_s3 = wide_rows(third, 0, a)
    r_s4 = wide_rows(third, a, 2 * a)
    r_r3 = wide_rows(third, 2 * a, 2 * a + b)
    r_r4 = wide_rows(third, 2 * a + b, 2 * a + 2 * b)
    r_dn = unfold(third, 2 * a + 2 * b, third.shape[1], nb)
    return (
        enew, anew, aout, gedge, gatom,
        r_s3, r_r3, r_dn[:, 0:n3], r_s4, r_r4, r_dn[:, n3:],
        r_bil[:, 0:n3], r_up[0:n3], r_bil[:, n3:], r_up[n3:],
        r_sk, r_r1, r_r2, r_ra, r_oa[:, aw:], r_concat, r_out, r_oa[:, 0:aw],
    )


def solution(mesh):
    both = P(("grp", "edge"), None)
    placed = (both,) * 10 + (P(("grp", "edge"), None, None),) + (P(),) * 18 + (both,) * 3
    shares = [P("edge", None)] * 18
    shares[7] = P(None, "edge")
    shares[9] = P(None, "edge")
    return jax.shard_map(
        per_device, mesh=mesh, in_specs=placed, out_specs=(both,) * 5 + tuple(shares), check_vma=False
    )
```

```python
import functools
import math

import jax
import jax.numpy as jnp
from jax import lax
from jax.experimental import pallas as pl
from jax.experimental.pallas import tpu as pltpu
from jax.sharding import PartitionSpec as P

HALF_ROOT = 1.0 / math.sqrt(2.0)
THIRD_ROOT = 1.0 / math.sqrt(3.0)
LOW = jnp.bfloat16
WIDE = jnp.float32
TILE = 256
LANES = 128
GROUP = 4
PARTS = 4
VMEM_BYTES = 60 * 1024 * 1024


def sigma(v):
    return 0.5 * jnp.tanh(0.5 * v) + 0.5


def slope_of(v, s):
    return s * (1.0 + v * (1.0 - s))


def nn(a, b):
    return jnp.dot(a, b, preferred_element_type=WIDE)


def nt(a, b):
    return lax.dot_general(a, b, (((1,), (1,)), ((), ())), preferred_element_type=WIDE)


def tn(a, b):
    return lax.dot_general(a, b, (((0,), (0,)), ((), ())), preferred_element_type=WIDE)


def split_pair(v):
    high = v.astype(LOW)
    rest = (v - high.astype(WIDE)).astype(LOW)
    return jnp.concatenate([high, rest], axis=0)


def whole(array):
    rank = len(array.shape)
    return pl.BlockSpec(array.shape, lambda i: (0,) * rank)


def rows(width, tile=TILE):
    return pl.BlockSpec((tile, width), lambda i: (i, 0))


def cols(height):
    return pl.BlockSpec((height, TILE), lambda i: (0, i))


def fixed(*shape):
    return pl.BlockSpec(shape, lambda i: (0,) * len(shape))


def call(body, name, steps, micros, ins, in_specs, outs, out_specs, scratch):
    return pl.pallas_call(
        body,
        name=name,
        out_shape=[jax.ShapeDtypeStruct(s, t) for s, t in outs],
        grid_spec=pltpu.PrefetchScalarGridSpec(
            num_scalar_prefetch=0,
            grid=(steps,),
            in_specs=in_specs,
            out_specs=out_specs,
            scratch_shapes=scratch,
        ),
        compiler_params=pltpu.CompilerParams(
            dimension_semantics=("arbitrary",), vmem_limit_bytes=VMEM_BYTES
        ),
        cost_estimate=pl.CostEstimate(
            flops=int(micros * 1.1e9), transcendentals=0, bytes_accessed=1 << 22
        ),
    )(*ins)


def up16(n):
    return -(-n // 16) * 16


def offsets(parts, peers):
    at, places = 0, []
    for kind, shape in parts:
        places.append(at)
        at += up16(shape[0] // peers if kind == "rows" else shape[0] // PARTS)
    return places, at


def fits(peers, rbf):
    return rbf % (16 * peers) == 0


def grad_outs(parts, peers, inside):
    if inside:
        shapes = [(PARTS, peers // 2, offsets(parts, peers)[1], LANES)] * 2
    else:
        shapes = [shape for _, shape in parts]
    return [(shape, LOW) for shape in shapes], [fixed(*shape) for shape in shapes]


def emit(outs, parts, values, peers, inside, start=0):
    if not inside:
        for out, value in zip(outs, values):
            out[...] = value[...].astype(LOW)
        return
    core = lax.axis_index("edge") & 1
    z = lax.axis_index("edge") >> 1
    grp = lax.axis_index("grp")
    places, _ = offsets(parts, peers)
    for to, side in zip(outs, (1 - core, core)):
        for mz in range(peers // 2):
            for mg in range(PARTS):
                e = ((z ^ mz) << 1) + side
                q = grp ^ mg
                for (kind, shape), place, value in zip(parts, places, values):
                    place += start
                    if kind == "rows":
                        m = shape[0] // peers
                        at = pl.multiple_of(e * m, m)
                        to[mg, mz, place : place + m, :] = value[
                            pl.ds(at, m), pl.ds(pl.multiple_of(q * LANES, LANES), LANES)
                        ].astype(LOW)
                    else:
                        h, w = shape[0] // PARTS, shape[1] // peers
                        at = pl.multiple_of(q * h, 8)
                        if w == LANES:
                            got = value[pl.ds(at, h), pl.ds(pl.multiple_of(e * w, w), w)]
                        else:
                            two = value[pl.ds(at, h), pl.ds(pl.multiple_of((z ^ mz) * LANES, LANES), LANES)]
                            got = jnp.where(side > 0, jnp.concatenate([two[:, w:], two[:, :w]], axis=1), two)
                        if up16(h) > h:
                            got = jnp.concatenate([got, jnp.zeros((up16(h) - h, LANES), WIDE)], axis=0)
                        to[mg, mz, place : place + up16(h), :] = got.astype(LOW)


def pack(parts, grads, peers):
    packed = []
    for (kind, shape), g in zip(parts, grads):
        if kind == "rows":
            g = g.reshape(peers // 2, 2, shape[0] // peers, PARTS, LANES).transpose(1, 3, 0, 2, 4)
        else:
            w = shape[1] // peers
            g = g.reshape(PARTS, shape[0] // PARTS, peers // 2, 2, w).transpose(3, 0, 2, 1, 4)
            g = jnp.pad(g, ((0, 0),) * 4 + ((0, LANES - w),))
        rows_up = up16(g.shape[3])
        packed.append(jnp.pad(g, ((0, 0),) * 3 + ((0, rows_up - g.shape[3]), (0, 0))))
    packed = jnp.concatenate(packed, axis=3)
    place = lax.axis_index("edge")
    own = place & 1
    packed = jnp.take(packed, jnp.arange(PARTS) ^ lax.axis_index("grp"), axis=1)
    packed = jnp.take(packed, jnp.arange(peers // 2) ^ (place >> 1), axis=2)
    return [lax.dynamic_index_in_dim(packed, side, 0, keepdims=False) for side in (1 - own, own)]


def assemble_body(*refs, parts, peers):
    arrived, outs, tmp = refs[:PARTS], refs[PARTS:-1], refs[-1]
    grp = lax.axis_index("grp")
    for (kind, shape), place, out in zip(parts, offsets(parts, peers)[0], outs):
        m = shape[0] // peers
        h, w = shape[0] // PARTS, shape[1] // peers
        for mg in range(PARTS):
            q = grp ^ mg
            if kind == "rows":
                got = arrived[mg][place : place + m, :].astype(WIDE)
                out[:, pl.ds(pl.multiple_of(q * LANES, LANES), LANES)] = got
            else:
                tmp[pl.ds(pl.multiple_of(q * h, 8), h), :] = arrived[mg][place : place + h, :].astype(WIDE)
        if kind == "cols":
            out[...] = tmp[0 : shape[0], 0:w]
        if kind == "turned":
            out[...] = tmp[0 : shape[0], :].T[0:w, :]


def assemble(arrived, parts, peers, name):
    shapes = []
    for kind, (n, w) in parts:
        shapes.append((n // peers, w) if kind == "rows" else (n, w // peers) if kind == "cols" else (w // peers, n))
    return call(
        functools.partial(assemble_body, parts=parts, peers=peers), name, 1, 2, arrived,
        [whole(v) for v in arrived], [(shape, WIDE) for shape in shapes], [fixed(*shape) for shape in shapes],
        [pltpu.VMEM((LANES, LANES), WIDE)],
    )


def source_body(edge, radial, ws3, wr3, wd3, ws4, wr4, wd4, table, down):
    e = edge[...]
    r = radial[...]
    pre3 = nn(e, ws3[...])
    mix3 = (pre3 * sigma(pre3) * nn(r, wr3[...])).astype(LOW)
    down3 = nt(wd3[...], mix3)
    pre4 = nn(e, ws4[...])
    mix4 = (pre4 * sigma(pre4) * nn(r, wr4[...])).astype(LOW)
    down4 = nt(wd4[...], mix4)
    both = jnp.concatenate([down3, down4], axis=0)
    down[...] = both
    table[...] = (both * sigma(both)).astype(LOW)


def sent_body(table, asked, sent, row):
    nb, edges = table.shape
    ghosts = row.shape[1]
    got = jnp.concatenate([asked[p : p + 1, :] for p in range(asked.shape[0])], axis=1) & (edges - 1)
    row[...] = got
    total = jnp.zeros((nb, ghosts), WIDE)
    for s in range(edges // TILE):
        place = lax.broadcasted_iota(jnp.int32, (TILE, ghosts), 0) + s * TILE
        total = total + nn(table[:, s * TILE : (s + 1) * TILE], (place == got).astype(LOW))
    total = jnp.concatenate([total, jnp.zeros((LANES - nb, ghosts), WIDE)], axis=0)
    sent[...] = total.T.astype(LOW)


def fill_slabs(tab, ghost, t3, t4, n3, n4):
    local = tab.shape[1] // TILE
    for s in range(local):
        t3[s * n3 : (s + 1) * n3, :] = tab[0:n3, s * TILE : (s + 1) * TILE]
        t4[s * n4 : (s + 1) * n4, :] = tab[n3 : n3 + n4, s * TILE : (s + 1) * TILE]
    for g in range(0, ghost.shape[0], TILE):
        s = local + g // TILE
        size = min(TILE, ghost.shape[0] - g)
        part = ghost[g : g + size, :].astype(WIDE).T
        if size < TILE:
            part = jnp.concatenate([part, jnp.zeros((LANES, TILE - size), WIDE)], axis=1)
        t3[s * n3 : (s + 1) * n3, :] = part[0:n3, :].astype(LOW)
        t4[s * n4 : (s + 1) * n4, :] = part[n3 : n3 + n4, :].astype(LOW)


def hot_of(low_part):
    place = lax.broadcasted_iota(jnp.int32, (TILE, TILE), 0).astype(WIDE).astype(LOW)
    return jnp.where(place == low_part, jnp.ones((), LOW), jnp.zeros((), LOW))


def pick(tab, index_row, width):
    slabs = tab.shape[0] // width
    low_part = (index_row & (TILE - 1)).astype(WIDE).astype(LOW)
    slab = jnp.broadcast_to((index_row >> 8).astype(WIDE), (width, TILE)).astype(LOW)
    found = nn(tab[...], hot_of(low_part)).astype(LOW)
    got = jnp.zeros((width, TILE), LOW)
    for s in range(slabs):
        got = jnp.where(slab == s, found[s * width : (s + 1) * width, :], got)
    return got


def weigh(coef, picked, out, group, basis, width):
    for cb in range(basis // 4):
        acc = [None] * 4
        for k in range(group * GROUP, (group + 1) * GROUP):
            g = picked[k]
            for j in range(4):
                row = k * basis + cb * 4 + j
                term = jnp.broadcast_to(coef[row : row + 1, :], g.shape).astype(LOW) * g
                acc[j] = term if acc[j] is None else acc[j] + term
        for j in range(4):
            at = (cb * 4 + j) * width
            before = out[at : at + width, :] + acc[j] if group else acc[j]
            out[at : at + width, :] = before


def chosen(index, mask):
    return jnp.where(mask > 0, index, -1)


def gather_body(
    tab, ghost, i3, m3, i4, m4, b3, b4, w3t, w4t, s3, s4, p3, p4, t3, t4, g3, g4, c3, c4
):
    n3, n4 = w3t.shape[0], w4t.shape[0]
    k3, k4 = i3.shape[0], i4.shape[0]

    @pl.when(pl.program_id(0) == 0)
    def _():
        fill_slabs(tab, ghost, t3, t4, n3, n4)

    c3[...] = b3[...].astype(WIDE).T
    c4[...] = b4[...].astype(WIDE).T

    work = [(t3, i3, m3, g3, c3, s3, n3, k3, j) for j in range(k3 // GROUP)]
    work += [(t4, i4, m4, g4, c4, s4, n4, k4, j) for j in range(k4 // GROUP)]
    for at in range(len(work) + 1):
        if at < len(work):
            t, i, m, g, _, _, n, _, j = work[at]
            for k in range(j * GROUP, (j + 1) * GROUP):
                g[k] = pick(t, chosen(i[k : k + 1, :], m[k : k + 1, :]), n)
        if at:
            _, _, _, g, c, out, n, count, j = work[at - 1]
            weigh(c, g, out, j, c.shape[0] // count, n)
    p3[...] = nn(w3t[...], s3[...])
    p4[...] = nn(w4t[...], s4[...])


def mix_body(
    edge, radial, p3, p4, trow, wu3, wu4, wsk, wr1, wr2, wra, wat, atom,
    merged, mixlow, reshid, dsk, du3, du4, dr1, dr2, gath, anew, aslope, acc,
):
    step = pl.program_id(0)
    atoms = acc.shape[0]
    v3 = p3[...]
    v4 = p4[...]
    h3 = (v3 * sigma(v3)).T.astype(LOW)
    h4 = (v4 * sigma(v4)).T.astype(LOW)
    up3 = nn(h3, wu3[...])
    s = sigma(up3)
    du3[...] = slope_of(up3, s).astype(LOW)
    total = up3 * s
    up4 = nn(h4, wu4[...])
    s = sigma(up4)
    du4[...] = slope_of(up4, s).astype(LOW)
    total = total + up4 * s
    skip = nn(edge[...], wsk[...])
    s = sigma(skip)
    dsk[...] = slope_of(skip, s).astype(LOW)
    mixed = (total + skip * s) * THIRD_ROOT
    low_mixed = mixed.astype(LOW)
    mixlow[...] = low_mixed
    res = nn(low_mixed, wr1[...])
    s = sigma(res)
    dr1[...] = slope_of(res, s).astype(LOW)
    hid = (res * s).astype(LOW)
    reshid[...] = hid
    res2 = nn(hid, wr2[...])
    s = sigma(res2)
    dr2[...] = (0.5 * slope_of(res2, s)).astype(LOW)
    out = (edge[...].astype(WIDE) + (mixed + res2 * s) * HALF_ROOT) * HALF_ROOT
    merged[...] = out
    weighted = (out * nn(radial[...], wra[...])).astype(LOW)
    hot_t = (lax.broadcasted_iota(jnp.int32, (atoms, TILE), 0) == trow[...]).astype(LOW)
    part = nn(hot_t, weighted)

    @pl.when(step == 0)
    def _():
        acc[...] = part

    @pl.when(step > 0)
    def _():
        acc[...] += part

    @pl.when(step == pl.num_programs(0) - 1)
    def _():
        g = acc[...].astype(LOW)
        gath[...] = g
        pre = nn(g, wat[...])
        sa = sigma(pre)
        aslope[...] = HALF_ROOT * slope_of(pre, sa)
        anew[...] = ((atom[...].astype(WIDE) + pre * sa) * HALF_ROOT).astype(LOW)


def out_body(
    merged, radial, trow, anew, cot, wc, wro, wout, ocot, acot, aslope, gath, wat,
    enew, gmer, aout, gatom, gw2, *rest, parts, peers, inside,
):
    outs, (ogat, seg, both, awc, aro, aoa) = rest[:-6], rest[-6:]
    step = pl.program_id(0)
    atoms, wide = ogat.shape
    aw = anew.shape[1]

    @pl.when(step == 0)
    def _():
        both[:, 0:wide] = split_pair(nt(ocot[...], wout[...]))
        both[:, wide : 2 * wide] = split_pair(nn(anew[...], wc[0:aw, :]))
        ogat[...] = jnp.zeros_like(ogat)
        seg[...] = jnp.zeros_like(seg)
        awc[...] = jnp.zeros_like(awc)
        aro[...] = jnp.zeros_like(aro)

    hot_t = (lax.broadcasted_iota(jnp.int32, (atoms, TILE), 0) == trow[...]).astype(LOW)
    spread = tn(jnp.concatenate([hot_t, hot_t], axis=0), both[...])
    gow = spread[:, 0:wide]
    m = merged[...]
    ml = m.astype(LOW)
    wcm = wc[aw:, :]
    pre = spread[:, wide:] + nn(ml, wcm)
    s = sigma(pre)
    new = (m + pre * s) * HALF_ROOT
    enew[...] = new.astype(LOW)
    rout = nn(radial[...], wro[...])
    ogat[...] += nn(hot_t, (new * rout).astype(LOW))
    gnew = cot[...].astype(WIDE) + gow * rout
    aro[...] += tn(radial[...], (gow * new).astype(LOW))
    lc = (gnew * (HALF_ROOT * slope_of(pre, s))).astype(LOW)
    awc[aw:, :] += tn(ml, lc)
    seg[...] += nn(hot_t, lc)
    gmer[...] = gnew * HALF_ROOT + nt(lc, wcm)

    @pl.when(step == pl.num_programs(0) - 1)
    def _():
        ol = ogat[...].astype(LOW)
        aout[...] = nn(ol, wout[...]).astype(LOW)
        aoa[:, 0:aw] = tn(ol, ocot[...])
        pair = split_pair(seg[...])
        hi = pair[0:atoms, :]
        lo = pair[atoms:, :]
        awc[0:aw, :] = tn(anew[...], hi) + tn(anew[...], lo)
        wca = wc[0:aw, :]
        ga = acot[...].astype(WIDE) + nt(hi, wca) + nt(lo, wca)
        gatom[...] = (ga * HALF_ROOT).astype(LOW)
        la = (ga * aslope[...]).astype(LOW)
        aoa[:, aw : 2 * aw] = tn(gath[...], la)
        gw2[...] = split_pair(nt(la, wat[...]))
        emit(outs, parts, (awc, aoa, aro), peers, inside)


def back_body(
    edge, radial, trow, s3, s4, merged, gmer, gw2, p3, p4, mixlow, reshid, dsk, du3, du4, dr1, dr2,
    wu3, wu4, wsk, wr1, wr2, wra, *rest, parts, peers, inside,
):
    if inside:
        before, rest = rest[:2], rest[2:]
    (gm_out, ls_out, lb3, lb4), outs = rest[:4], rest[4:-6]
    ask, ar1, ar2, ara, aup, abil = rest[-6:]
    step = pl.program_id(0)
    pair = gw2.shape[0]
    n3 = wu3.shape[0]

    @pl.when(step == 0)
    def _():
        ask[...] = jnp.zeros_like(ask)
        ar1[...] = jnp.zeros_like(ar1)
        ar2[...] = jnp.zeros_like(ar2)
        ara[...] = jnp.zeros_like(ara)
        aup[...] = jnp.zeros_like(aup)
        abil[...] = jnp.zeros_like(abil)

    hot_t = (lax.broadcasted_iota(jnp.int32, (pair // 2, TILE), 0) == trow[...]).astype(LOW)
    gw = tn(jnp.concatenate([hot_t, hot_t], axis=0), gw2[...])
    gm = gmer[...] + gw * nn(radial[...], wra[...])
    ara[...] += tn(radial[...], (gw * merged[...]).astype(LOW))
    l2 = (gm * dr2[...].astype(WIDE)).astype(LOW)
    ar2[...] += tn(reshid[...], l2)
    l1 = (nt(l2, wr2[...]) * dr1[...].astype(WIDE)).astype(LOW)
    ar1[...] += tn(mixlow[...], l1)
    gmix = (gm * 0.5 + nt(l1, wr1[...])) * THIRD_ROOT
    ls = (gmix * dsk[...].astype(WIDE)).astype(LOW)
    l3 = (gmix * du3[...].astype(WIDE)).astype(LOW)
    l4 = (gmix * du4[...].astype(WIDE)).astype(LOW)
    ask[...] += tn(edge[...], ls)
    gm_out[...] = gm * HALF_ROOT
    ls_out[...] = ls
    v3 = p3[...]
    g3 = sigma(v3)
    v4 = p4[...]
    g4 = sigma(v4)
    aup[0:n3, :] += nn((v3 * g3).astype(LOW), l3)
    aup[n3:, :] += nn((v4 * g4).astype(LOW), l4)
    low3 = (nt(wu3[...], l3) * slope_of(v3, g3)).astype(LOW)
    low4 = (nt(wu4[...], l4) * slope_of(v4, g4)).astype(LOW)
    lb3[...] = low3
    lb4[...] = low4
    abil[0:n3, :] += nt(low3, s3[...])
    abil[n3:, :] += nt(low4, s4[...])

    @pl.when(step == pl.num_programs(0) - 1)
    def _():
        values = (ask, ar1, ar2, ara, aup, abil)
        if inside:
            first = before[0].shape[2]
            for out, past in zip(outs, before):
                out[:, :, 0:first, :] = past[...]
            emit(outs, parts, values, peers, inside, first)
        else:
            emit(outs, parts, values, peers, inside)


def unweigh(coef, dsum, index, mask, spread, hots, group, basis, width):
    slabs = spread.shape[0] // width
    for k in range(group * GROUP, (group + 1) * GROUP):
        low_part = (index[k : k + 1, :] & (TILE - 1)).astype(WIDE).astype(LOW)
        hots[:, k * TILE : (k + 1) * TILE] = hot_of(low_part)
    acc = [None] * GROUP
    for c in range(basis):
        d = dsum[c * width : (c + 1) * width, :]
        for j in range(GROUP):
            row = (group * GROUP + j) * basis + c
            term = jnp.broadcast_to(coef[row : row + 1, :], d.shape).astype(LOW) * d
            acc[j] = term if acc[j] is None else acc[j] + term
    for j in range(GROUP):
        k = group * GROUP + j
        got = chosen(index[k : k + 1, :], mask[k : k + 1, :]) >> 8
        slab = jnp.broadcast_to(got.astype(WIDE), (width, TILE)).astype(LOW)
        for s in range(slabs):
            spread[s * width : (s + 1) * width, k * TILE : (k + 1) * TILE] = jnp.where(
                slab == s, acc[j], jnp.zeros((), LOW)
            )


def scatter_body(lb, idx, mask, basis, wt, grad, far, acc, coef, dsum, spread, hots, w, *, edges):
    step = pl.program_id(0)
    n = wt.shape[0]
    slots = idx.shape[0]

    @pl.when(step == 0)
    def _():
        acc[...] = jnp.zeros_like(acc)
        w[...] = wt[...].astype(WIDE).T.astype(LOW)

    coef[...] = basis[...].astype(WIDE).T
    dsum[...] = nn(w[...], lb[...]).astype(LOW)
    for group in range(slots // GROUP):
        part = slice(group * GROUP * TILE, (group + 1) * GROUP * TILE)
        unweigh(coef, dsum, idx, mask, spread, hots, group, coef.shape[0] // slots, n)
        acc[...] += nt(spread[:, part], hots[:, part])

    @pl.when(step == pl.num_programs(0) - 1)
    def _():
        local = edges // TILE
        for s in range(local):
            grad[:, s * TILE : (s + 1) * TILE] = acc[s * n : (s + 1) * n, :]
        for s in range(local, acc.shape[0] // n):
            filler = jnp.zeros((LANES - n, TILE), WIDE)
            part = jnp.concatenate([acc[s * n : (s + 1) * n, :], filler], axis=0).T.astype(LOW)
            at = (s - local) * TILE
            size = min(TILE, far.shape[0] - at)
            far[at : at + size, :] = part[0:size, :]


def source_back_body(edge, radial, grad, down, ret, asked, ws, wr, wd, *rest, low, parts, peers, inside, after):
    if inside and after:
        before, rest = rest[:2], rest[2:]
    low_out, outs, (asum, arad, adn, rt) = rest[0], rest[1:-4], rest[-4:]
    step = pl.program_id(0)
    n = grad.shape[0]

    @pl.when(step == 0)
    def _():
        rt[...] = ret[...].astype(WIDE).T.astype(LOW)
        asum[...] = jnp.zeros_like(asum)
        arad[...] = jnp.zeros_like(arad)
        adn[...] = jnp.zeros_like(adn)

    place = lax.broadcasted_iota(jnp.int32, (TILE, asked.shape[1]), 0) + step * TILE
    back = nt(rt[0:n, :], (place == asked[...]).astype(LOW))
    v = down[low : low + n, :]
    ld = (grad[...] + back) * slope_of(v, sigma(v))
    ldt = ld.astype(LOW)
    low_rows = ld.T.astype(LOW)
    e = edge[...]
    r = radial[...]
    pre = nn(e, ws[...])
    rad = nn(r, wr[...])
    s = sigma(pre)
    act = pre * s
    adn[...] += nn(ldt, (act * rad).astype(LOW))
    gm = nn(low_rows, wd[...])
    lo = (gm * rad * slope_of(pre, s)).astype(LOW)
    low_out[...] = lo
    arad[...] += tn(r, (gm * act).astype(LOW))
    asum[...] += tn(e, lo)

    @pl.when(step == pl.num_programs(0) - 1)
    def _():
        if inside and after:
            first = before[0].shape[2]
            for out, past in zip(outs, before):
                out[:, :, 0:first, :] = past[...]
            emit(outs, parts, (asum, arad, adn), peers, inside, first)
        else:
            emit(outs, parts, (asum, arad, adn), peers, inside)


def edge_grad_body(gm, ls, l3, l4, wsk, ws3, ws4, gedge):
    total = gm[...] + nt(ls[...], wsk[...]) + nt(l3[...], ws3[...]) + nt(l4[...], ws4[...])
    gedge[...] = total.astype(LOW)


def swap(v, axis, mask):
    count = lax.axis_size(axis)
    return lax.ppermute(v, axis, [(j, j ^ mask) for j in range(count)])


def summed(v, axis, shift):
    total = v[0].astype(WIDE)
    for m in range(1, v.shape[0]):
        total = total + swap(v[m], axis, m << shift).astype(WIDE)
    return total.astype(LOW)


def core_sum(send, keep):
    return (keep.astype(WIDE) + swap(send, "edge", 1).astype(WIDE)).astype(LOW)


def group_sum(v):
    return summed(v, "grp", 0)


def share_sum(v):
    at = 1
    while v.shape[0] > 1:
        width = min(4, v.shape[0])
        v = v.reshape(v.shape[0] // width, width, *v.shape[1:])
        v = summed(jnp.moveaxis(v, 1, 0), "edge", at)
        at += width.bit_length() - 1
    return v[0]


def group_gather(v):
    return (v,) + tuple(swap(v, "grp", m) for m in range(1, PARTS))


def exchange(v, peers):
    parts = v.reshape(peers, v.shape[0] // peers, v.shape[1])
    return lax.all_to_all(parts, "edge", split_axis=0, concat_axis=0, tiled=True).reshape(v.shape)


def per_device(
    edge_embed, atom_embed, radial_basis, triplet_basis, quadruplet_basis,
    triplet_source_row, triplet_mask, quadruplet_source_row, quadruplet_mask,
    edge_target_atom, borrowed_edges,
    w_source_trip, w_rbf_trip, w_down_trip, w_source_quad, w_rbf_quad, w_down_quad,
    triplet_bilinear_weight, w_up_trip, w_bilinear_quad, w_up_quad, w_skip,
    w_res_first, w_res_second, w_rbf_atom, w_atom, w_concat, w_rbf_out, w_out,
    edge_cotangent, atom_cotangent, output_cotangent,
):
    edges, wide = edge_embed.shape
    atoms, aw = atom_embed.shape
    rbf = radial_basis.shape[1]
    peers = lax.axis_size("edge")
    cap = borrowed_edges.shape[2]
    steps = edges // TILE
    n3, n4 = w_down_trip.shape[1], w_down_quad.shape[1]
    nb = n3 + n4
    k3, k4 = triplet_mask.shape[1], quadruplet_mask.shape[1]
    f3, f4 = triplet_bilinear_weight.shape[0], w_bilinear_quad.shape[0]
    q3, q4 = triplet_basis.shape[1], quadruplet_basis.shape[1]
    ghosts = peers * cap
    ghosts_up = -(-ghosts // TILE) * TILE
    slabs = (edges + ghosts_up) // TILE

    inside = fits(peers, rbf)
    far_ids = lax.all_to_all(borrowed_edges[0], "edge", split_axis=0, concat_axis=0, tiled=True)

    i3, m3 = triplet_source_row.T, triplet_mask.T
    i4, m4 = quadruplet_source_row.T, quadruplet_mask.T
    wd3, wd4 = w_down_trip.T, w_down_quad.T
    wb3, wb4 = triplet_bilinear_weight.T, w_bilinear_quad.T
    trow = edge_target_atom
    sources = (w_source_trip, w_rbf_trip, wd3, w_source_quad, w_rbf_quad, wd4)

    table, down = call(
        source_body, "source_rows", steps, 10, (edge_embed, radial_basis) + sources,
        [rows(wide), rows(rbf)] + [whole(w) for w in sources],
        [((nb, edges), LOW), ((nb, edges), WIDE)], [cols(nb), cols(nb)], [],
    )
    table, far_ids = lax.optimization_barrier((table, far_ids))
    sent, asked = call(
        sent_body, "sent_rows", 1, 2, (table, far_ids), [whole(table), whole(far_ids)],
        [((ghosts, LANES), LOW), ((1, ghosts), jnp.int32)], [fixed(ghosts, LANES), fixed(1, ghosts)], [],
    )
    ghost = exchange(sent, peers)

    s3, s4, p3, p4 = call(
        gather_body, "gather_sums", steps, 25,
        (table, ghost, i3, m3, i4, m4, triplet_basis, quadruplet_basis, wb3, wb4),
        [whole(table), whole(ghost), cols(k3), cols(k3), cols(k4), cols(k4), rows(q3), rows(q4),
         whole(wb3), whole(wb4)],
        [((f3, edges), LOW), ((f4, edges), LOW), ((n3, edges), WIDE), ((n4, edges), WIDE)],
        [cols(f3), cols(f4), cols(n3), cols(n4)],
        [
            pltpu.VMEM((slabs * n3, TILE), LOW), pltpu.VMEM((slabs * n4, TILE), LOW),
            pltpu.VMEM((k3, n3, TILE), LOW), pltpu.VMEM((k4, n4, TILE), LOW),
            pltpu.VMEM((q3, TILE), WIDE), pltpu.VMEM((q4, TILE), WIDE),
        ],
    )

    act = ((edges, wide), LOW)
    ups = (w_up_trip, w_up_quad, w_skip, w_res_first, w_res_second, w_rbf_atom)
    merged, mixlow, reshid, dsk, du3, du4, dr1, dr2, gath, anew, aslope = call(
        mix_body, "edge_update", steps, 19,
        (edge_embed, radial_basis, p3, p4, trow) + ups + (w_atom, atom_embed),
        [rows(wide), rows(rbf), cols(n3), cols(n4), cols(1)] + [whole(w) for w in ups + (w_atom, atom_embed)],
        [((edges, wide), WIDE), act, act, act, act, act, act, act,
         ((atoms, wide), LOW), ((atoms, aw), LOW), ((atoms, aw), WIDE)],
        [rows(wide)] * 8 + [fixed(atoms, wide), fixed(atoms, aw), fixed(atoms, aw)],
        [pltpu.VMEM((atoms, wide), WIDE)],
    )

    first_parts = (("rows", w_concat.shape), ("rows", (wide, 2 * aw)), ("rows", w_rbf_out.shape))
    outs = (w_concat, w_rbf_out, w_out, output_cotangent, atom_cotangent, aslope, gath, w_atom)
    shapes, specs = grad_outs(first_parts, peers, inside)
    enew, gmer, aout, gatom, gw2, *first = call(
        functools.partial(out_body, parts=first_parts, peers=peers, inside=inside), "output_block", steps, 16,
        (merged, radial_basis, trow, anew, edge_cotangent) + outs,
        [rows(wide), rows(rbf), cols(1), whole(anew), rows(wide)] + [whole(w) for w in outs],
        [act, ((edges, wide), WIDE), ((atoms, aw), LOW), ((atoms, aw), LOW), ((2 * atoms, wide), LOW)] + shapes,
        [rows(wide), rows(wide), fixed(atoms, aw), fixed(atoms, aw), fixed(2 * atoms, wide)] + specs,
        [
            pltpu.VMEM((atoms, wide), WIDE), pltpu.VMEM((atoms, wide), WIDE),
            pltpu.VMEM((2 * atoms, 2 * wide), LOW),
            pltpu.VMEM(w_concat.shape, WIDE), pltpu.VMEM(w_rbf_out.shape, WIDE), pltpu.VMEM((wide, 2 * aw), WIDE),
        ],
    )

    square = w_skip.shape
    second_parts = (
        ("rows", square), ("rows", square), ("rows", square), ("rows", w_rbf_atom.shape),
        ("cols", (nb, wide)), ("cols", (nb, f3)),
    )
    if inside:
        shapes, specs = grad_outs(first_parts + second_parts, peers, inside)
    else:
        shapes, specs = grad_outs(second_parts, peers, inside)
    more = tuple(first) if inside else ()
    gmh, ls, lb3, lb4, *grads = call(
        functools.partial(back_body, parts=second_parts, peers=peers, inside=inside), "edge_update_back", steps, 24,
        (edge_embed, radial_basis, trow, s3, s4, merged, gmer, gw2, p3, p4, mixlow, reshid, dsk,
         du3, du4, dr1, dr2) + ups + more,
        [rows(wide), rows(rbf), cols(1), cols(f3), cols(f4), rows(wide), rows(wide), whole(gw2),
         cols(n3), cols(n4)] + [rows(wide)] * 7 + [whole(w) for w in ups + more],
        [((edges, wide), WIDE), act, ((n3, edges), LOW), ((n4, edges), LOW)] + shapes,
        [rows(wide), rows(wide), cols(n3), cols(n4)] + specs,
        [pltpu.VMEM(square, WIDE)] * 3
        + [pltpu.VMEM(w_rbf_atom.shape, WIDE), pltpu.VMEM((nb, wide), WIDE), pltpu.VMEM((nb, f3), WIDE)],
    )
    early_parts = first_parts + second_parts
    early = core_sum(*(grads if inside else pack(early_parts, tuple(first) + tuple(grads), peers)))

    def scatter(lb, idx, mask, basis, wt, name, micros):
        n, slots, q, f = wt.shape[0], idx.shape[0], basis.shape[1], wt.shape[1]
        return call(
            functools.partial(scatter_body, edges=edges), name, steps, micros, (lb, idx, mask, basis, wt),
            [cols(n), cols(slots), cols(slots), rows(q), whole(wt)],
            [((n, edges), WIDE), ((ghosts, LANES), LOW)],
            [fixed(n, edges), fixed(ghosts, LANES)],
            [
                pltpu.VMEM((slabs * n, TILE), WIDE), pltpu.VMEM((q, TILE), WIDE), pltpu.VMEM((f, TILE), LOW),
                pltpu.VMEM((slabs * n, slots * TILE), LOW), pltpu.VMEM((TILE, slots * TILE), LOW),
                pltpu.VMEM((f, n), LOW),
            ],
        )

    third_parts = (("rows", square), ("rows", w_rbf_trip.shape))
    quad_parts = third_parts + (("cols", (n4, wide)),)
    trip_parts = third_parts + (("cols", (n3, wide)),)

    def source_back(grad, ret, ws, wr, wd, low, parts, before, name):
        n = wd.shape[0]
        whole_parts = (quad_parts if before else ()) + parts
        shapes, specs = grad_outs(whole_parts if inside else parts, peers, inside)
        more = tuple(before) if inside else ()
        body = functools.partial(
            source_back_body, low=low, parts=parts, peers=peers, inside=inside, after=bool(before)
        )
        ins = (ret, asked, ws, wr, wd) + more
        low_rows, *grads = call(
            body, name, steps, 11, (edge_embed, radial_basis, grad, down) + ins,
            [rows(wide), rows(rbf), cols(n), cols(nb)] + [whole(x) for x in ins],
            [act] + shapes, [rows(wide)] + specs,
            [pltpu.VMEM(square, WIDE), pltpu.VMEM(w_rbf_trip.shape, WIDE), pltpu.VMEM((n, wide), WIDE),
             pltpu.VMEM((LANES, ghosts), LOW)],
        )
        return low_rows, grads

    grad4, far4 = scatter(lb4, i4, m4, quadruplet_basis, wb4, "scatter_quad", 11)
    lb3, far4, early = lax.optimization_barrier((lb3, far4, early))
    early = group_sum(early)
    ret4 = exchange(far4, peers)
    grad3, far3 = scatter(lb3, i3, m3, triplet_basis, wb3, "scatter_trip", 18)
    ret4, far3, early = lax.optimization_barrier((ret4, far3, early))
    ret3 = exchange(far3, peers)
    early = share_sum(early)
    l4, quads = source_back(grad4, ret4, w_source_quad, w_rbf_quad, wd4, n3, quad_parts, (), "source_back_quad")
    ret3, quads, early = lax.optimization_barrier((ret3, quads, early))
    early = group_gather(early)
    l3, trips = source_back(grad3, ret3, w_source_trip, w_rbf_trip, wd3, 0, trip_parts, quads, "source_back_trip")
    late_parts = quad_parts + trip_parts
    late = trips if inside else pack(late_parts, tuple(quads) + tuple(trips), peers)
    late, gmh, early = lax.optimization_barrier((late, gmh, early))
    late = core_sum(*late)
    last = (w_skip, w_source_trip, w_source_quad)
    (gedge,) = call(
        edge_grad_body, "edge_grad", steps // 2, 6, (gmh, ls, l3, l4) + last,
        [rows(wide, 2 * TILE)] * 4 + [whole(w) for w in last], [act], [rows(wide, 2 * TILE)], [],
    )
    late, gedge = lax.optimization_barrier((late, gedge))
    late = group_gather(share_sum(group_sum(late)))

    turned = tuple(("turned", shape) if kind == "cols" else (kind, shape) for kind, shape in trip_parts)
    r_concat, r_oa, r_out, r_sk, r_r1, r_r2, r_ra, r_up, r_bil = assemble(early, early_parts, peers, "assemble_early")
    r_s4, r_r4, r_d4, r_s3, r_r3, r_d3 = assemble(late, quad_parts + turned, peers, "assemble_late")
    return (
        enew, anew, aout, gedge, gatom,
        r_s3, r_r3, r_d3, r_s4, r_r4, r_d4.T,
        r_bil[0:n3].T, r_up[0:n3], r_bil[n3:].T, r_up[n3:],
        r_sk, r_r1, r_r2, r_ra, r_oa[:, aw:], r_concat, r_out, r_oa[:, 0:aw],
    )


def solution(mesh):
    both = P(("grp", "edge"), None)
    placed = (both,) * 10 + (P(("grp", "edge"), None, None),) + (P(),) * 18 + (both,) * 3
    shares = [P("edge", None)] * 18
    shares[7] = P(None, "edge")
    shares[9] = P(None, "edge")
    return jax.shard_map(
        per_device, mesh=mesh, in_specs=placed, out_specs=(both,) * 5 + tuple(shares), check_vma=False
    )
```

```python
import functools
import math

import jax
import jax.numpy as jnp
from jax import lax
from jax.experimental import pallas as pl
from jax.experimental.pallas import tpu as pltpu
from jax.sharding import PartitionSpec as P

HALF_ROOT = 1.0 / math.sqrt(2.0)
THIRD_ROOT = 1.0 / math.sqrt(3.0)
LOW = jnp.bfloat16
WIDE = jnp.float32
TILE = 256
BIG = 512
LANES = 128
GROUP = 4
PARTS = 4
ROOM = {
    "source_rows": 16, "sent_rows": 8, "gather_sums": 14, "edge_update": 18, "output_block": 20,
    "edge_update_back": 24, "scatter_quad": 14, "scatter_trip": 16, "source_back_quad": 16,
    "source_back_trip": 18, "edge_grad": 12, "assemble_early": 8, "assemble_late": 8,
}


def sigma(v):
    return 0.5 * jnp.tanh(0.5 * v) + 0.5


def slope_of(v, s):
    return s * (1.0 + v * (1.0 - s))


def nn(a, b):
    return jnp.dot(a, b, preferred_element_type=WIDE)


def nt(a, b):
    return lax.dot_general(a, b, (((1,), (1,)), ((), ())), preferred_element_type=WIDE)


def tn(a, b):
    return lax.dot_general(a, b, (((0,), (0,)), ((), ())), preferred_element_type=WIDE)


def split_pair(v):
    high = v.astype(LOW)
    rest = (v - high.astype(WIDE)).astype(LOW)
    return jnp.concatenate([high, rest], axis=0)


def whole(array):
    rank = len(array.shape)
    return pl.BlockSpec(array.shape, lambda i: (0,) * rank)


def rows(width, tile=TILE):
    return pl.BlockSpec((tile, width), lambda i: (i, 0))


def cols(height, tile=TILE):
    return pl.BlockSpec((height, tile), lambda i: (0, i))


def fixed(*shape):
    return pl.BlockSpec(shape, lambda i: (0,) * len(shape))


def far_array(v):
    return pltpu.with_memory_space_constraint(v, pltpu.HBM)


def call(body, name, steps, micros, ins, in_specs, outs, out_specs, scratch, far=(), alias={}):
    return pl.pallas_call(
        body,
        name=name,
        out_shape=[(pltpu.HBM if i in far else jax.ShapeDtypeStruct)(s, t) for i, (s, t) in enumerate(outs)],
        grid_spec=pltpu.PrefetchScalarGridSpec(
            num_scalar_prefetch=0,
            grid=(steps,),
            in_specs=in_specs,
            out_specs=out_specs,
            scratch_shapes=scratch,
        ),
        input_output_aliases=alias,
        compiler_params=pltpu.CompilerParams(
            dimension_semantics=("arbitrary",), vmem_limit_bytes=ROOM[name] << 20
        ),
        cost_estimate=pl.CostEstimate(
            flops=int(micros * 1.1e9), transcendentals=0, bytes_accessed=1 << 22
        ),
    )(*ins)


def up16(n):
    return -(-n // 16) * 16


def offsets(parts, peers):
    at, places = 0, []
    for kind, shape in parts:
        places.append(at)
        at += up16(shape[0] // peers if kind == "rows" else shape[0] // PARTS)
    return places, at


def fits(peers, rbf):
    return rbf % (16 * peers) == 0


def grad_outs(parts, peers, inside):
    if inside:
        shapes = [(PARTS, peers // 2, offsets(parts, peers)[1], LANES)] * 2
    else:
        shapes = [shape for _, shape in parts]
    return [(shape, LOW) for shape in shapes], [fixed(*shape) for shape in shapes]


def emit(outs, parts, values, peers, inside, start=0):
    if not inside:
        for out, value in zip(outs, values):
            out[...] = value[...].astype(LOW)
        return
    core = lax.axis_index("edge") & 1
    z = lax.axis_index("edge") >> 1
    grp = lax.axis_index("grp")
    places, _ = offsets(parts, peers)
    for to, side in zip(outs, (1 - core, core)):
        for mz in range(peers // 2):
            for mg in range(PARTS):
                e = ((z ^ mz) << 1) + side
                q = grp ^ mg
                for (kind, shape), place, value in zip(parts, places, values):
                    place += start
                    if kind == "rows":
                        m = shape[0] // peers
                        at = pl.multiple_of(e * m, m)
                        to[mg, mz, place : place + m, :] = value[
                            pl.ds(at, m), pl.ds(pl.multiple_of(q * LANES, LANES), LANES)
                        ].astype(LOW)
                    else:
                        h, w = shape[0] // PARTS, shape[1] // peers
                        at = pl.multiple_of(q * h, 8)
                        if w == LANES:
                            got = value[pl.ds(at, h), pl.ds(pl.multiple_of(e * w, w), w)]
                        else:
                            two = value[pl.ds(at, h), pl.ds(pl.multiple_of((z ^ mz) * LANES, LANES), LANES)]
                            got = jnp.where(side > 0, jnp.concatenate([two[:, w:], two[:, :w]], axis=1), two)
                        if up16(h) > h:
                            got = jnp.concatenate([got, jnp.zeros((up16(h) - h, LANES), WIDE)], axis=0)
                        to[mg, mz, place : place + up16(h), :] = got.astype(LOW)


def pack(parts, grads, peers):
    packed = []
    for (kind, shape), g in zip(parts, grads):
        if kind == "rows":
            g = g.reshape(peers // 2, 2, shape[0] // peers, PARTS, LANES).transpose(1, 3, 0, 2, 4)
        else:
            w = shape[1] // peers
            g = g.reshape(PARTS, shape[0] // PARTS, peers // 2, 2, w).transpose(3, 0, 2, 1, 4)
            g = jnp.pad(g, ((0, 0),) * 4 + ((0, LANES - w),))
        rows_up = up16(g.shape[3])
        packed.append(jnp.pad(g, ((0, 0),) * 3 + ((0, rows_up - g.shape[3]), (0, 0))))
    packed = jnp.concatenate(packed, axis=3)
    place = lax.axis_index("edge")
    own = place & 1
    packed = jnp.take(packed, jnp.arange(PARTS) ^ lax.axis_index("grp"), axis=1)
    packed = jnp.take(packed, jnp.arange(peers // 2) ^ (place >> 1), axis=2)
    return [lax.dynamic_index_in_dim(packed, side, 0, keepdims=False) for side in (1 - own, own)]


def assemble_body(*refs, parts, peers):
    arrived, outs, tmp = refs[:PARTS], refs[PARTS:-1], refs[-1]
    grp = lax.axis_index("grp")
    for (kind, shape), place, out in zip(parts, offsets(parts, peers)[0], outs):
        m = shape[0] // peers
        h, w = shape[0] // PARTS, shape[1] // peers
        for mg in range(PARTS):
            q = grp ^ mg
            if kind == "rows":
                got = arrived[mg][place : place + m, :].astype(WIDE)
                out[:, pl.ds(pl.multiple_of(q * LANES, LANES), LANES)] = got
            else:
                tmp[pl.ds(pl.multiple_of(q * h, 8), h), :] = arrived[mg][place : place + h, :].astype(WIDE)
        if kind == "cols":
            out[...] = tmp[0 : shape[0], 0:w]
        if kind == "turned":
            out[...] = tmp[0 : shape[0], :].T[0:w, :]


def assemble(arrived, parts, peers, name):
    shapes = []
    for kind, (n, w) in parts:
        shapes.append((n // peers, w) if kind == "rows" else (n, w // peers) if kind == "cols" else (w // peers, n))
    return call(
        functools.partial(assemble_body, parts=parts, peers=peers), name, 1, 2, arrived,
        [whole(v) for v in arrived], [(shape, WIDE) for shape in shapes], [fixed(*shape) for shape in shapes],
        [pltpu.VMEM((LANES, LANES), WIDE)],
    )


def source_body(edge, radial, ws3, wr3, wd3, ws4, wr4, wd4, table, down):
    e = edge[...]
    r = radial[...]
    pre3 = nn(e, ws3[...])
    mix3 = (pre3 * sigma(pre3) * nn(r, wr3[...])).astype(LOW)
    down3 = nt(wd3[...], mix3)
    pre4 = nn(e, ws4[...])
    mix4 = (pre4 * sigma(pre4) * nn(r, wr4[...])).astype(LOW)
    down4 = nt(wd4[...], mix4)
    both = jnp.concatenate([down3, down4], axis=0)
    down[...] = both
    table[...] = (both * sigma(both)).astype(LOW)


def sent_body(table, asked, sent, row):
    nb, edges = table.shape
    ghosts = row.shape[1]
    got = jnp.concatenate([asked[p : p + 1, :] for p in range(asked.shape[0])], axis=1) & (edges - 1)
    row[...] = got
    total = jnp.zeros((nb, ghosts), WIDE)
    for s in range(edges // TILE):
        place = lax.broadcasted_iota(jnp.int32, (TILE, ghosts), 0) + s * TILE
        total = total + nn(table[:, s * TILE : (s + 1) * TILE], (place == got).astype(LOW))
    total = jnp.concatenate([total, jnp.zeros((LANES - nb, ghosts), WIDE)], axis=0)
    sent[...] = total.T.astype(LOW)


def fill_slabs(tab, ghost, t3, t4, n3, n4):
    local = tab.shape[1] // TILE
    for s in range(local):
        t3[s * n3 : (s + 1) * n3, :] = tab[0:n3, s * TILE : (s + 1) * TILE]
        t4[s * n4 : (s + 1) * n4, :] = tab[n3 : n3 + n4, s * TILE : (s + 1) * TILE]
    for g in range(0, ghost.shape[0], TILE):
        s = local + g // TILE
        size = min(TILE, ghost.shape[0] - g)
        part = ghost[g : g + size, :].astype(WIDE).T
        if size < TILE:
            part = jnp.concatenate([part, jnp.zeros((LANES, TILE - size), WIDE)], axis=1)
        t3[s * n3 : (s + 1) * n3, :] = part[0:n3, :].astype(LOW)
        t4[s * n4 : (s + 1) * n4, :] = part[n3 : n3 + n4, :].astype(LOW)


def hot_of(low_part):
    place = lax.broadcasted_iota(jnp.int32, (TILE, TILE), 0).astype(WIDE).astype(LOW)
    return jnp.where(place == low_part, jnp.ones((), LOW), jnp.zeros((), LOW))


def pick(tab, index_row, width):
    slabs = tab.shape[0] // width
    low_part = (index_row & (TILE - 1)).astype(WIDE).astype(LOW)
    slab = jnp.broadcast_to((index_row >> 8).astype(WIDE), (width, TILE)).astype(LOW)
    found = nn(tab[...], hot_of(low_part)).astype(LOW)
    got = jnp.zeros((width, TILE), LOW)
    for s in range(slabs):
        got = jnp.where(slab == s, found[s * width : (s + 1) * width, :], got)
    return got


def weigh(coef, picked, out, group, basis, width):
    for cb in range(basis // 4):
        acc = [None] * 4
        for k in range(group * GROUP, (group + 1) * GROUP):
            g = picked[k]
            for j in range(4):
                row = k * basis + cb * 4 + j
                term = jnp.broadcast_to(coef[row : row + 1, :], g.shape).astype(LOW) * g
                acc[j] = term if acc[j] is None else acc[j] + term
        for j in range(4):
            at = (cb * 4 + j) * width
            before = out[at : at + width, :] + acc[j] if group else acc[j]
            out[at : at + width, :] = before


def chosen(index, mask):
    return jnp.where(mask > 0, index, -1)


def gather_body(
    tab, ghost, i3, m3, i4, m4, b3, b4, w3t, w4t, s3, s4, p3, p4, t3, t4, g3, g4, c3, c4
):
    n3, n4 = w3t.shape[0], w4t.shape[0]
    k3, k4 = i3.shape[0], i4.shape[0]

    @pl.when(pl.program_id(0) == 0)
    def _():
        fill_slabs(tab, ghost, t3, t4, n3, n4)

    c3[...] = b3[...].astype(WIDE).T
    c4[...] = b4[...].astype(WIDE).T

    work = [(t3, i3, m3, g3, c3, s3, n3, k3, j) for j in range(k3 // GROUP)]
    work += [(t4, i4, m4, g4, c4, s4, n4, k4, j) for j in range(k4 // GROUP)]
    for at in range(len(work) + 1):
        if at < len(work):
            t, i, m, g, _, _, n, _, j = work[at]
            for k in range(j * GROUP, (j + 1) * GROUP):
                g[k] = pick(t, chosen(i[k : k + 1, :], m[k : k + 1, :]), n)
        if at:
            _, _, _, g, c, out, n, count, j = work[at - 1]
            weigh(c, g, out, j, c.shape[0] // count, n)
    p3[...] = nn(w3t[...], s3[...])
    p4[...] = nn(w4t[...], s4[...])


def mix_body(
    edge, radial, p3, p4, trow, wu3, wu4, wsk, wr1, wr2, wra, wat, atom,
    merged, mixlow, reshid, dsk, du3, du4, dr1, dr2, gath, anew, aslope, acc,
):
    step = pl.program_id(0)
    atoms = acc.shape[0]
    v3 = p3[...]
    v4 = p4[...]
    h3 = (v3 * sigma(v3)).T.astype(LOW)
    h4 = (v4 * sigma(v4)).T.astype(LOW)
    up3 = nn(h3, wu3[...])
    s = sigma(up3)
    du3[...] = slope_of(up3, s).astype(LOW)
    total = up3 * s
    up4 = nn(h4, wu4[...])
    s = sigma(up4)
    du4[...] = slope_of(up4, s).astype(LOW)
    total = total + up4 * s
    skip = nn(edge[...], wsk[...])
    s = sigma(skip)
    dsk[...] = slope_of(skip, s).astype(LOW)
    mixed = (total + skip * s) * THIRD_ROOT
    low_mixed = mixed.astype(LOW)
    mixlow[...] = low_mixed
    res = nn(low_mixed, wr1[...])
    s = sigma(res)
    dr1[...] = slope_of(res, s).astype(LOW)
    hid = (res * s).astype(LOW)
    reshid[...] = hid
    res2 = nn(hid, wr2[...])
    s = sigma(res2)
    dr2[...] = (0.5 * slope_of(res2, s)).astype(LOW)
    out = (edge[...].astype(WIDE) + (mixed + res2 * s) * HALF_ROOT) * HALF_ROOT
    merged[...] = out
    weighted = (out * nn(radial[...], wra[...])).astype(LOW)
    hot_t = (lax.broadcasted_iota(jnp.int32, (atoms, edge.shape[0]), 0) == trow[...]).astype(LOW)
    part = nn(hot_t, weighted)

    @pl.when(step == 0)
    def _():
        acc[...] = part

    @pl.when(step > 0)
    def _():
        acc[...] += part

    @pl.when(step == pl.num_programs(0) - 1)
    def _():
        g = acc[...].astype(LOW)
        gath[...] = g
        pre = nn(g, wat[...])
        sa = sigma(pre)
        aslope[...] = HALF_ROOT * slope_of(pre, sa)
        anew[...] = ((atom[...].astype(WIDE) + pre * sa) * HALF_ROOT).astype(LOW)


def out_body(
    merged, radial, trow, anew, cot, wc, wro, wout, ocot, acot, aslope, gath, wat,
    enew, gmer, aout, gatom, gw2, *rest, parts, peers, inside,
):
    outs, (ogat, seg, both, awc, aro, aoa) = rest[:-6], rest[-6:]
    step = pl.program_id(0)
    atoms, wide = ogat.shape
    aw = anew.shape[1]

    @pl.when(step == 0)
    def _():
        both[:, 0:wide] = split_pair(nt(ocot[...], wout[...]))
        both[:, wide : 2 * wide] = split_pair(nn(anew[...], wc[0:aw, :]))
        ogat[...] = jnp.zeros_like(ogat)
        seg[...] = jnp.zeros_like(seg)
        awc[...] = jnp.zeros_like(awc)
        aro[...] = jnp.zeros_like(aro)

    hot_t = (lax.broadcasted_iota(jnp.int32, (atoms, merged.shape[0]), 0) == trow[...]).astype(LOW)
    spread = tn(jnp.concatenate([hot_t, hot_t], axis=0), both[...])
    gow = spread[:, 0:wide]
    m = merged[...]
    ml = m.astype(LOW)
    wcm = wc[aw:, :]
    pre = spread[:, wide:] + nn(ml, wcm)
    s = sigma(pre)
    new = (m + pre * s) * HALF_ROOT
    enew[...] = new.astype(LOW)
    rout = nn(radial[...], wro[...])
    ogat[...] += nn(hot_t, (new * rout).astype(LOW))
    gnew = cot[...].astype(WIDE) + gow * rout
    aro[...] += tn(radial[...], (gow * new).astype(LOW))
    lc = (gnew * (HALF_ROOT * slope_of(pre, s))).astype(LOW)
    awc[aw:, :] += tn(ml, lc)
    seg[...] += nn(hot_t, lc)
    gmer[...] = gnew * HALF_ROOT + nt(lc, wcm)

    @pl.when(step == pl.num_programs(0) - 1)
    def _():
        ol = ogat[...].astype(LOW)
        aout[...] = nn(ol, wout[...]).astype(LOW)
        aoa[:, 0:aw] = tn(ol, ocot[...])
        pair = split_pair(seg[...])
        hi = pair[0:atoms, :]
        lo = pair[atoms:, :]
        awc[0:aw, :] = tn(anew[...], hi) + tn(anew[...], lo)
        wca = wc[0:aw, :]
        ga = acot[...].astype(WIDE) + nt(hi, wca) + nt(lo, wca)
        gatom[...] = (ga * HALF_ROOT).astype(LOW)
        la = (ga * aslope[...]).astype(LOW)
        aoa[:, aw : 2 * aw] = tn(gath[...], la)
        gw2[...] = split_pair(nt(la, wat[...]))
        emit(outs, parts, (awc, aoa, aro), peers, inside)


def back_body(
    edge, radial, trow, s3, s4, merged, gmer, gw2, p3, p4, mixlow, reshid, dsk, du3, du4, dr1, dr2,
    wu3, wu4, wsk, wr1, wr2, wra, *rest, parts, peers, inside,
):
    if inside:
        before, rest = rest[:2], rest[2:]
    (gm_out, ls_out, lb3, lb4), outs = rest[:4], rest[4:-6]
    ask, ar1, ar2, ara, aup, abil = rest[-6:]
    step = pl.program_id(0)
    pair = gw2.shape[0]
    n3 = wu3.shape[0]

    @pl.when(step == 0)
    def _():
        ask[...] = jnp.zeros_like(ask)
        ar1[...] = jnp.zeros_like(ar1)
        ar2[...] = jnp.zeros_like(ar2)
        ara[...] = jnp.zeros_like(ara)
        aup[...] = jnp.zeros_like(aup)
        abil[...] = jnp.zeros_like(abil)

    hot_t = (lax.broadcasted_iota(jnp.int32, (pair // 2, edge.shape[0]), 0) == trow[...]).astype(LOW)
    gw = tn(jnp.concatenate([hot_t, hot_t], axis=0), gw2[...])
    gm = gmer[...] + gw * nn(radial[...], wra[...])
    ara[...] += tn(radial[...], (gw * merged[...]).astype(LOW))
    l2 = (gm * dr2[...].astype(WIDE)).astype(LOW)
    ar2[...] += tn(reshid[...], l2)
    l1 = (nt(l2, wr2[...]) * dr1[...].astype(WIDE)).astype(LOW)
    ar1[...] += tn(mixlow[...], l1)
    gmix = (gm * 0.5 + nt(l1, wr1[...])) * THIRD_ROOT
    ls = (gmix * dsk[...].astype(WIDE)).astype(LOW)
    l3 = (gmix * du3[...].astype(WIDE)).astype(LOW)
    l4 = (gmix * du4[...].astype(WIDE)).astype(LOW)
    ask[...] += tn(edge[...], ls)
    gm_out[...] = gm * HALF_ROOT
    ls_out[...] = ls
    v3 = p3[...]
    g3 = sigma(v3)
    v4 = p4[...]
    g4 = sigma(v4)
    aup[0:n3, :] += nn((v3 * g3).astype(LOW), l3)
    aup[n3:, :] += nn((v4 * g4).astype(LOW), l4)
    low3 = (nt(wu3[...], l3) * slope_of(v3, g3)).astype(LOW)
    low4 = (nt(wu4[...], l4) * slope_of(v4, g4)).astype(LOW)
    lb3[...] = low3
    lb4[...] = low4
    abil[0:n3, :] += nt(low3, s3[...])
    abil[n3:, :] += nt(low4, s4[...])

    @pl.when(step == pl.num_programs(0) - 1)
    def _():
        values = (ask, ar1, ar2, ara, aup, abil)
        if inside:
            first = before[0].shape[2]
            for out, past in zip(outs, before):
                out[:, :, 0:first, :] = past[...]
            emit(outs, parts, values, peers, inside, first)
        else:
            emit(outs, parts, values, peers, inside)


def unweigh(coef, dsum, index, mask, spread, hots, group, basis, width):
    slabs = spread.shape[0] // width
    for k in range(group * GROUP, (group + 1) * GROUP):
        low_part = (index[k : k + 1, :] & (TILE - 1)).astype(WIDE).astype(LOW)
        hots[:, k * TILE : (k + 1) * TILE] = hot_of(low_part)
    acc = [None] * GROUP
    for c in range(basis):
        d = dsum[c * width : (c + 1) * width, :]
        for j in range(GROUP):
            row = (group * GROUP + j) * basis + c
            term = jnp.broadcast_to(coef[row : row + 1, :], d.shape).astype(LOW) * d
            acc[j] = term if acc[j] is None else acc[j] + term
    for j in range(GROUP):
        k = group * GROUP + j
        got = chosen(index[k : k + 1, :], mask[k : k + 1, :]) >> 8
        slab = jnp.broadcast_to(got.astype(WIDE), (width, TILE)).astype(LOW)
        for s in range(slabs):
            spread[s * width : (s + 1) * width, k * TILE : (k + 1) * TILE] = jnp.where(
                slab == s, acc[j], jnp.zeros((), LOW)
            )


def scatter_body(lb, idx, mask, basis, wt, grad, far, acc, coef, dsum, spread, hots, w, *, edges):
    step = pl.program_id(0)
    n = wt.shape[0]
    slots = idx.shape[0]

    @pl.when(step == 0)
    def _():
        acc[...] = jnp.zeros_like(acc)
        w[...] = wt[...].astype(WIDE).T.astype(LOW)

    coef[...] = basis[...].astype(WIDE).T
    dsum[...] = nn(w[...], lb[...]).astype(LOW)
    for group in range(slots // GROUP):
        part = slice(group * GROUP * TILE, (group + 1) * GROUP * TILE)
        unweigh(coef, dsum, idx, mask, spread, hots, group, coef.shape[0] // slots, n)
        acc[...] += nt(spread[:, part], hots[:, part])

    @pl.when(step == pl.num_programs(0) - 1)
    def _():
        local = edges // TILE
        for s in range(local):
            grad[:, s * TILE : (s + 1) * TILE] = acc[s * n : (s + 1) * n, :]
        for s in range(local, acc.shape[0] // n):
            filler = jnp.zeros((LANES - n, TILE), WIDE)
            part = jnp.concatenate([acc[s * n : (s + 1) * n, :], filler], axis=0).T.astype(LOW)
            at = (s - local) * TILE
            size = min(TILE, far.shape[0] - at)
            far[at : at + size, :] = part[0:size, :]


def source_back_body(edge, radial, grad, down, ret, asked, ws, wr, wd, *rest, low, parts, peers, inside, after):
    if inside and after:
        before, rest = rest[:2], rest[2:]
    low_out, outs, (asum, arad, adn, rt) = rest[0], rest[1:-4], rest[-4:]
    step = pl.program_id(0)
    n = grad.shape[0]

    @pl.when(step == 0)
    def _():
        rt[...] = ret[...].astype(WIDE).T.astype(LOW)
        asum[...] = jnp.zeros_like(asum)
        arad[...] = jnp.zeros_like(arad)
        adn[...] = jnp.zeros_like(adn)

    place = lax.broadcasted_iota(jnp.int32, (edge.shape[0], asked.shape[1]), 0) + step * edge.shape[0]
    back = nt(rt[0:n, :], (place == asked[...]).astype(LOW))
    v = down[low : low + n, :]
    ld = (grad[...] + back) * slope_of(v, sigma(v))
    ldt = ld.astype(LOW)
    low_rows = ld.T.astype(LOW)
    e = edge[...]
    r = radial[...]
    pre = nn(e, ws[...])
    rad = nn(r, wr[...])
    s = sigma(pre)
    act = pre * s
    adn[...] += nn(ldt, (act * rad).astype(LOW))
    gm = nn(low_rows, wd[...])
    lo = (gm * rad * slope_of(pre, s)).astype(LOW)
    low_out[...] = lo
    arad[...] += tn(r, (gm * act).astype(LOW))
    asum[...] += tn(e, lo)

    @pl.when(step == pl.num_programs(0) - 1)
    def _():
        if inside and after:
            first = before[0].shape[2]
            for out, past in zip(outs, before):
                out[:, :, 0:first, :] = past[...]
            emit(outs, parts, (asum, arad, adn), peers, inside, first)
        else:
            emit(outs, parts, (asum, arad, adn), peers, inside)


def edge_grad_body(*refs):
    gm, ls, l3, l4, wsk, ws3, ws4 = refs[:7]
    gedge = refs[-1]
    total = gm[...] + nt(ls[...], wsk[...]) + nt(l3[...], ws3[...]) + nt(l4[...], ws4[...])
    gedge[...] = total.astype(LOW)


def swap(v, axis, mask):
    count = lax.axis_size(axis)
    return lax.ppermute(v, axis, [(j, j ^ mask) for j in range(count)])


def summed(v, axis, shift):
    total = v[0].astype(WIDE)
    for m in range(1, v.shape[0]):
        total = total + swap(v[m], axis, m << shift).astype(WIDE)
    return total.astype(LOW)


def core_sum(send, keep):
    return (keep.astype(WIDE) + swap(send, "edge", 1).astype(WIDE)).astype(LOW)


def group_sum(v):
    return summed(v, "grp", 0)


def share_sum(v):
    at = 1
    while v.shape[0] > 1:
        width = min(4, v.shape[0])
        v = v.reshape(v.shape[0] // width, width, *v.shape[1:])
        v = summed(jnp.moveaxis(v, 1, 0), "edge", at)
        at += width.bit_length() - 1
    return v[0]


def group_gather(v):
    return (v,) + tuple(swap(v, "grp", m) for m in range(1, PARTS))


def exchange(v, peers):
    parts = v.reshape(peers, v.shape[0] // peers, v.shape[1])
    return lax.all_to_all(parts, "edge", split_axis=0, concat_axis=0, tiled=True).reshape(v.shape)


def per_device(
    edge_embed, atom_embed, radial_basis, triplet_basis, quadruplet_basis,
    triplet_source_row, triplet_mask, quadruplet_source_row, quadruplet_mask,
    edge_target_atom, borrowed_edges,
    w_source_trip, w_rbf_trip, w_down_trip, w_source_quad, w_rbf_quad, w_down_quad,
    triplet_bilinear_weight, w_up_trip, w_bilinear_quad, w_up_quad, w_skip,
    w_res_first, w_res_second, w_rbf_atom, w_atom, w_concat, w_rbf_out, w_out,
    edge_cotangent, atom_cotangent, output_cotangent,
):
    edges, wide = edge_embed.shape
    atoms, aw = atom_embed.shape
    rbf = radial_basis.shape[1]
    peers = lax.axis_size("edge")
    cap = borrowed_edges.shape[2]
    steps = edges // TILE
    n3, n4 = w_down_trip.shape[1], w_down_quad.shape[1]
    nb = n3 + n4
    k3, k4 = triplet_mask.shape[1], quadruplet_mask.shape[1]
    f3, f4 = triplet_bilinear_weight.shape[0], w_bilinear_quad.shape[0]
    q3, q4 = triplet_basis.shape[1], quadruplet_basis.shape[1]
    ghosts = peers * cap
    ghosts_up = -(-ghosts // TILE) * TILE
    slabs = (edges + ghosts_up) // TILE

    inside = fits(peers, rbf)
    (
        edge_embed, atom_embed, radial_basis, triplet_basis, quadruplet_basis, edge_cotangent,
        w_source_trip, w_rbf_trip, w_source_quad, w_rbf_quad, w_skip, w_res_first, w_res_second, w_rbf_atom,
        w_atom, w_concat, w_rbf_out, w_out, w_up_trip, w_up_quad, atom_cotangent, output_cotangent,
    ) = map(far_array, (
        edge_embed, atom_embed, radial_basis, triplet_basis, quadruplet_basis, edge_cotangent,
        w_source_trip, w_rbf_trip, w_source_quad, w_rbf_quad, w_skip, w_res_first, w_res_second, w_rbf_atom,
        w_atom, w_concat, w_rbf_out, w_out, w_up_trip, w_up_quad, atom_cotangent, output_cotangent,
    ))
    far_ids = lax.all_to_all(borrowed_edges[0], "edge", split_axis=0, concat_axis=0, tiled=True)

    i3, m3, i4, m4, wd3, wd4, wb3, wb4 = [
        far_array(v.T)
        for v in (
            triplet_source_row, triplet_mask, quadruplet_source_row, quadruplet_mask,
            w_down_trip, w_down_quad, triplet_bilinear_weight, w_bilinear_quad,
        )
    ]
    trow = far_array(edge_target_atom)
    sources = (w_source_trip, w_rbf_trip, wd3, w_source_quad, w_rbf_quad, wd4)

    table, down = call(
        source_body, "source_rows", edges // BIG, 10, (edge_embed, radial_basis) + sources,
        [rows(wide, BIG), rows(rbf, BIG)] + [whole(w) for w in sources],
        [((nb, edges), LOW), ((nb, edges), WIDE)], [cols(nb, BIG), cols(nb, BIG)], [],
    )
    table, far_ids = lax.optimization_barrier((table, far_ids))
    sent, asked = call(
        sent_body, "sent_rows", 1, 2, (table, far_ids), [whole(table), whole(far_ids)],
        [((ghosts, LANES), LOW), ((1, ghosts), jnp.int32)], [fixed(ghosts, LANES), fixed(1, ghosts)], [], far=(1,),
    )
    asked = far_array(asked)
    ghost = exchange(sent, peers)

    s3, s4, p3, p4 = call(
        gather_body, "gather_sums", steps, 25,
        (table, ghost, i3, m3, i4, m4, triplet_basis, quadruplet_basis, wb3, wb4),
        [whole(table), whole(ghost), cols(k3), cols(k3), cols(k4), cols(k4), rows(q3), rows(q4),
         whole(wb3), whole(wb4)],
        [((f3, edges), LOW), ((f4, edges), LOW), ((n3, edges), WIDE), ((n4, edges), WIDE)],
        [cols(f3), cols(f4), cols(n3), cols(n4)],
        [
            pltpu.VMEM((slabs * n3, TILE), LOW), pltpu.VMEM((slabs * n4, TILE), LOW),
            pltpu.VMEM((k3, n3, TILE), LOW), pltpu.VMEM((k4, n4, TILE), LOW),
            pltpu.VMEM((q3, TILE), WIDE), pltpu.VMEM((q4, TILE), WIDE),
        ],
        far=(0, 1),
    )

    act = ((edges, wide), LOW)
    ups = (w_up_trip, w_up_quad, w_skip, w_res_first, w_res_second, w_rbf_atom)
    merged, mixlow, reshid, dsk, du3, du4, dr1, dr2, gath, anew, aslope = call(
        mix_body, "edge_update", edges // BIG, 19,
        (edge_embed, radial_basis, p3, p4, trow) + ups + (w_atom, atom_embed),
        [rows(wide, BIG), rows(rbf, BIG), cols(n3, BIG), cols(n4, BIG), cols(1, BIG)] + [whole(w) for w in ups + (w_atom, atom_embed)],
        [((edges, wide), WIDE), act, act, act, act, act, act, act,
         ((atoms, wide), LOW), ((atoms, aw), LOW), ((atoms, aw), WIDE)],
        [rows(wide, BIG)] * 8 + [fixed(atoms, wide), fixed(atoms, aw), fixed(atoms, aw)],
        [pltpu.VMEM((atoms, wide), WIDE)],
        far=(9,),
    )
    anew = far_array(anew)

    first_parts = (("rows", w_concat.shape), ("rows", (wide, 2 * aw)), ("rows", w_rbf_out.shape))
    outs = (w_concat, w_rbf_out, w_out, output_cotangent, atom_cotangent, aslope, gath, w_atom)
    shapes, specs = grad_outs(first_parts, peers, inside)
    enew, gmer, aout, gatom, gw2, *first = call(
        functools.partial(out_body, parts=first_parts, peers=peers, inside=inside), "output_block", edges // BIG, 16,
        (merged, radial_basis, trow, anew, edge_cotangent) + outs,
        [rows(wide, BIG), rows(rbf, BIG), cols(1, BIG), whole(anew), rows(wide, BIG)] + [whole(w) for w in outs],
        [act, ((edges, wide), WIDE), ((atoms, aw), LOW), ((atoms, aw), LOW), ((2 * atoms, wide), LOW)] + shapes,
        [rows(wide, BIG), rows(wide, BIG), fixed(atoms, aw), fixed(atoms, aw), fixed(2 * atoms, wide)] + specs,
        [
            pltpu.VMEM((atoms, wide), WIDE), pltpu.VMEM((atoms, wide), WIDE),
            pltpu.VMEM((2 * atoms, 2 * wide), LOW),
            pltpu.VMEM(w_concat.shape, WIDE), pltpu.VMEM(w_rbf_out.shape, WIDE), pltpu.VMEM((wide, 2 * aw), WIDE),
        ],
        far=(0, 1, 2, 3),
    )
    gmer = far_array(gmer)

    square = w_skip.shape
    second_parts = (
        ("rows", square), ("rows", square), ("rows", square), ("rows", w_rbf_atom.shape),
        ("cols", (nb, wide)), ("cols", (nb, f3)),
    )
    if inside:
        shapes, specs = grad_outs(first_parts + second_parts, peers, inside)
    else:
        shapes, specs = grad_outs(second_parts, peers, inside)
    more = tuple(first) if inside else ()
    gmh, ls, lb3, lb4, *grads = call(
        functools.partial(back_body, parts=second_parts, peers=peers, inside=inside), "edge_update_back", edges // BIG, 24,
        (edge_embed, radial_basis, trow, s3, s4, merged, gmer, gw2, p3, p4, mixlow, reshid, dsk,
         du3, du4, dr1, dr2) + ups + more,
        [rows(wide, BIG), rows(rbf, BIG), cols(1, BIG), cols(f3, BIG), cols(f4, BIG), rows(wide, BIG), rows(wide, BIG), whole(gw2),
         cols(n3, BIG), cols(n4, BIG)] + [rows(wide, BIG)] * 7 + [whole(w) for w in ups + more],
        [((edges, wide), WIDE), act, ((n3, edges), LOW), ((n4, edges), LOW)] + shapes,
        [rows(wide, BIG), rows(wide, BIG), cols(n3, BIG), cols(n4, BIG)] + specs,
        [pltpu.VMEM(square, WIDE)] * 3
        + [pltpu.VMEM(w_rbf_atom.shape, WIDE), pltpu.VMEM((nb, wide), WIDE), pltpu.VMEM((nb, f3), WIDE)],
        far=(0, 2),
    )
    early_parts = first_parts + second_parts
    early = core_sum(*(grads if inside else pack(early_parts, tuple(first) + tuple(grads), peers)))

    def scatter(lb, idx, mask, basis, wt, name, micros):
        n, slots, q, f = wt.shape[0], idx.shape[0], basis.shape[1], wt.shape[1]
        return call(
            functools.partial(scatter_body, edges=edges), name, steps, micros, (lb, idx, mask, basis, wt),
            [cols(n), cols(slots), cols(slots), rows(q), whole(wt)],
            [((n, edges), WIDE), ((ghosts, LANES), LOW)],
            [fixed(n, edges), fixed(ghosts, LANES)],
            [
                pltpu.VMEM((slabs * n, TILE), WIDE), pltpu.VMEM((q, TILE), WIDE), pltpu.VMEM((f, TILE), LOW),
                pltpu.VMEM((slabs * n, slots * TILE), LOW), pltpu.VMEM((TILE, slots * TILE), LOW),
                pltpu.VMEM((f, n), LOW),
            ],
            far=(0,),
        )

    third_parts = (("rows", square), ("rows", w_rbf_trip.shape))
    quad_parts = third_parts + (("cols", (n4, wide)),)
    trip_parts = third_parts + (("cols", (n3, wide)),)

    def source_back(grad, ret, ws, wr, wd, low, parts, before, name):
        n = wd.shape[0]
        whole_parts = (quad_parts if before else ()) + parts
        shapes, specs = grad_outs(whole_parts if inside else parts, peers, inside)
        more = tuple(before) if inside else ()
        body = functools.partial(
            source_back_body, low=low, parts=parts, peers=peers, inside=inside, after=bool(before)
        )
        ins = (ret, asked, ws, wr, wd) + more
        low_rows, *grads = call(
            body, name, edges // BIG, 11, (edge_embed, radial_basis, grad, down) + ins,
            [rows(wide, BIG), rows(rbf, BIG), cols(n, BIG), cols(nb, BIG)] + [whole(x) for x in ins],
            [act] + shapes, [rows(wide, BIG)] + specs,
            [pltpu.VMEM(square, WIDE), pltpu.VMEM(w_rbf_trip.shape, WIDE), pltpu.VMEM((n, wide), WIDE),
             pltpu.VMEM((LANES, ghosts), LOW)],
            far=() if before else (0, 1, 2),
        )
        return low_rows, grads

    grad4, far4 = scatter(lb4, i4, m4, quadruplet_basis, wb4, "scatter_quad", 11)
    lb3, far4, early = lax.optimization_barrier((lb3, far4, early))
    lb3 = far_array(lb3)
    early = group_sum(early)
    ret4 = exchange(far4, peers)
    grad3, far3 = scatter(lb3, i3, m3, triplet_basis, wb3, "scatter_trip", 18)
    grad3, grad4 = far_array(grad3), far_array(grad4)
    ret4, far3, early = lax.optimization_barrier((ret4, far3, early))
    ret3 = exchange(far3, peers)
    early = share_sum(early)
    l4, quads = source_back(grad4, ret4, w_source_quad, w_rbf_quad, wd4, n3, quad_parts, (), "source_back_quad")
    ret3, quads, early = lax.optimization_barrier((ret3, quads, early))
    quads = [far_array(v) for v in quads] if inside else quads
    early = group_gather(early)
    l3, trips = source_back(grad3, ret3, w_source_trip, w_rbf_trip, wd3, 0, trip_parts, quads, "source_back_trip")
    late_parts = quad_parts + trip_parts
    late = trips if inside else pack(late_parts, tuple(quads) + tuple(trips), peers)
    late, gmh, early = lax.optimization_barrier((late, gmh, early))
    late = core_sum(*late)
    gmh, l4 = far_array(gmh), far_array(l4)
    last = (w_skip, w_source_trip, w_source_quad)
    halves = 2
    for half in range(halves):
        first = half * edges // BIG // halves
        block = pl.BlockSpec((BIG, wide), lambda i, first=first: (first + i, 0))
        ins, extra, alias = (gmh, ls, l3, l4) + last, [], {}
        if half:
            ins, extra, alias = ins + (gedge,), [pl.BlockSpec(memory_space=pl.ANY)], {7: 0}
        (gedge,) = call(
            edge_grad_body, "edge_grad", edges // BIG // halves, 4, ins,
            [block] * 4 + [whole(w) for w in last] + extra, [act], [block], [], far=(0,), alias=alias,
        )
        late, gedge = lax.optimization_barrier((late, gedge))
        late = (group_sum, share_sum)[half](late)
    late = group_gather(late)

    turned = tuple(("turned", shape) if kind == "cols" else (kind, shape) for kind, shape in trip_parts)
    r_concat, r_oa, r_out, r_sk, r_r1, r_r2, r_ra, r_up, r_bil = assemble(early, early_parts, peers, "assemble_early")
    r_s4, r_r4, r_d4, r_s3, r_r3, r_d3 = assemble(late, quad_parts + turned, peers, "assemble_late")
    return (
        enew, anew, aout, gedge, gatom,
        r_s3, r_r3, r_d3, r_s4, r_r4, r_d4.T,
        r_bil[0:n3].T, r_up[0:n3], r_bil[n3:].T, r_up[n3:],
        r_sk, r_r1, r_r2, r_ra, r_oa[:, aw:], r_concat, r_out, r_oa[:, 0:aw],
    )


def solution(mesh):
    both = P(("grp", "edge"), None)
    placed = (both,) * 10 + (P(("grp", "edge"), None, None),) + (P(),) * 18 + (both,) * 3
    shares = [P("edge", None)] * 18
    shares[7] = P(None, "edge")
    shares[9] = P(None, "edge")
    return jax.shard_map(
        per_device, mesh=mesh, in_specs=placed, out_specs=(both,) * 5 + tuple(shares), check_vma=False
    )
```

```python
import functools
import math

import jax
import jax.numpy as jnp
from jax import lax
from jax.experimental import pallas as pl
from jax.experimental.pallas import tpu as pltpu
from jax.sharding import PartitionSpec as P

HALF_ROOT = 1.0 / math.sqrt(2.0)
THIRD_ROOT = 1.0 / math.sqrt(3.0)
LOW = jnp.bfloat16
WIDE = jnp.float32
TILE = 256
BIG = 512
LANES = 128
GROUP = 4
PARTS = 4
ROOM = {
    "source_rows": 16, "sent_rows": 8, "skip_branch": 10, "gather_sums": 14, "edge_update": 18, "output_block": 20,
    "edge_update_back": 24, "scatter_quad": 14, "scatter_trip": 16, "source_back_quad": 16,
    "source_back_trip": 18, "edge_grad": 12, "assemble_early": 8, "assemble_late": 8,
}


def sigma(v):
    return 0.5 * jnp.tanh(0.5 * v) + 0.5


def slope_of(v, s):
    return s * (1.0 + v * (1.0 - s))


def nn(a, b):
    return jnp.dot(a, b, preferred_element_type=WIDE)


def nt(a, b):
    return lax.dot_general(a, b, (((1,), (1,)), ((), ())), preferred_element_type=WIDE)


def tn(a, b):
    return lax.dot_general(a, b, (((0,), (0,)), ((), ())), preferred_element_type=WIDE)


def split_pair(v):
    high = v.astype(LOW)
    rest = (v - high.astype(WIDE)).astype(LOW)
    return jnp.concatenate([high, rest], axis=0)


def whole(array):
    rank = len(array.shape)
    return pl.BlockSpec(array.shape, lambda i: (0,) * rank)


def rows(width, tile=TILE):
    return pl.BlockSpec((tile, width), lambda i: (i, 0))


def cols(height, tile=TILE):
    return pl.BlockSpec((height, tile), lambda i: (0, i))


def fixed(*shape):
    return pl.BlockSpec(shape, lambda i: (0,) * len(shape))


def far_array(v):
    return pltpu.with_memory_space_constraint(v, pltpu.HBM)


def call(body, name, steps, micros, ins, in_specs, outs, out_specs, scratch, far=(), alias={}):
    return pl.pallas_call(
        body,
        name=name,
        out_shape=[(pltpu.HBM if i in far else jax.ShapeDtypeStruct)(s, t) for i, (s, t) in enumerate(outs)],
        grid_spec=pltpu.PrefetchScalarGridSpec(
            num_scalar_prefetch=0,
            grid=(steps,),
            in_specs=in_specs,
            out_specs=out_specs,
            scratch_shapes=scratch,
        ),
        input_output_aliases=alias,
        compiler_params=pltpu.CompilerParams(
            dimension_semantics=("arbitrary",), vmem_limit_bytes=ROOM[name] << 20
        ),
        cost_estimate=pl.CostEstimate(
            flops=int(micros * 1.1e9), transcendentals=0, bytes_accessed=1 << 22
        ),
    )(*ins)


def up16(n):
    return -(-n // 16) * 16


def offsets(parts, peers):
    at, places = 0, []
    for kind, shape in parts:
        places.append(at)
        at += up16(shape[0] // peers if kind == "rows" else shape[0] // PARTS)
    return places, at


def fits(peers, rbf):
    return rbf % (16 * peers) == 0


def grad_outs(parts, peers, inside):
    if inside:
        shapes = [(PARTS, peers // 2, offsets(parts, peers)[1], LANES)] * 2
    else:
        shapes = [shape for _, shape in parts]
    return [(shape, LOW) for shape in shapes], [fixed(*shape) for shape in shapes]


def emit(outs, parts, values, peers, inside, start=0):
    if not inside:
        for out, value in zip(outs, values):
            out[...] = value[...].astype(LOW)
        return
    core = lax.axis_index("edge") & 1
    z = lax.axis_index("edge") >> 1
    grp = lax.axis_index("grp")
    places, _ = offsets(parts, peers)
    for to, side in zip(outs, (1 - core, core)):
        for mz in range(peers // 2):
            for mg in range(PARTS):
                e = ((z ^ mz) << 1) + side
                q = grp ^ mg
                for (kind, shape), place, value in zip(parts, places, values):
                    place += start
                    if kind == "rows":
                        m = shape[0] // peers
                        at = pl.multiple_of(e * m, m)
                        to[mg, mz, place : place + m, :] = value[
                            pl.ds(at, m), pl.ds(pl.multiple_of(q * LANES, LANES), LANES)
                        ].astype(LOW)
                    else:
                        h, w = shape[0] // PARTS, shape[1] // peers
                        at = pl.multiple_of(q * h, 8)
                        if w == LANES:
                            got = value[pl.ds(at, h), pl.ds(pl.multiple_of(e * w, w), w)]
                        else:
                            two = value[pl.ds(at, h), pl.ds(pl.multiple_of((z ^ mz) * LANES, LANES), LANES)]
                            got = jnp.where(side > 0, jnp.concatenate([two[:, w:], two[:, :w]], axis=1), two)
                        if up16(h) > h:
                            got = jnp.concatenate([got, jnp.zeros((up16(h) - h, LANES), WIDE)], axis=0)
                        to[mg, mz, place : place + up16(h), :] = got.astype(LOW)


def pack(parts, grads, peers):
    packed = []
    for (kind, shape), g in zip(parts, grads):
        if kind == "rows":
            g = g.reshape(peers // 2, 2, shape[0] // peers, PARTS, LANES).transpose(1, 3, 0, 2, 4)
        else:
            w = shape[1] // peers
            g = g.reshape(PARTS, shape[0] // PARTS, peers // 2, 2, w).transpose(3, 0, 2, 1, 4)
            g = jnp.pad(g, ((0, 0),) * 4 + ((0, LANES - w),))
        rows_up = up16(g.shape[3])
        packed.append(jnp.pad(g, ((0, 0),) * 3 + ((0, rows_up - g.shape[3]), (0, 0))))
    packed = jnp.concatenate(packed, axis=3)
    place = lax.axis_index("edge")
    own = place & 1
    packed = jnp.take(packed, jnp.arange(PARTS) ^ lax.axis_index("grp"), axis=1)
    packed = jnp.take(packed, jnp.arange(peers // 2) ^ (place >> 1), axis=2)
    return [lax.dynamic_index_in_dim(packed, side, 0, keepdims=False) for side in (1 - own, own)]


def assemble_body(*refs, parts, peers):
    arrived, outs, tmp = refs[:PARTS], refs[PARTS:-1], refs[-1]
    grp = lax.axis_index("grp")
    for (kind, shape), place, out in zip(parts, offsets(parts, peers)[0], outs):
        m = shape[0] // peers
        h, w = shape[0] // PARTS, shape[1] // peers
        for mg in range(PARTS):
            q = grp ^ mg
            if kind == "rows":
                got = arrived[mg][place : place + m, :].astype(WIDE)
                out[:, pl.ds(pl.multiple_of(q * LANES, LANES), LANES)] = got
            else:
                tmp[pl.ds(pl.multiple_of(q * h, 8), h), :] = arrived[mg][place : place + h, :].astype(WIDE)
        if kind == "cols":
            out[...] = tmp[0 : shape[0], 0:w]
        if kind == "turned":
            out[...] = tmp[0 : shape[0], :].T[0:w, :]


def assemble(arrived, parts, peers, name):
    shapes = []
    for kind, (n, w) in parts:
        shapes.append((n // peers, w) if kind == "rows" else (n, w // peers) if kind == "cols" else (w // peers, n))
    return call(
        functools.partial(assemble_body, parts=parts, peers=peers), name, 1, 2, arrived,
        [whole(v) for v in arrived], [(shape, WIDE) for shape in shapes], [fixed(*shape) for shape in shapes],
        [pltpu.VMEM((LANES, LANES), WIDE)],
    )


def source_body(edge, radial, ws3, wr3, wd3, ws4, wr4, wd4, table, down):
    e = edge[...]
    r = radial[...]
    pre3 = nn(e, ws3[...])
    mix3 = (pre3 * sigma(pre3) * nn(r, wr3[...])).astype(LOW)
    down3 = nt(wd3[...], mix3)
    pre4 = nn(e, ws4[...])
    mix4 = (pre4 * sigma(pre4) * nn(r, wr4[...])).astype(LOW)
    down4 = nt(wd4[...], mix4)
    both = jnp.concatenate([down3, down4], axis=0)
    down[...] = both
    table[...] = (both * sigma(both)).astype(LOW)


def sent_body(table, asked, sent, row):
    nb, edges = table.shape
    ghosts = row.shape[1]
    got = jnp.concatenate([asked[p : p + 1, :] for p in range(asked.shape[0])], axis=1) & (edges - 1)
    row[...] = got
    total = jnp.zeros((nb, ghosts), WIDE)
    for s in range(edges // TILE):
        place = lax.broadcasted_iota(jnp.int32, (TILE, ghosts), 0) + s * TILE
        total = total + nn(table[:, s * TILE : (s + 1) * TILE], (place == got).astype(LOW))
    total = jnp.concatenate([total, jnp.zeros((LANES - nb, ghosts), WIDE)], axis=0)
    sent[...] = total.T.astype(LOW)


def fill_slabs(tab, ghost, t3, t4, n3, n4):
    local = tab.shape[1] // TILE
    for s in range(local):
        t3[s * n3 : (s + 1) * n3, :] = tab[0:n3, s * TILE : (s + 1) * TILE]
        t4[s * n4 : (s + 1) * n4, :] = tab[n3 : n3 + n4, s * TILE : (s + 1) * TILE]
    for g in range(0, ghost.shape[0], TILE):
        s = local + g // TILE
        size = min(TILE, ghost.shape[0] - g)
        part = ghost[g : g + size, :].astype(WIDE).T
        if size < TILE:
            part = jnp.concatenate([part, jnp.zeros((LANES, TILE - size), WIDE)], axis=1)
        t3[s * n3 : (s + 1) * n3, :] = part[0:n3, :].astype(LOW)
        t4[s * n4 : (s + 1) * n4, :] = part[n3 : n3 + n4, :].astype(LOW)


def hot_of(low_part):
    place = lax.broadcasted_iota(jnp.int32, (TILE, TILE), 0).astype(WIDE).astype(LOW)
    return jnp.where(place == low_part, jnp.ones((), LOW), jnp.zeros((), LOW))


def pick(tab, index_row, width):
    slabs = tab.shape[0] // width
    low_part = (index_row & (TILE - 1)).astype(WIDE).astype(LOW)
    slab = jnp.broadcast_to((index_row >> 8).astype(WIDE), (width, TILE)).astype(LOW)
    found = nn(tab[...], hot_of(low_part)).astype(LOW)
    got = jnp.zeros((width, TILE), LOW)
    for s in range(slabs):
        got = jnp.where(slab == s, found[s * width : (s + 1) * width, :], got)
    return got


def weigh(coef, picked, out, group, basis, width):
    for cb in range(basis // 4):
        acc = [None] * 4
        for k in range(group * GROUP, (group + 1) * GROUP):
            g = picked[k]
            for j in range(4):
                row = k * basis + cb * 4 + j
                term = jnp.broadcast_to(coef[row : row + 1, :], g.shape).astype(LOW) * g
                acc[j] = term if acc[j] is None else acc[j] + term
        for j in range(4):
            at = (cb * 4 + j) * width
            before = out[at : at + width, :] + acc[j] if group else acc[j]
            out[at : at + width, :] = before


def chosen(index, mask):
    return jnp.where(mask > 0, index, -1)


def gather_body(
    tab, ghost, i3, m3, i4, m4, b3, b4, w3t, w4t, s3, s4, p3, p4, t3, t4, g3, g4, c3, c4
):
    n3, n4 = w3t.shape[0], w4t.shape[0]
    k3, k4 = i3.shape[0], i4.shape[0]

    @pl.when(pl.program_id(0) == 0)
    def _():
        fill_slabs(tab, ghost, t3, t4, n3, n4)

    c3[...] = b3[...].astype(WIDE).T
    c4[...] = b4[...].astype(WIDE).T

    work = [(t3, i3, m3, g3, c3, s3, n3, k3, j) for j in range(k3 // GROUP)]
    work += [(t4, i4, m4, g4, c4, s4, n4, k4, j) for j in range(k4 // GROUP)]
    for at in range(len(work) + 1):
        if at < len(work):
            t, i, m, g, _, _, n, _, j = work[at]
            for k in range(j * GROUP, (j + 1) * GROUP):
                g[k] = pick(t, chosen(i[k : k + 1, :], m[k : k + 1, :]), n)
        if at:
            _, _, _, g, c, out, n, count, j = work[at - 1]
            weigh(c, g, out, j, c.shape[0] // count, n)
    p3[...] = nn(w3t[...], s3[...])
    p4[...] = nn(w4t[...], s4[...])


def skip_body(edge, wsk, skip_out, dsk):
    skip = nn(edge[...], wsk[...])
    s = sigma(skip)
    dsk[...] = slope_of(skip, s).astype(LOW)
    skip_out[...] = (skip * s).astype(LOW)


def mix_body(
    edge, radial, p3, p4, trow, skip, wu3, wu4, wr1, wr2, wra, wat, atom,
    merged, mixlow, reshid, du3, du4, dr1, dr2, gath, anew, aslope, acc,
):
    step = pl.program_id(0)
    atoms = acc.shape[0]
    v3 = p3[...]
    v4 = p4[...]
    h3 = (v3 * sigma(v3)).T.astype(LOW)
    h4 = (v4 * sigma(v4)).T.astype(LOW)
    up3 = nn(h3, wu3[...])
    s = sigma(up3)
    du3[...] = slope_of(up3, s).astype(LOW)
    total = up3 * s
    up4 = nn(h4, wu4[...])
    s = sigma(up4)
    du4[...] = slope_of(up4, s).astype(LOW)
    mixed = (total + up4 * s + skip[...].astype(WIDE)) * THIRD_ROOT
    low_mixed = mixed.astype(LOW)
    mixlow[...] = low_mixed
    res = nn(low_mixed, wr1[...])
    s = sigma(res)
    dr1[...] = slope_of(res, s).astype(LOW)
    hid = (res * s).astype(LOW)
    reshid[...] = hid
    res2 = nn(hid, wr2[...])
    s = sigma(res2)
    dr2[...] = (0.5 * slope_of(res2, s)).astype(LOW)
    out = (edge[...].astype(WIDE) + (mixed + res2 * s) * HALF_ROOT) * HALF_ROOT
    merged[...] = out
    weighted = (out * nn(radial[...], wra[...])).astype(LOW)
    hot_t = (lax.broadcasted_iota(jnp.int32, (atoms, edge.shape[0]), 0) == trow[...]).astype(LOW)
    part = nn(hot_t, weighted)

    @pl.when(step == 0)
    def _():
        acc[...] = part

    @pl.when(step > 0)
    def _():
        acc[...] += part

    @pl.when(step == pl.num_programs(0) - 1)
    def _():
        g = acc[...].astype(LOW)
        gath[...] = g
        pre = nn(g, wat[...])
        sa = sigma(pre)
        aslope[...] = HALF_ROOT * slope_of(pre, sa)
        anew[...] = ((atom[...].astype(WIDE) + pre * sa) * HALF_ROOT).astype(LOW)


def out_body(
    merged, radial, trow, anew, cot, wc, wro, wout, ocot, acot, aslope, gath, wat,
    enew, gmer, aout, gatom, gw2, *rest, parts, peers, inside,
):
    outs, (ogat, seg, both, awc, aro, aoa) = rest[:-6], rest[-6:]
    step = pl.program_id(0)
    atoms, wide = ogat.shape
    aw = anew.shape[1]

    @pl.when(step == 0)
    def _():
        both[:, 0:wide] = split_pair(nt(ocot[...], wout[...]))
        both[:, wide : 2 * wide] = split_pair(nn(anew[...], wc[0:aw, :]))
        ogat[...] = jnp.zeros_like(ogat)
        seg[...] = jnp.zeros_like(seg)
        awc[...] = jnp.zeros_like(awc)
        aro[...] = jnp.zeros_like(aro)

    hot_t = (lax.broadcasted_iota(jnp.int32, (atoms, merged.shape[0]), 0) == trow[...]).astype(LOW)
    spread = tn(jnp.concatenate([hot_t, hot_t], axis=0), both[...])
    gow = spread[:, 0:wide]
    m = merged[...]
    ml = m.astype(LOW)
    wcm = wc[aw:, :]
    pre = spread[:, wide:] + nn(ml, wcm)
    s = sigma(pre)
    new = (m + pre * s) * HALF_ROOT
    enew[...] = new.astype(LOW)
    rout = nn(radial[...], wro[...])
    ogat[...] += nn(hot_t, (new * rout).astype(LOW))
    gnew = cot[...].astype(WIDE) + gow * rout
    aro[...] += tn(radial[...], (gow * new).astype(LOW))
    lc = (gnew * (HALF_ROOT * slope_of(pre, s))).astype(LOW)
    awc[aw:, :] += tn(ml, lc)
    seg[...] += nn(hot_t, lc)
    gmer[...] = gnew * HALF_ROOT + nt(lc, wcm)

    @pl.when(step == pl.num_programs(0) - 1)
    def _():
        ol = ogat[...].astype(LOW)
        aout[...] = nn(ol, wout[...]).astype(LOW)
        aoa[:, 0:aw] = tn(ol, ocot[...])
        pair = split_pair(seg[...])
        hi = pair[0:atoms, :]
        lo = pair[atoms:, :]
        awc[0:aw, :] = tn(anew[...], hi) + tn(anew[...], lo)
        wca = wc[0:aw, :]
        ga = acot[...].astype(WIDE) + nt(hi, wca) + nt(lo, wca)
        gatom[...] = (ga * HALF_ROOT).astype(LOW)
        la = (ga * aslope[...]).astype(LOW)
        aoa[:, aw : 2 * aw] = tn(gath[...], la)
        gw2[...] = split_pair(nt(la, wat[...]))
        emit(outs, parts, (awc, aoa, aro), peers, inside)


def back_body(
    edge, radial, trow, s3, s4, merged, gmer, gw2, p3, p4, mixlow, reshid, dsk, du3, du4, dr1, dr2,
    wu3, wu4, wr1, wr2, wra, *rest, parts, peers, inside,
):
    if inside:
        before, rest = rest[:2], rest[2:]
    (gm_out, ls_out, lb3, lb4), outs = rest[:4], rest[4:-6]
    ask, ar1, ar2, ara, aup, abil = rest[-6:]
    step = pl.program_id(0)
    pair = gw2.shape[0]
    n3 = wu3.shape[0]

    @pl.when(step == 0)
    def _():
        ask[...] = jnp.zeros_like(ask)
        ar1[...] = jnp.zeros_like(ar1)
        ar2[...] = jnp.zeros_like(ar2)
        ara[...] = jnp.zeros_like(ara)
        aup[...] = jnp.zeros_like(aup)
        abil[...] = jnp.zeros_like(abil)

    hot_t = (lax.broadcasted_iota(jnp.int32, (pair // 2, edge.shape[0]), 0) == trow[...]).astype(LOW)
    gw = tn(jnp.concatenate([hot_t, hot_t], axis=0), gw2[...])
    gm = gmer[...] + gw * nn(radial[...], wra[...])
    ara[...] += tn(radial[...], (gw * merged[...]).astype(LOW))
    l2 = (gm * dr2[...].astype(WIDE)).astype(LOW)
    ar2[...] += tn(reshid[...], l2)
    l1 = (nt(l2, wr2[...]) * dr1[...].astype(WIDE)).astype(LOW)
    ar1[...] += tn(mixlow[...], l1)
    gmix = (gm * 0.5 + nt(l1, wr1[...])) * THIRD_ROOT
    ls = (gmix * dsk[...].astype(WIDE)).astype(LOW)
    l3 = (gmix * du3[...].astype(WIDE)).astype(LOW)
    l4 = (gmix * du4[...].astype(WIDE)).astype(LOW)
    ask[...] += tn(edge[...], ls)
    gm_out[...] = gm * HALF_ROOT
    ls_out[...] = ls
    v3 = p3[...]
    g3 = sigma(v3)
    v4 = p4[...]
    g4 = sigma(v4)
    aup[0:n3, :] += nn((v3 * g3).astype(LOW), l3)
    aup[n3:, :] += nn((v4 * g4).astype(LOW), l4)
    low3 = (nt(wu3[...], l3) * slope_of(v3, g3)).astype(LOW)
    low4 = (nt(wu4[...], l4) * slope_of(v4, g4)).astype(LOW)
    lb3[...] = low3
    lb4[...] = low4
    abil[0:n3, :] += nt(low3, s3[...])
    abil[n3:, :] += nt(low4, s4[...])

    @pl.when(step == pl.num_programs(0) - 1)
    def _():
        values = (ask, ar1, ar2, ara, aup, abil)
        if inside:
            first = before[0].shape[2]
            for out, past in zip(outs, before):
                out[:, :, 0:first, :] = past[...]
            emit(outs, parts, values, peers, inside, first)
        else:
            emit(outs, parts, values, peers, inside)


def unweigh(coef, dsum, index, mask, spread, hots, group, basis, width):
    slabs = spread.shape[0] // width
    for k in range(group * GROUP, (group + 1) * GROUP):
        low_part = (index[k : k + 1, :] & (TILE - 1)).astype(WIDE).astype(LOW)
        hots[:, k * TILE : (k + 1) * TILE] = hot_of(low_part)
    acc = [None] * GROUP
    for c in range(basis):
        d = dsum[c * width : (c + 1) * width, :]
        for j in range(GROUP):
            row = (group * GROUP + j) * basis + c
            term = jnp.broadcast_to(coef[row : row + 1, :], d.shape).astype(LOW) * d
            acc[j] = term if acc[j] is None else acc[j] + term
    for j in range(GROUP):
        k = group * GROUP + j
        got = chosen(index[k : k + 1, :], mask[k : k + 1, :]) >> 8
        slab = jnp.broadcast_to(got.astype(WIDE), (width, TILE)).astype(LOW)
        for s in range(slabs):
            spread[s * width : (s + 1) * width, k * TILE : (k + 1) * TILE] = jnp.where(
                slab == s, acc[j], jnp.zeros((), LOW)
            )


def scatter_body(lb, idx, mask, basis, wt, grad, far, acc, coef, dsum, spread, hots, w, *, edges):
    step = pl.program_id(0)
    n = wt.shape[0]
    slots = idx.shape[0]

    @pl.when(step == 0)
    def _():
        acc[...] = jnp.zeros_like(acc)
        w[...] = wt[...].astype(WIDE).T.astype(LOW)

    coef[...] = basis[...].astype(WIDE).T
    dsum[...] = nn(w[...], lb[...]).astype(LOW)
    for group in range(slots // GROUP):
        part = slice(group * GROUP * TILE, (group + 1) * GROUP * TILE)
        unweigh(coef, dsum, idx, mask, spread, hots, group, coef.shape[0] // slots, n)
        acc[...] += nt(spread[:, part], hots[:, part])

    @pl.when(step == pl.num_programs(0) - 1)
    def _():
        local = edges // TILE
        for s in range(local):
            grad[:, s * TILE : (s + 1) * TILE] = acc[s * n : (s + 1) * n, :]
        for s in range(local, acc.shape[0] // n):
            filler = jnp.zeros((LANES - n, TILE), WIDE)
            part = jnp.concatenate([acc[s * n : (s + 1) * n, :], filler], axis=0).T.astype(LOW)
            at = (s - local) * TILE
            size = min(TILE, far.shape[0] - at)
            far[at : at + size, :] = part[0:size, :]


def source_back_body(edge, radial, grad, down, ret, asked, ws, wr, wd, *rest, low, parts, peers, inside, after):
    if inside and after:
        before, rest = rest[:2], rest[2:]
    low_out, outs, (asum, arad, adn, rt) = rest[0], rest[1:-4], rest[-4:]
    step = pl.program_id(0)
    n = grad.shape[0]

    @pl.when(step == 0)
    def _():
        rt[...] = ret[...].astype(WIDE).T.astype(LOW)
        asum[...] = jnp.zeros_like(asum)
        arad[...] = jnp.zeros_like(arad)
        adn[...] = jnp.zeros_like(adn)

    place = lax.broadcasted_iota(jnp.int32, (edge.shape[0], asked.shape[1]), 0) + step * edge.shape[0]
    back = nt(rt[0:n, :], (place == asked[...]).astype(LOW))
    v = down[low : low + n, :]
    ld = (grad[...] + back) * slope_of(v, sigma(v))
    ldt = ld.astype(LOW)
    low_rows = ld.T.astype(LOW)
    e = edge[...]
    r = radial[...]
    pre = nn(e, ws[...])
    rad = nn(r, wr[...])
    s = sigma(pre)
    act = pre * s
    adn[...] += nn(ldt, (act * rad).astype(LOW))
    gm = nn(low_rows, wd[...])
    lo = (gm * rad * slope_of(pre, s)).astype(LOW)
    low_out[...] = lo
    arad[...] += tn(r, (gm * act).astype(LOW))
    asum[...] += tn(e, lo)

    @pl.when(step == pl.num_programs(0) - 1)
    def _():
        if inside and after:
            first = before[0].shape[2]
            for out, past in zip(outs, before):
                out[:, :, 0:first, :] = past[...]
            emit(outs, parts, (asum, arad, adn), peers, inside, first)
        else:
            emit(outs, parts, (asum, arad, adn), peers, inside)


def edge_grad_body(*refs):
    gm, ls, l3, l4, wsk, ws3, ws4 = refs[:7]
    gedge = refs[-1]
    total = gm[...] + nt(ls[...], wsk[...]) + nt(l3[...], ws3[...]) + nt(l4[...], ws4[...])
    gedge[...] = total.astype(LOW)


def swap(v, axis, mask):
    count = lax.axis_size(axis)
    return lax.ppermute(v, axis, [(j, j ^ mask) for j in range(count)])


def summed(v, axis, shift):
    total = v[0].astype(WIDE)
    for m in range(1, v.shape[0]):
        total = total + swap(v[m], axis, m << shift).astype(WIDE)
    return total.astype(LOW)


def core_sum(send, keep):
    return (keep.astype(WIDE) + swap(send, "edge", 1).astype(WIDE)).astype(LOW)


def group_sum(v):
    return summed(v, "grp", 0)


def share_sum(v):
    at = 1
    while v.shape[0] > 1:
        width = min(4, v.shape[0])
        v = v.reshape(v.shape[0] // width, width, *v.shape[1:])
        v = summed(jnp.moveaxis(v, 1, 0), "edge", at)
        at += width.bit_length() - 1
    return v[0]


def group_gather(v):
    return (v,) + tuple(swap(v, "grp", m) for m in range(1, PARTS))


def exchange(v, peers):
    parts = v.reshape(peers, v.shape[0] // peers, v.shape[1])
    return lax.all_to_all(parts, "edge", split_axis=0, concat_axis=0, tiled=True).reshape(v.shape)


def per_device(
    edge_embed, atom_embed, radial_basis, triplet_basis, quadruplet_basis,
    triplet_source_row, triplet_mask, quadruplet_source_row, quadruplet_mask,
    edge_target_atom, borrowed_edges,
    w_source_trip, w_rbf_trip, w_down_trip, w_source_quad, w_rbf_quad, w_down_quad,
    triplet_bilinear_weight, w_up_trip, w_bilinear_quad, w_up_quad, w_skip,
    w_res_first, w_res_second, w_rbf_atom, w_atom, w_concat, w_rbf_out, w_out,
    edge_cotangent, atom_cotangent, output_cotangent,
):
    edges, wide = edge_embed.shape
    atoms, aw = atom_embed.shape
    rbf = radial_basis.shape[1]
    peers = lax.axis_size("edge")
    cap = borrowed_edges.shape[2]
    steps = edges // TILE
    n3, n4 = w_down_trip.shape[1], w_down_quad.shape[1]
    nb = n3 + n4
    k3, k4 = triplet_mask.shape[1], quadruplet_mask.shape[1]
    f3, f4 = triplet_bilinear_weight.shape[0], w_bilinear_quad.shape[0]
    q3, q4 = triplet_basis.shape[1], quadruplet_basis.shape[1]
    ghosts = peers * cap
    ghosts_up = -(-ghosts // TILE) * TILE
    slabs = (edges + ghosts_up) // TILE

    inside = fits(peers, rbf)
    (
        edge_embed, atom_embed, radial_basis, triplet_basis, quadruplet_basis, edge_cotangent,
        w_source_trip, w_rbf_trip, w_source_quad, w_rbf_quad, w_skip, w_res_first, w_res_second, w_rbf_atom,
        w_atom, w_concat, w_rbf_out, w_out, w_up_trip, w_up_quad, atom_cotangent, output_cotangent,
    ) = map(far_array, (
        edge_embed, atom_embed, radial_basis, triplet_basis, quadruplet_basis, edge_cotangent,
        w_source_trip, w_rbf_trip, w_source_quad, w_rbf_quad, w_skip, w_res_first, w_res_second, w_rbf_atom,
        w_atom, w_concat, w_rbf_out, w_out, w_up_trip, w_up_quad, atom_cotangent, output_cotangent,
    ))
    far_ids = lax.all_to_all(borrowed_edges[0], "edge", split_axis=0, concat_axis=0, tiled=True)

    i3, m3, i4, m4, wd3, wd4, wb3, wb4 = [
        far_array(v.T)
        for v in (
            triplet_source_row, triplet_mask, quadruplet_source_row, quadruplet_mask,
            w_down_trip, w_down_quad, triplet_bilinear_weight, w_bilinear_quad,
        )
    ]
    trow = far_array(edge_target_atom)
    sources = (w_source_trip, w_rbf_trip, wd3, w_source_quad, w_rbf_quad, wd4)

    table, down = call(
        source_body, "source_rows", edges // BIG, 10, (edge_embed, radial_basis) + sources,
        [rows(wide, BIG), rows(rbf, BIG)] + [whole(w) for w in sources],
        [((nb, edges), LOW), ((nb, edges), WIDE)], [cols(nb, BIG), cols(nb, BIG)], [],
    )
    table, far_ids = lax.optimization_barrier((table, far_ids))
    sent, asked = call(
        sent_body, "sent_rows", 1, 2, (table, far_ids), [whole(table), whole(far_ids)],
        [((ghosts, LANES), LOW), ((1, ghosts), jnp.int32)], [fixed(ghosts, LANES), fixed(1, ghosts)], [], far=(1,),
    )
    asked = far_array(asked)
    ghost = exchange(sent, peers)
    sent, later = lax.optimization_barrier((sent, w_skip))
    act = ((edges, wide), LOW)
    skip, dsk = call(
        skip_body, "skip_branch", edges // BIG, 5, (edge_embed, far_array(later)),
        [rows(wide, BIG), whole(w_skip)], [act, act], [rows(wide, BIG)] * 2, [], far=(0, 1),
    )
    skip, dsk = far_array(skip), far_array(dsk)

    s3, s4, p3, p4 = call(
        gather_body, "gather_sums", steps, 25,
        (table, ghost, i3, m3, i4, m4, triplet_basis, quadruplet_basis, wb3, wb4),
        [whole(table), whole(ghost), cols(k3), cols(k3), cols(k4), cols(k4), rows(q3), rows(q4),
         whole(wb3), whole(wb4)],
        [((f3, edges), LOW), ((f4, edges), LOW), ((n3, edges), WIDE), ((n4, edges), WIDE)],
        [cols(f3), cols(f4), cols(n3), cols(n4)],
        [
            pltpu.VMEM((slabs * n3, TILE), LOW), pltpu.VMEM((slabs * n4, TILE), LOW),
            pltpu.VMEM((k3, n3, TILE), LOW), pltpu.VMEM((k4, n4, TILE), LOW),
            pltpu.VMEM((q3, TILE), WIDE), pltpu.VMEM((q4, TILE), WIDE),
        ],
        far=(0, 1),
    )

    s3, s4 = far_array(s3), far_array(s4)
    ups = (w_up_trip, w_up_quad, w_res_first, w_res_second, w_rbf_atom)
    merged, mixlow, reshid, du3, du4, dr1, dr2, gath, anew, aslope = call(
        mix_body, "edge_update", edges // BIG, 19,
        (edge_embed, radial_basis, p3, p4, trow, skip) + ups + (w_atom, atom_embed),
        [rows(wide, BIG), rows(rbf, BIG), cols(n3, BIG), cols(n4, BIG), cols(1, BIG), rows(wide, BIG)] + [whole(w) for w in ups + (w_atom, atom_embed)],
        [((edges, wide), WIDE), act, act, act, act, act, act,
         ((atoms, wide), LOW), ((atoms, aw), LOW), ((atoms, aw), WIDE)],
        [rows(wide, BIG)] * 7 + [fixed(atoms, wide), fixed(atoms, aw), fixed(atoms, aw)],
        [pltpu.VMEM((atoms, wide), WIDE)],
        far=(8,),
    )
    anew = far_array(anew)

    first_parts = (("rows", w_concat.shape), ("rows", (wide, 2 * aw)), ("rows", w_rbf_out.shape))
    outs = (w_concat, w_rbf_out, w_out, output_cotangent, atom_cotangent, aslope, gath, w_atom)
    shapes, specs = grad_outs(first_parts, peers, inside)
    enew, gmer, aout, gatom, gw2, *first = call(
        functools.partial(out_body, parts=first_parts, peers=peers, inside=inside), "output_block", edges // BIG, 16,
        (merged, radial_basis, trow, anew, edge_cotangent) + outs,
        [rows(wide, BIG), rows(rbf, BIG), cols(1, BIG), whole(anew), rows(wide, BIG)] + [whole(w) for w in outs],
        [act, ((edges, wide), WIDE), ((atoms, aw), LOW), ((atoms, aw), LOW), ((2 * atoms, wide), LOW)] + shapes,
        [rows(wide, BIG), rows(wide, BIG), fixed(atoms, aw), fixed(atoms, aw), fixed(2 * atoms, wide)] + specs,
        [
            pltpu.VMEM((atoms, wide), WIDE), pltpu.VMEM((atoms, wide), WIDE),
            pltpu.VMEM((2 * atoms, 2 * wide), LOW),
            pltpu.VMEM(w_concat.shape, WIDE), pltpu.VMEM(w_rbf_out.shape, WIDE), pltpu.VMEM((wide, 2 * aw), WIDE),
        ],
        far=(0, 1, 2, 3),
    )
    gmer = far_array(gmer)

    square = w_skip.shape
    second_parts = (
        ("rows", square), ("rows", square), ("rows", square), ("rows", w_rbf_atom.shape),
        ("cols", (nb, wide)), ("cols", (nb, f3)),
    )
    if inside:
        shapes, specs = grad_outs(first_parts + second_parts, peers, inside)
    else:
        shapes, specs = grad_outs(second_parts, peers, inside)
    more = tuple(first) if inside else ()
    gmh, ls, lb3, lb4, *grads = call(
        functools.partial(back_body, parts=second_parts, peers=peers, inside=inside), "edge_update_back", edges // BIG, 24,
        (edge_embed, radial_basis, trow, s3, s4, merged, gmer, gw2, p3, p4, mixlow, reshid, dsk,
         du3, du4, dr1, dr2) + ups + more,
        [rows(wide, BIG), rows(rbf, BIG), cols(1, BIG), cols(f3, BIG), cols(f4, BIG), rows(wide, BIG), rows(wide, BIG), whole(gw2),
         cols(n3, BIG), cols(n4, BIG)] + [rows(wide, BIG)] * 7 + [whole(w) for w in ups + more],
        [((edges, wide), WIDE), act, ((n3, edges), LOW), ((n4, edges), LOW)] + shapes,
        [rows(wide, BIG), rows(wide, BIG), cols(n3, BIG), cols(n4, BIG)] + specs,
        [pltpu.VMEM(square, WIDE)] * 3
        + [pltpu.VMEM(w_rbf_atom.shape, WIDE), pltpu.VMEM((nb, wide), WIDE), pltpu.VMEM((nb, f3), WIDE)],
        far=(0, 2),
    )
    early_parts = first_parts + second_parts
    early = core_sum(*(grads if inside else pack(early_parts, tuple(first) + tuple(grads), peers)))

    def scatter(lb, idx, mask, basis, wt, name, micros):
        n, slots, q, f = wt.shape[0], idx.shape[0], basis.shape[1], wt.shape[1]
        return call(
            functools.partial(scatter_body, edges=edges), name, steps, micros, (lb, idx, mask, basis, wt),
            [cols(n), cols(slots), cols(slots), rows(q), whole(wt)],
            [((n, edges), WIDE), ((ghosts, LANES), LOW)],
            [fixed(n, edges), fixed(ghosts, LANES)],
            [
                pltpu.VMEM((slabs * n, TILE), WIDE), pltpu.VMEM((q, TILE), WIDE), pltpu.VMEM((f, TILE), LOW),
                pltpu.VMEM((slabs * n, slots * TILE), LOW), pltpu.VMEM((TILE, slots * TILE), LOW),
                pltpu.VMEM((f, n), LOW),
            ],
            far=(0,),
        )

    third_parts = (("rows", square), ("rows", w_rbf_trip.shape))
    quad_parts = third_parts + (("cols", (n4, wide)),)
    trip_parts = third_parts + (("cols", (n3, wide)),)

    def source_back(grad, ret, ws, wr, wd, low, parts, before, name):
        n = wd.shape[0]
        whole_parts = (quad_parts if before else ()) + parts
        shapes, specs = grad_outs(whole_parts if inside else parts, peers, inside)
        more = tuple(before) if inside else ()
        body = functools.partial(
            source_back_body, low=low, parts=parts, peers=peers, inside=inside, after=bool(before)
        )
        ins = (ret, asked, ws, wr, wd) + more
        low_rows, *grads = call(
            body, name, edges // BIG, 11, (edge_embed, radial_basis, grad, down) + ins,
            [rows(wide, BIG), rows(rbf, BIG), cols(n, BIG), cols(nb, BIG)] + [whole(x) for x in ins],
            [act] + shapes, [rows(wide, BIG)] + specs,
            [pltpu.VMEM(square, WIDE), pltpu.VMEM(w_rbf_trip.shape, WIDE), pltpu.VMEM((n, wide), WIDE),
             pltpu.VMEM((LANES, ghosts), LOW)],
            far=() if before else (0, 1, 2),
        )
        return low_rows, grads

    grad4, far4 = scatter(lb4, i4, m4, quadruplet_basis, wb4, "scatter_quad", 11)
    lb3, far4, early = lax.optimization_barrier((lb3, far4, early))
    lb3 = far_array(lb3)
    early = group_sum(early)
    ret4 = exchange(far4, peers)
    grad3, far3 = scatter(lb3, i3, m3, triplet_basis, wb3, "scatter_trip", 18)
    grad3, grad4 = far_array(grad3), far_array(grad4)
    ret4, far3, early = lax.optimization_barrier((ret4, far3, early))
    ret3 = exchange(far3, peers)
    early = share_sum(early)
    l4, quads = source_back(grad4, ret4, w_source_quad, w_rbf_quad, wd4, n3, quad_parts, (), "source_back_quad")
    ret3, quads, early = lax.optimization_barrier((ret3, quads, early))
    quads = [far_array(v) for v in quads] if inside else quads
    early = group_gather(early)
    l3, trips = source_back(grad3, ret3, w_source_trip, w_rbf_trip, wd3, 0, trip_parts, quads, "source_back_trip")
    late_parts = quad_parts + trip_parts
    late = trips if inside else pack(late_parts, tuple(quads) + tuple(trips), peers)
    late, gmh, early = lax.optimization_barrier((late, gmh, early))
    late = core_sum(*late)
    gmh, l4 = far_array(gmh), far_array(l4)
    last = (w_skip, w_source_trip, w_source_quad)
    halves = 2
    for half in range(halves):
        first = half * edges // BIG // halves
        block = pl.BlockSpec((BIG, wide), lambda i, first=first: (first + i, 0))
        ins, extra, alias = (gmh, ls, l3, l4) + last, [], {}
        if half:
            ins, extra, alias = ins + (gedge,), [pl.BlockSpec(memory_space=pl.ANY)], {7: 0}
        (gedge,) = call(
            edge_grad_body, "edge_grad", edges // BIG // halves, 4, ins,
            [block] * 4 + [whole(w) for w in last] + extra, [act], [block], [], far=(0,), alias=alias,
        )
        late, gedge = lax.optimization_barrier((late, gedge))
        late = (group_sum, share_sum)[half](late)
    late = group_gather(late)

    turned = tuple(("turned", shape) if kind == "cols" else (kind, shape) for kind, shape in trip_parts)
    r_concat, r_oa, r_out, r_sk, r_r1, r_r2, r_ra, r_up, r_bil = assemble(early, early_parts, peers, "assemble_early")
    r_s4, r_r4, r_d4, r_s3, r_r3, r_d3 = assemble(late, quad_parts + turned, peers, "assemble_late")
    return (
        enew, anew, aout, gedge, gatom,
        r_s3, r_r3, r_d3, r_s4, r_r4, r_d4.T,
        r_bil[0:n3].T, r_up[0:n3], r_bil[n3:].T, r_up[n3:],
        r_sk, r_r1, r_r2, r_ra, r_oa[:, aw:], r_concat, r_out, r_oa[:, 0:aw],
    )


def solution(mesh):
    both = P(("grp", "edge"), None)
    placed = (both,) * 10 + (P(("grp", "edge"), None, None),) + (P(),) * 18 + (both,) * 3
    shares = [P("edge", None)] * 18
    shares[7] = P(None, "edge")
    shares[9] = P(None, "edge")
    return jax.shard_map(
        per_device, mesh=mesh, in_specs=placed, out_specs=(both,) * 5 + tuple(shares), check_vma=False
    )
```
